32 devices in a mesh: pb: 8 (over y, x, core), ka: 4 (over z).
Axes of the slice: x: 2, y: 2, z: 4, core: 2. Of those that a mesh axis runs over, the one named last changes fastest.
Arguments:
- coupling: bfloat16 [2, 320, 4800, 320], P(None, 'ka', 'pb'), may hold values from -0.019897461 to 0.019897461
- kpoints: int32 [3, 16], replicated, may hold values from 0 to 99
- qpoints: int32 [3, 32], replicated, may hold values from 0 to 99
- electron_cells: int32 [3, 320], replicated, may hold values from -6 to 6
- phonon_cells: int32 [3, 320], replicated, may hold values from -6 to 6
- phonon_modes: bfloat16 [32, 2, 120, 120], P('pb'), may hold values from -0.375 to 0.375
- band_vectors: bfloat16 [32, 16, 2, 40, 40], P('pb', 'ka'), may hold values from -0.625 to 0.625
- energies_kq: float32 [32, 16, 40], P('pb', 'ka'), may hold values from -0.5 to 0.5
- occupations_kq: float32 [32, 16, 40], P('pb', 'ka'), may hold values from 0 to 1
- energy_k: float32 [16], P('ka'), may hold values from -0.5 to 0.5
- occupation_k: float32 [16], P('ka'), may hold values from 0 to 1
- frequencies: float32 [32, 120], P('pb'), may hold values from 0.02 to 0.2
- bose_factors: float32 [32, 120], P('pb'), may hold values from 0.1 to 5
Outputs:
- electron_width: float32 [16, 120], P('ka')
- phonon_width: float32 [32, 120], P('pb')
The draws below stay inside these ranges and needn't reach their ends.
All inputs are finite; a program needn't handle non-finite values.
Results may differ from the reference program's by a relative error of at most 0.0066.
Values may be sent and summed in bfloat16 or wider, within the bound.
A program may use at most 320 MiB of HBM per device.

```python
import math
import jax
import jax.numpy as jnp
from jax import lax

NB = 40
MODES = 120
CE = 320
CP = 320
NG = 100
QD = 4
PAIRS = 4800
KTOT = 16
QTOT = 32


def set_ends(result, key, least, top_value):
    place = [jax.random.randint(jax.random.fold_in(key, axis), (), 0, length) for axis, length in enumerate(result.shape)]
    main_axis = result.shape.index(max(result.shape))
    beside = place[:main_axis] + [(place[main_axis] + 1) % result.shape[main_axis]] + place[main_axis + 1:]
    return result.at[tuple(place)].set(least).at[tuple(beside)].set(top_value)


def level_of(key, extent, shards, smallest, high):
    gain = 1.0
    for position, shards_of in shards:
        steps = jax.random.uniform(jax.random.fold_in(jax.random.fold_in(key, 6), position), (shards_of,), jnp.float32, smallest / len(shards), high / len(shards))
        gain = gain * jnp.repeat(jnp.exp(steps), extent[position] // shards_of).reshape((-1,) + (1,) * (len(extent) - 1 - position))
    return gain


def centred(own_key, dims, scale, limit, split=(), held_as=jnp.bfloat16):
    array = scale * jax.random.normal(own_key, dims, jnp.float32)
    if split:
        array = array * level_of(own_key, dims, split, -0.22, 0.18)
    return jnp.clip(array, -limit, limit).astype(held_as)


def setup_inputs(seed: int = 0) -> dict:
    seeds = jax.random.split(jax.random.key(seed), 14)
    coupling = centred(seeds[0], (2, CE, PAIRS, CP), 0.003125, 0.019897461, ((1, 4), (2, 8)))
    kpoints = set_ends(jax.random.randint(seeds[1], (3, KTOT), 0, NG), jax.random.fold_in(seeds[1], 1), 0, NG - 1).astype(jnp.int32)
    qpoints = set_ends(jax.random.randint(seeds[2], (3, QTOT), 0, NG), jax.random.fold_in(seeds[2], 1), 0, NG - 1).astype(jnp.int32)
    electron_cells = set_ends(jax.random.randint(seeds[3], (3, CE), -6, 7), jax.random.fold_in(seeds[3], 1), -6, 6).astype(jnp.int32)
    phonon_cells = set_ends(jax.random.randint(seeds[4], (3, CP), -6, 7), jax.random.fold_in(seeds[4], 1), -6, 6).astype(jnp.int32)
    phonon_modes = centred(seeds[5], (QTOT, 2, MODES, MODES), (2 * MODES) ** -0.5, 0.375, ((0, 8),))
    band_vectors = centred(seeds[6], (QTOT, KTOT, 2, NB, NB), (2 * NB) ** -0.5, 0.625, ((0, 8), (1, 4)))
    energies_kq = jnp.clip(jax.random.uniform(seeds[7], (QTOT, KTOT, NB), jnp.float32, -0.5, 0.5) * level_of(seeds[7], (QTOT, KTOT, NB), ((0, 8), (1, 4)), -0.4, 0.0), -0.5, 0.5)
    occupations_kq = jnp.clip(1.0 * jax.random.uniform(seeds[8], (QTOT, KTOT, NB), jnp.float32) ** level_of(seeds[8], (QTOT, KTOT, NB), ((0, 8), (1, 4)), -0.2, 0.2), 0.0, 1.0)
    energy_k = jnp.clip(jax.random.uniform(seeds[9], (KTOT,), jnp.float32, -0.5, 0.5) * level_of(seeds[9], (KTOT,), ((0, 4),), -0.4, 0.0), -0.5, 0.5)
    occupation_k = jnp.clip(1.0 * jax.random.uniform(seeds[10], (KTOT,), jnp.float32) ** level_of(seeds[10], (KTOT,), ((0, 4),), -0.2, 0.2), 0.0, 1.0)
    frequencies = jnp.clip(jnp.exp(math.log(0.2) - 2.3025851 * jax.random.uniform(seeds[11], (QTOT, MODES), jnp.float32) ** level_of(seeds[11], (QTOT, MODES), ((0, 8),), -0.2, 0.2)), 0.02, 0.2)
    bose_factors = jnp.clip(jnp.exp(math.log(5.0) - 3.912023 * jax.random.uniform(seeds[12], (QTOT, MODES), jnp.float32) ** level_of(seeds[12], (QTOT, MODES), ((0, 8),), -0.2, 0.2)), 0.1, 5.0)
    return {"coupling": coupling, "kpoints": kpoints, "qpoints": qpoints, "electron_cells": electron_cells, "phonon_cells": phonon_cells, "phonon_modes": phonon_modes, "band_vectors": band_vectors, "energies_kq": energies_kq, "occupations_kq": occupations_kq, "energy_k": energy_k, "occupation_k": occupation_k, "frequencies": frequencies, "bose_factors": bose_factors}


smearing = 0.05

def phase_table(points, cells):
    product = points[0][:, None] * cells[0][None, :] + points[1][:, None] * cells[1][None, :] + points[2][:, None] * cells[2][None, :]
    angle = jnp.mod(product, NG).astype(jnp.float32) * (2.0 * math.pi / NG)
    return (jnp.cos(angle).astype(jnp.bfloat16), jnp.sin(angle).astype(jnp.bfloat16))

def gaussian(offset):
    return jnp.exp(-0.5 * (offset / smearing) ** 2) / (smearing * math.sqrt(2.0 * math.pi))

def contract_last(left, right):
    return lax.dot_general(left, right, (((1,), (1,)), ((), ())), preferred_element_type=jnp.float32)

def floated(form, left, right):
    return jnp.einsum(form, left.astype(jnp.float32), right.astype(jnp.float32))

def widths(bloch_real, bloch_imag, modes, vectors, levels, filled, energy_k, occupation_k, omega, bose):
    mode_real = modes[:, 0]
    mode_imag = modes[:, 1]
    moded_real = (floated('kqnm,qmv->kqnv', bloch_real, mode_real) - floated('kqnm,qmv->kqnv', bloch_imag, mode_imag)).astype(jnp.bfloat16)
    moded_imag = (floated('kqnm,qmv->kqnv', bloch_real, mode_imag) + floated('kqnm,qmv->kqnv', bloch_imag, mode_real)).astype(jnp.bfloat16)
    vector_real = vectors[:, :, 0]
    vector_imag = vectors[:, :, 1]
    band_real = floated('qknb,kqnv->kqbv', vector_real, moded_real) + floated('qknb,kqnv->kqbv', vector_imag, moded_imag)
    band_imag = floated('qknb,kqnv->kqbv', vector_real, moded_imag) - floated('qknb,kqnv->kqbv', vector_imag, moded_real)
    weight = band_real * band_real + band_imag * band_imag
    level_kq = jnp.transpose(levels, (1, 0, 2))[..., None]
    filled_kq = jnp.transpose(filled, (1, 0, 2))[..., None]
    offset = energy_k[:, None, None, None] - level_kq
    freq = omega[None, :, None, :]
    boson = bose[None, :, None, :]
    absorb = gaussian(offset + freq)
    emit = gaussian(offset - freq)
    electron = lax.optimization_barrier(jnp.sum(weight * ((boson + filled_kq) * absorb + (boson + 1.0 - filled_kq) * emit), axis=(1, 2)))
    phonon = lax.optimization_barrier(jnp.sum(weight * (occupation_k[:, None, None, None] - filled_kq) * absorb, axis=(0, 2)))
    return (electron, phonon)

def reference(coupling, kpoints, qpoints, electron_cells, phonon_cells, phonon_modes, band_vectors, energies_kq, occupations_kq, energy_k, occupation_k, frequencies, bose_factors):
    cos_k, sin_k = phase_table(kpoints, electron_cells)
    cos_q, sin_q = phase_table(qpoints, phonon_cells)
    real_flat = coupling[0].reshape(CE * PAIRS, CP)
    imag_flat = coupling[1].reshape(CE * PAIRS, CP)
    count = QTOT // QD

    def block_step(total, index):
        start = (index * QD).astype(jnp.int32)
        cos_block = lax.dynamic_slice_in_dim(cos_q, start, QD, 0)
        sin_block = lax.dynamic_slice_in_dim(sin_q, start, QD, 0)
        half_real = (contract_last(cos_block, real_flat) - contract_last(sin_block, imag_flat)).astype(jnp.bfloat16).reshape(QD, CE, PAIRS)
        half_imag = (contract_last(cos_block, imag_flat) + contract_last(sin_block, real_flat)).astype(jnp.bfloat16).reshape(QD, CE, PAIRS)
        bloch_real = (floated('kr,qrp->kqp', cos_k, half_real) - floated('kr,qrp->kqp', sin_k, half_imag)).astype(jnp.bfloat16)
        bloch_imag = (floated('kr,qrp->kqp', cos_k, half_imag) + floated('kr,qrp->kqp', sin_k, half_real)).astype(jnp.bfloat16)
        bloch_real = bloch_real.reshape(KTOT, QD, NB, MODES)
        bloch_imag = bloch_imag.reshape(KTOT, QD, NB, MODES)
        electron, phonon = widths(bloch_real, bloch_imag, lax.dynamic_slice_in_dim(phonon_modes, start, QD, 0), lax.dynamic_slice_in_dim(band_vectors, start, QD, 0), lax.dynamic_slice_in_dim(energies_kq, start, QD, 0), lax.dynamic_slice_in_dim(occupations_kq, start, QD, 0), energy_k, occupation_k, lax.dynamic_slice_in_dim(frequencies, start, QD, 0), lax.dynamic_slice_in_dim(bose_factors, start, QD, 0))
        return (total + electron / (QTOT * NB), phonon / (KTOT * NB))
    initial = jnp.zeros((KTOT, MODES), jnp.float32)
    electron_width, phonon_blocks = lax.scan(block_step, initial, jnp.arange(count, dtype=jnp.int32))
    return (electron_width, phonon_blocks.reshape(QTOT, MODES))
```

```python
import functools
import math

import jax
import jax.numpy as jnp
from jax import lax
from jax.experimental import pallas as pl
from jax.experimental.pallas import tpu as pltpu
from jax.sharding import PartitionSpec as P

NB = 40
MODES = 120
NG = 100


smearing = 0.05


def phase_table(points, cells):
    product = (
        points[0][:, None] * cells[0][None, :]
        + points[1][:, None] * cells[1][None, :]
        + points[2][:, None] * cells[2][None, :]
    )
    angle = jnp.mod(product, NG).astype(jnp.float32) * (2.0 * math.pi / NG)
    return (jnp.cos(angle).astype(jnp.bfloat16), jnp.sin(angle).astype(jnp.bfloat16))


def gaussian(offset):
    return jnp.exp(-0.5 * (offset / smearing) ** 2) / (smearing * math.sqrt(2.0 * math.pi))


def contract_last(left, right):
    return lax.dot_general(
        left, right, (((1,), (1,)), ((), ())), preferred_element_type=jnp.float32
    )


def mixed(form, left, right):
    return jnp.einsum(form, left, right, preferred_element_type=jnp.float32)


def widths(
    bloch_real, bloch_imag, modes, vectors, levels, filled, energy_k, occupation_k, omega, bose
):
    mode_real = modes[:, 0]
    mode_imag = modes[:, 1]
    moded_real = (
        mixed("kqnm,qmv->kqnv", bloch_real, mode_real)
        - mixed("kqnm,qmv->kqnv", bloch_imag, mode_imag)
    ).astype(jnp.bfloat16)
    moded_imag = (
        mixed("kqnm,qmv->kqnv", bloch_real, mode_imag)
        + mixed("kqnm,qmv->kqnv", bloch_imag, mode_real)
    ).astype(jnp.bfloat16)
    vector_real = vectors[:, :, 0]
    vector_imag = vectors[:, :, 1]
    band_real = mixed("qknb,kqnv->kqbv", vector_real, moded_real) + mixed(
        "qknb,kqnv->kqbv", vector_imag, moded_imag
    )
    band_imag = mixed("qknb,kqnv->kqbv", vector_real, moded_imag) - mixed(
        "qknb,kqnv->kqbv", vector_imag, moded_real
    )
    weight = band_real * band_real + band_imag * band_imag
    level_kq = jnp.transpose(levels, (1, 0, 2))[..., None]
    filled_kq = jnp.transpose(filled, (1, 0, 2))[..., None]
    offset = energy_k[:, None, None, None] - level_kq
    freq = omega[None, :, None, :]
    boson = bose[None, :, None, :]
    absorb = gaussian(offset + freq)
    emit = gaussian(offset - freq)
    electron = jnp.sum(
        weight * ((boson + filled_kq) * absorb + (boson + 1.0 - filled_kq) * emit), axis=(1, 2)
    )
    phonon = jnp.sum(weight * (occupation_k[:, None, None, None] - filled_kq) * absorb, axis=(0, 2))
    return (electron, phonon)


MESH = pl.DeviceIdType.MESH
LANES = 128


def bloch_kernel(
    cells_block, tile, last, wq_ref, wk_ref, x_ref, out_ref,
    half, parts, recv, send_sem, recv_sem,
):
    pairs_step = pl.program_id(0)
    cell_step = pl.program_id(1)
    tiles = pl.num_programs(0)
    cell_steps = pl.num_programs(1)
    bands, kas = lax.axis_size("pb"), lax.axis_size("ka")
    devices = bands * kas
    me = lax.axis_index("pb") * kas + lax.axis_index("ka")
    columns = wq_ref.shape[0]
    cells = half.shape[1] // columns
    groups = parts.shape[2]
    mine = groups // bands
    rows = parts.shape[3] // 2
    barrier = pltpu.get_barrier_semaphore()

    @pl.when((pairs_step == 0) & (cell_step == 0))
    def _():
        def greet(step, carry):
            peer = lax.rem(me + step, devices)
            pl.semaphore_signal(
                barrier, inc=1, device_id={"pb": peer // kas, "ka": lax.rem(peer, kas)},
                device_id_type=MESH,
            )
            return carry

        lax.fori_loop(1, devices, greet, 0)

    for cell in range(cells_block):
        right = jnp.concatenate([x_ref[0, cell], x_ref[1, cell]], axis=0)
        product = jnp.dot(wq_ref[...], right, preferred_element_type=jnp.float32)
        row = cell_step * cells_block + cell
        for lane in range(tile // LANES):
            half[lane, pl.ds(row, columns, stride=cells), :] = product[
                :, lane * LANES : (lane + 1) * LANES
            ]

    def strip(index):
        start = pl.multiple_of(index * cells, cells)
        return jnp.concatenate(
            [half[lane, pl.ds(start, cells), :] for lane in range(tile // LANES)], axis=1
        ).astype(jnp.bfloat16)

    @pl.when(cell_step == cell_steps - 1)
    def _():
        def contract(group, carry):
            sums = []
            for member in range(2):
                q = group * 2 + member
                right = jnp.concatenate([strip(q), strip(columns // 2 + q)], axis=0)
                sums.append(
                    jnp.dot(wk_ref[...], right, preferred_element_type=jnp.float32)
                )
            for ka in range(kas):
                block = slice(ka * rows, (ka + 1) * rows)
                parts[pairs_step, ka, group] = jnp.concatenate(
                    [sums[0][block], sums[1][block]], axis=0
                ).astype(jnp.bfloat16)
            return carry

        lax.fori_loop(0, groups, contract, 0, unroll=4)

    @pl.when((cell_step == cell_steps - 1) & (pairs_step == 0))
    def _():
        pl.semaphore_wait(barrier, devices - 1)

    def send(index, width):
        def one(step, carry):
            peer = lax.rem(me + step, devices)
            to_pb, to_ka = peer // kas, lax.rem(peer, kas)
            pltpu.make_async_remote_copy(
                src_ref=parts.at[index, to_ka, pl.ds(to_pb * mine, mine), :, pl.ds(0, width)],
                dst_ref=recv.at[index, me, :, :, pl.ds(0, width)],
                send_sem=send_sem.at[index],
                recv_sem=recv_sem.at[index],
                device_id={"pb": to_pb, "ka": to_ka},
                device_id_type=MESH,
            ).start()
            return carry

        lax.fori_loop(1, devices, one, 0)

    @pl.when((cell_step == cell_steps - 1) & (pairs_step < tiles - 1))
    def _():
        send(pairs_step, tile)

    @pl.when((cell_step == cell_steps - 1) & (pairs_step == tiles - 1))
    def _():
        count = recv.shape[0]
        send(count - 1, last)
        my_pb, my_ka = lax.axis_index("pb"), lax.axis_index("ka")
        for index in range(count):
            recv[index, me] = parts[index, my_ka, pl.ds(my_pb * mine, mine)]
        for index in range(count):
            width = tile if index < count - 1 else last
            window = recv.at[index, pl.ds(1, devices - 1), :, :, pl.ds(0, width)]
            pltpu.make_async_copy(window, window, send_sem.at[index]).wait()
            pltpu.make_async_copy(window, window, recv_sem.at[index]).wait()
            for band in range(bands):
                total = recv[index, band * kas, :, :, :width].astype(jnp.float32)
                for ka in range(1, kas):
                    total = total + recv[index, band * kas + ka, :, :, :width].astype(jnp.float32)
                out_ref[band, :, :, index * tile : index * tile + width] = total.astype(
                    jnp.bfloat16
                )


def bloch(coupling, wq, wk, q_local, k_local):
    bands, kas = lax.axis_size("pb"), lax.axis_size("ka")
    devices = bands * kas
    parts_count, cells, pairs, phonons = coupling.shape
    moved = jnp.transpose(coupling, (0, 1, 3, 2))
    padded = -(-pairs // LANES) * LANES
    if pairs < LANES:
        moved = jnp.pad(moved, ((0, 0), (0, 0), (0, 0), (0, LANES - pairs)))
    tile = min(2 * LANES, padded)
    tiles = -(-padded // tile)
    last = padded - (tiles - 1) * tile
    cells_block = 16
    columns = wq.shape[0]
    groups = columns // 4
    mine = q_local // 2
    rows = 4 * k_local
    result = pl.pallas_call(
        functools.partial(bloch_kernel, cells_block, tile, last),
        grid=(tiles, cells // cells_block),
        in_specs=[
            pl.BlockSpec(wq.shape, lambda t, e: (0, 0)),
            pl.BlockSpec(wk.shape, lambda t, e: (0, 0)),
            pl.BlockSpec((parts_count, cells_block, phonons, tile), lambda t, e: (0, e, 0, t)),
        ],
        out_specs=pl.BlockSpec((bands, mine, rows, padded), lambda t, e: (0, 0, 0, 0)),
        out_shape=jax.ShapeDtypeStruct((bands, mine, rows, padded), jnp.bfloat16),
        scratch_shapes=[
            pltpu.VMEM((tile // LANES, columns * cells, LANES), jnp.float32),
            pltpu.VMEM((tiles, kas, groups, rows, tile), jnp.bfloat16),
            pltpu.VMEM((tiles, devices, mine, rows, tile), jnp.bfloat16),
            pltpu.SemaphoreType.DMA((tiles,)),
            pltpu.SemaphoreType.DMA((tiles,)),
        ],
        compiler_params=pltpu.CompilerParams(
            collective_id=0,
            has_side_effects=True,
            dimension_semantics=("arbitrary", "arbitrary"),
            vmem_limit_bytes=60 * 1024 * 1024,
        ),
        name="bloch",
    )(wq, wk, moved)
    return result[..., :pairs]


def sums_kernel(electron_ref, phonon_ref, electron_out, phonon_out, got_e, got_p, send, recv_e, recv_p):
    bands, kas = lax.axis_size("pb"), lax.axis_size("ka")
    my_pb, my_ka = lax.axis_index("pb"), lax.axis_index("ka")
    barrier = pltpu.get_barrier_semaphore()
    for step in range(1, bands):
        pl.semaphore_signal(
            barrier, inc=1, device_id={"pb": lax.rem(my_pb + step, bands), "ka": my_ka},
            device_id_type=MESH,
        )
    for step in range(1, kas):
        pl.semaphore_signal(
            barrier, inc=1, device_id={"pb": my_pb, "ka": lax.rem(my_ka + step, kas)},
            device_id_type=MESH,
        )
    pl.semaphore_wait(barrier, bands + kas - 2)
    copies = []
    for step in range(1, bands):
        copies.append(pltpu.make_async_remote_copy(
            electron_ref, got_e.at[my_pb], send.at[step - 1], recv_e.at[step - 1],
            device_id={"pb": lax.rem(my_pb + step, bands), "ka": my_ka}, device_id_type=MESH,
        ))
    for step in range(1, kas):
        copies.append(pltpu.make_async_remote_copy(
            phonon_ref, got_p.at[my_ka], send.at[bands + step - 2], recv_p.at[step - 1],
            device_id={"pb": my_pb, "ka": lax.rem(my_ka + step, kas)}, device_id_type=MESH,
        ))
    for copy in copies:
        copy.start()
    got_e[my_pb] = electron_ref[...]
    got_p[my_ka] = phonon_ref[...]
    for copy in copies:
        copy.wait()
    total = got_e[0]
    for step in range(1, bands):
        total = total + got_e[step]
    electron_out[...] = total
    total = got_p[0]
    for step in range(1, kas):
        total = total + got_p[step]
    phonon_out[...] = total


def exchange(electron, phonon):
    bands, kas = lax.axis_size("pb"), lax.axis_size("ka")
    whole = pl.BlockSpec(memory_space=pltpu.VMEM)
    return pl.pallas_call(
        sums_kernel,
        in_specs=[whole, whole],
        out_specs=[whole, whole],
        out_shape=[
            jax.ShapeDtypeStruct(electron.shape, electron.dtype),
            jax.ShapeDtypeStruct(phonon.shape, phonon.dtype),
        ],
        scratch_shapes=[
            pltpu.VMEM((bands, *electron.shape), jnp.float32),
            pltpu.VMEM((kas, *phonon.shape), jnp.float32),
            pltpu.SemaphoreType.DMA((bands + kas - 2,)),
            pltpu.SemaphoreType.DMA((bands - 1,)),
            pltpu.SemaphoreType.DMA((kas - 1,)),
        ],
        compiler_params=pltpu.CompilerParams(collective_id=1, has_side_effects=True),
        name="sums",
    )(electron, phonon)


def angles(points, cells):
    product = lax.dot_general(
        points.astype(jnp.float32).astype(jnp.bfloat16),
        cells.astype(jnp.float32).astype(jnp.bfloat16),
        (((0,), (0,)), ((), ())),
        preferred_element_type=jnp.float32,
    )
    turns = jnp.floor((product + 0.5) * (1.0 / NG))
    angle = (product - turns * NG) * (2.0 * math.pi / NG)
    return jnp.cos(angle), jnp.sin(angle)


def ring_kernel(
    pairs, kpoints, qpoints, electron_cells, phonon_cells, modes, vectors,
    levels, filled, energy_k, occupation_k, omega, bose, edge_ref, x_hbm, out_ref,
    wq, wk, half, ring, parts, recv, relay, sums, table, lifted, rows_ref, turned,
    emission, absorption, totals, got_e, got_p,
    ring_sem, relay_send, relay_recv, plane_send, plane_recv, raw_send, raw_recv,
    sum_send, sum_recv, send_e, recv_e, send_p, recv_p,
):
    step = pl.program_id(0)
    steps = pl.num_programs(0)
    bands, kas = lax.axis_size("pb"), lax.axis_size("ka")
    devices = bands * kas
    my_pb, my_ka = lax.axis_index("pb"), lax.axis_index("ka")
    me = my_pb * kas + my_ka
    columns = wq.shape[0]
    q_total = columns // 2
    cells = half.shape[0] // columns
    slots, unit = ring.shape[0], ring.shape[2]
    chunks = cells // unit
    tiles = parts.shape[0]
    halves = parts.shape[3]
    mine = 2 * halves
    q_local, k_local = vectors.shape[0], vectors.shape[1]
    rows = 2 * k_local
    bands_n = vectors.shape[3]
    bands_own = bands_n // bands
    up, down = lax.rem(my_ka + 1, kas), lax.rem(my_ka + kas - 1, kas)
    across = lax.rem(my_ka + 2, kas)
    barrier = pltpu.get_barrier_semaphore()
    overlaps = []
    for tile in range(tiles):
        for n in range(bands_own):
            low = max(tile * LANES, n * MODES)
            high = min((tile + 1) * LANES, (n + 1) * MODES)
            if low < high:
                overlaps.append((tile, n, low - tile * LANES, low - n * MODES, high - low))

    def fetch(index, slot):
        tile, chunk = index // chunks, lax.rem(index, chunks)
        return pltpu.make_async_copy(
            x_hbm.at[
                :, pl.ds(chunk * unit, unit), :, pl.ds(pl.multiple_of(tile * LANES, LANES), LANES)
            ],
            ring.at[slot],
            ring_sem.at[slot],
        )

    def project(real, imag, row):
        right = jnp.concatenate([real, imag], axis=0)
        product = jnp.dot(wq[...], right, preferred_element_type=jnp.float32)
        half[pl.ds(row, columns, stride=cells), :] = product

    def strip(index):
        return half[index * cells : (index + 1) * cells, :].astype(jnp.bfloat16)

    def contract(order):
        for group in range(q_total // 2):
            products = []
            for member in range(2):
                q = group * 2 + member
                right = jnp.concatenate([strip(q), strip(q_total + q)], axis=0)
                products.append(jnp.dot(wk[...], right, preferred_element_type=jnp.float32))
            m = group % mine
            for ka in range(kas):
                block = slice(ka * rows, (ka + 1) * rows)
                parts[order, ka, m // halves, m % halves, group // mine] = jnp.concatenate(
                    [products[0][block], products[1][block]], axis=0
                ).astype(jnp.bfloat16)

    def put(source, target, send_sem, recv_sem, to_pb, to_ka):
        pltpu.make_async_remote_copy(
            src_ref=source, dst_ref=target, send_sem=send_sem, recv_sem=recv_sem,
            device_id={"pb": to_pb, "ka": to_ka}, device_id_type=MESH,
        ).start()

    def settle(window, sem):
        pltpu.make_async_copy(window, window, sem).wait()

    def send(order):
        put(parts.at[order, across, 0], relay.at[order, 0], relay_send.at[0, order],
            relay_recv.at[0, order], my_pb, up)
        put(parts.at[order, across, 1], relay.at[order, 1], relay_send.at[1, order],
            relay_recv.at[1, order], my_pb, down)

        def raw(index, carry):
            to = lax.rem(my_pb + index, bands)
            put(parts.at[order, up, 1, :, to], recv.at[order, 1, 1, :, my_pb],
                raw_send.at[0, order], raw_recv.at[0, order], to, up)
            put(parts.at[order, down, 0, :, to], recv.at[order, 2, 0, :, my_pb],
                raw_send.at[1, order], raw_recv.at[1, order], to, down)
            return carry

        lax.fori_loop(0, bands, raw, 0)

        def plane(index, carry):
            to = lax.rem(my_pb + index, bands)
            put(parts.at[order, my_ka, :, :, to], recv.at[order, 0, :, :, my_pb],
                plane_send.at[order], plane_recv.at[order], to, my_ka)
            return carry

        lax.fori_loop(1, bands, plane, 0)

    def pass_on(order):
        for way, (target, place) in enumerate(((up, 1), (down, 2))):
            settle(relay.at[order, way], relay_recv.at[way, order])
            own = parts[order, target, way].astype(jnp.float32)
            sums[order, way] = (own + relay[order, way].astype(jnp.float32)).astype(jnp.bfloat16)

            def one(index, carry, way=way, target=target, place=place):
                to = lax.rem(my_pb + index, bands)
                put(sums.at[order, way, :, to], recv.at[order, place, way, :, my_pb],
                    sum_send.at[way, order], sum_recv.at[way, order], to, target)
                return carry

            lax.fori_loop(0, bands, one, 0)

    edge_cells = edge_ref.shape[1]

    def edge(index, carry):
        for inner in range(unit):
            cell = index * unit + inner
            project(edge_ref[0, cell], edge_ref[1, cell], step * edge_cells + cell)
        return carry

    @pl.when(step == 0)
    def _():
        def greet(index, carry):
            peer = lax.rem(me + index, devices)
            pl.semaphore_signal(
                barrier, inc=1, device_id={"pb": peer // kas, "ka": lax.rem(peer, kas)},
                device_id_type=MESH,
            )
            return carry

        lax.fori_loop(1, devices, greet, 0)

        def first(index, carry):
            fetch(index, index).start()
            return carry

        lax.fori_loop(0, slots, first, 0)
        cos, sin = angles(qpoints[...], phonon_cells[...])
        wq[...] = jnp.concatenate(
            [jnp.concatenate([cos, -sin], 1), jnp.concatenate([sin, cos], 1)], 0
        ).astype(jnp.bfloat16)
        cells_all = electron_cells[...]
        own = cells_all[:, :cells]
        for ka in range(1, kas):
            own = jnp.where(my_ka == ka, cells_all[:, ka * cells : (ka + 1) * cells], own)
        cos, sin = angles(kpoints[...], own)
        blocks = []
        for ka in range(kas):
            c = cos[ka * k_local : (ka + 1) * k_local]
            s = sin[ka * k_local : (ka + 1) * k_local]
            blocks += [jnp.concatenate([c, -s], 1), jnp.concatenate([s, c], 1)]
        wk[...] = jnp.concatenate(blocks, 0).astype(jnp.bfloat16)

    lax.fori_loop(0, edge_cells // unit, edge, 0)

    @pl.when(step == 0)
    def _():
        for q in range(q_local):
            freq = omega[q : q + 1, :]
            boson = bose[q : q + 1, :]
            level_q = jnp.transpose(levels[q])
            filled_q = jnp.transpose(filled[q])
            for k in range(k_local):
                f = filled_q[:, k : k + 1]
                offset = energy_k[k] - level_q[:, k : k + 1]
                absorb = gaussian(offset + freq)
                emit = gaussian(offset - freq)
                emission[q, k] = (boson + f) * absorb + (boson + 1.0 - f) * emit
                absorption[q, k] = (occupation_k[k] - f) * absorb
                for part in range(2):
                    rows_ref[part, :, :bands_n] = vectors[q, k, part].astype(jnp.float32)
                real, imag = (
                    jnp.concatenate(
                        [
                            rows_ref[part, pl.ds(n, bands, stride=bands_own), :]
                            for n in range(bands_own)
                        ],
                        axis=0,
                    )[:, :bands_n]
                    for part in range(2)
                )
                both = jnp.concatenate(
                    [jnp.concatenate([real, -imag], 1), jnp.concatenate([imag, real], 1)], 0
                )
                turned[q, k] = jnp.transpose(both).astype(jnp.bfloat16)
            for part in range(2):
                mode = modes[q, part].astype(jnp.float32)
                for index, (tile, n, row, start, count) in enumerate(overlaps):
                    pieces = []
                    if row:
                        pieces.append(jnp.zeros((row, MODES), jnp.float32))
                    pieces.append(mode[start : start + count])
                    if row + count < LANES:
                        pieces.append(jnp.zeros((LANES - row - count, MODES), jnp.float32))
                    placed = jnp.concatenate(pieces, 0) if len(pieces) > 1 else pieces[0]
                    table[q, index, :, part * LANES : part * LANES + MODES] = placed.astype(
                        jnp.bfloat16
                    )

    @pl.when(step == steps - 1)
    def _():
        contract(0)
        pl.semaphore_wait(barrier, devices - 1)
        send(0)

        def one_tile(tile, carry):
            def one_chunk(chunk, inner_carry):
                index = tile * chunks + chunk
                slot = lax.rem(index, slots)
                fetch(index, slot).wait()
                for inner in range(unit):
                    project(ring[slot, 0, inner], ring[slot, 1, inner], chunk * unit + inner)

                @pl.when(index + slots < (tiles - 1) * chunks)
                def _():
                    fetch(index + slots, slot).start()

                return inner_carry

            lax.fori_loop(0, chunks, one_chunk, 0)
            contract(tile + 1)
            send(tile + 1)
            pass_on(tile)
            return carry

        lax.fori_loop(0, tiles - 1, one_tile, 0)
        for order in range(tiles):
            recv[order, 0, :, :, my_pb] = parts[order, my_ka, :, :, my_pb]
        pass_on(tiles - 1)
        lane = lax.broadcasted_iota(jnp.int32, (1, LANES), 1)
        started = set()
        for order in range(tiles):
            tile = tiles - 1 if order == 0 else order - 1
            settle(recv.at[order, 0, :, :, pl.ds(1, bands - 1)], plane_recv.at[order])
            for way in range(2):
                settle(recv.at[order, 1 + way, 1 - way], raw_recv.at[way, order])
            for way in range(2):
                settle(recv.at[order, 1 + way, way], sum_recv.at[way, order])
            for m in range(mine):
                spot = (m // halves, m % halves)
                total = [
                    recv[order, 0, *spot, band].astype(jnp.float32)
                    + recv[order, 1, *spot, band].astype(jnp.float32)
                    + recv[order, 2, *spot, band].astype(jnp.float32)
                    for band in range(bands)
                ]
                for member in range(2):
                    q = 2 * m + member
                    left = jnp.concatenate(
                        [one[member * rows : (member + 1) * rows] for one in total], axis=0
                    )
                    if pairs < (tile + 1) * LANES:
                        left = jnp.where(lane < pairs - tile * LANES, left, 0.0)
                    left = left.astype(jnp.bfloat16)
                    for index, (other, n, _, _, _) in enumerate(overlaps):
                        if other != tile:
                            continue
                        product = jnp.dot(
                            left, table[q, index], preferred_element_type=jnp.float32
                        )
                        for side in range(2):
                            value = product[:, side * LANES : (side + 1) * LANES]
                            if (q, n) in started:
                                value = value + lifted[q, n, side]
                            lifted[q, n, side] = value
                        started.add((q, n))
        electron = [None] * k_local
        for q in range(q_local):
            phonon = None
            for k in range(k_local):
                real, imag = [], []
                for n in range(bands_own):
                    rr, ri, ir, ii = (
                        lifted[q, n, side, pl.ds(part * k_local + k, bands, stride=rows), :]
                        for part in range(2)
                        for side in range(2)
                    )
                    real.append(rr - ii)
                    imag.append(ri + ir)
                right = jnp.concatenate(real + imag, axis=0).astype(jnp.bfloat16)
                band = jnp.dot(turned[q, k], right, preferred_element_type=jnp.float32)
                band_real = band[:bands_n, :MODES]
                band_imag = band[bands_n:, :MODES]
                weight = band_real * band_real + band_imag * band_imag
                e_term = weight * emission[q, k]
                p_term = weight * absorption[q, k]
                electron[k] = e_term if q == 0 else electron[k] + e_term
                phonon = p_term if k == 0 else phonon + p_term
            totals[1, q : q + 1, :] = jnp.sum(phonon, axis=0, keepdims=True)
        for k in range(k_local):
            totals[0, k : k + 1, :] = jnp.sum(electron[k], axis=0, keepdims=True)
        copies = []
        for shift in range(1, bands):
            copies.append(pltpu.make_async_remote_copy(
                totals.at[0], got_e.at[my_pb], send_e.at[shift - 1], recv_e.at[shift - 1],
                device_id={"pb": lax.rem(my_pb + shift, bands), "ka": my_ka}, device_id_type=MESH,
            ))
        for shift in range(1, kas):
            copies.append(pltpu.make_async_remote_copy(
                totals.at[1], got_p.at[my_ka], send_p.at[shift - 1], recv_p.at[shift - 1],
                device_id={"pb": my_pb, "ka": lax.rem(my_ka + shift, kas)}, device_id_type=MESH,
            ))
        for copy in copies:
            copy.start()
        got_e[my_pb] = totals[0]
        got_p[my_ka] = totals[1]
        for order in range(tiles):
            settle(recv.at[order, 0, :, :, pl.ds(1, bands - 1)], plane_send.at[order])
            for way in range(2):
                settle(relay.at[order, way], relay_send.at[way, order])
                settle(recv.at[order, 1 + way, 1 - way], raw_send.at[way, order])
                settle(recv.at[order, 1 + way, way], sum_send.at[way, order])
        for copy in copies:
            copy.wait()
        total = got_e[0]
        for other in range(1, bands):
            total = total + got_e[other]
        out_ref[0] = total
        total = got_p[0]
        for other in range(1, kas):
            total = total + got_p[other]
        out_ref[1] = total


def everything(
    coupling, kpoints, qpoints, electron_cells, phonon_cells, phonon_modes, band_vectors,
    energies_kq, occupations_kq, energy_k, occupation_k, frequencies, bose_factors,
):
    bands, kas = lax.axis_size("pb"), lax.axis_size("ka")
    parts_count, cells, pairs, phonons = coupling.shape
    moved = jnp.transpose(coupling, (0, 1, 3, 2))
    tiles = -(-pairs // LANES)
    unit = cells // 4
    slots = 8
    q_local, k_local = band_vectors.shape[0], band_vectors.shape[1]
    bands_n = band_vectors.shape[3]
    columns = 2 * qpoints.shape[1]
    halves = q_local // 4
    rows = 4 * k_local
    bands_own = bands_n // bands
    overlaps = sum(
        max(t * LANES, n * MODES) < min((t + 1) * LANES, (n + 1) * MODES)
        for t in range(tiles)
        for n in range(bands_own)
    )
    small = pl.BlockSpec(memory_space=pltpu.VMEM)
    scalars = pl.BlockSpec(memory_space=pltpu.SMEM)
    dma = pltpu.SemaphoreType.DMA
    bf16, f32 = jnp.bfloat16, jnp.float32
    return pl.pallas_call(
        functools.partial(ring_kernel, pairs),
        grid=(2,),
        in_specs=[small] * 8
        + [scalars] * 2
        + [small] * 2
        + [
            pl.BlockSpec((parts_count, cells // 2, phonons, LANES), lambda e: (0, e, 0, tiles - 1)),
            pl.BlockSpec(memory_space=pl.ANY),
        ],
        out_specs=small,
        out_shape=jax.ShapeDtypeStruct((2, k_local, MODES), f32),
        scratch_shapes=[
            pltpu.VMEM((columns, 2 * phonons), bf16),
            pltpu.VMEM((2 * k_local * kas, 2 * cells), bf16),
            pltpu.VMEM((columns * cells, LANES), f32),
            pltpu.VMEM((slots, parts_count, unit, phonons, LANES), bf16),
            pltpu.VMEM((tiles, kas, 2, halves, bands, rows, LANES), bf16),
            pltpu.VMEM((tiles, 3, 2, halves, bands, rows, LANES), bf16),
            pltpu.VMEM((tiles, 2, halves, bands, rows, LANES), bf16),
            pltpu.VMEM((tiles, 2, halves, bands, rows, LANES), bf16),
            pltpu.VMEM((q_local, overlaps, LANES, 2 * LANES), bf16),
            pltpu.VMEM((q_local, bands_own, 2, bands * 2 * k_local, LANES), f32),
            pltpu.VMEM((2, bands_n, LANES), f32),
            pltpu.VMEM((q_local, k_local, 2 * bands_n, 2 * bands_n), bf16),
            pltpu.VMEM((q_local, k_local, bands_n, MODES), f32),
            pltpu.VMEM((q_local, k_local, bands_n, MODES), f32),
            pltpu.VMEM((2, k_local, MODES), f32),
            pltpu.VMEM((bands, k_local, MODES), f32),
            pltpu.VMEM((kas, k_local, MODES), f32),
            dma((slots,)),
            dma((2, tiles)),
            dma((2, tiles)),
            dma((tiles,)),
            dma((tiles,)),
            dma((2, tiles)),
            dma((2, tiles)),
            dma((2, tiles)),
            dma((2, tiles)),
            dma((bands - 1,)),
            dma((bands - 1,)),
            dma((kas - 1,)),
            dma((kas - 1,)),
        ],
        compiler_params=pltpu.CompilerParams(
            collective_id=2,
            has_side_effects=True,
            dimension_semantics=("arbitrary",),
            vmem_limit_bytes=60 * 1024 * 1024,
        ),
        name="widths",
    )(
        kpoints, qpoints, electron_cells, phonon_cells, phonon_modes, band_vectors, energies_kq,
        occupations_kq, energy_k, occupation_k, frequencies, bose_factors, moved, moved,
    )


def on_device(
    coupling,
    kpoints,
    qpoints,
    electron_cells,
    phonon_cells,
    phonon_modes,
    band_vectors,
    energies_kq,
    occupations_kq,
    energy_k,
    occupation_k,
    frequencies,
    bose_factors,
):
    k_local = energy_k.shape[0]
    q_local = frequencies.shape[0]
    cells_local = coupling.shape[1]
    bands, kas = lax.axis_size("pb"), lax.axis_size("ka")
    q_total = q_local * bands
    k_total = k_local * kas
    whole_bands = coupling.shape[2] % MODES == 0 and coupling.shape[2] > LANES
    even = q_local % 4 == 0 and cells_local % 16 == 0
    if kas == 4 and whole_bands and even and k_local == q_local:
        sums = everything(
            coupling, kpoints, qpoints, electron_cells, phonon_cells, phonon_modes, band_vectors,
            energies_kq, occupations_kq, energy_k, occupation_k, frequencies, bose_factors,
        )
        return (sums[0] / (q_total * NB), sums[1] / (k_total * NB))
    cos_q, sin_q = phase_table(qpoints, phonon_cells)
    own_cells = lax.dynamic_slice_in_dim(
        electron_cells, lax.axis_index("ka") * cells_local, cells_local, 1
    )
    cos_k, sin_k = phase_table(kpoints, own_cells)
    wq = jnp.concatenate(
        [jnp.concatenate([cos_q, -sin_q], 1), jnp.concatenate([sin_q, cos_q], 1)], 0
    )
    wk = jnp.stack(
        [jnp.concatenate([cos_k, -sin_k], 1), jnp.concatenate([sin_k, cos_k], 1)], 1
    ).reshape(2 * k_total, 2 * cells_local)
    values = bloch(coupling, wq, wk, q_local, k_local)
    values = values.reshape(bands, q_local // 2, 2, k_local, 2, -1)
    values = jnp.transpose(values, (4, 3, 1, 2, 0, 5)).reshape(2, k_local, q_local, NB, MODES)
    electron, phonon = widths(
        values[0],
        values[1],
        phonon_modes,
        band_vectors,
        energies_kq,
        occupations_kq,
        energy_k,
        occupation_k,
        frequencies,
        bose_factors,
    )
    electron_width, phonon_width = exchange(electron / (q_total * NB), phonon / (k_total * NB))
    return (electron_width, phonon_width)


def solution(mesh):
    in_specs = (
        P(None, "ka", "pb", None),
        P(),
        P(),
        P(),
        P(),
        P("pb", None, None, None),
        P("pb", "ka", None, None, None),
        P("pb", "ka", None),
        P("pb", "ka", None),
        P("ka"),
        P("ka"),
        P("pb", None),
        P("pb", None),
    )
    out_specs = (P("ka", None), P("pb", None))
    return jax.shard_map(
        on_device, mesh=mesh, in_specs=in_specs, out_specs=out_specs, check_vma=False
    )
```

```python
import functools
import math

import jax
import jax.numpy as jnp
from jax import lax
from jax.experimental import pallas as pl
from jax.experimental.pallas import tpu as pltpu
from jax.sharding import PartitionSpec as P

NB = 40
MODES = 120
NG = 100


smearing = 0.05


def phase_table(points, cells):
    product = (
        points[0][:, None] * cells[0][None, :]
        + points[1][:, None] * cells[1][None, :]
        + points[2][:, None] * cells[2][None, :]
    )
    angle = jnp.mod(product, NG).astype(jnp.float32) * (2.0 * math.pi / NG)
    return (jnp.cos(angle).astype(jnp.bfloat16), jnp.sin(angle).astype(jnp.bfloat16))


def gaussian(offset):
    return jnp.exp(-0.5 * (offset / smearing) ** 2) / (smearing * math.sqrt(2.0 * math.pi))


def contract_last(left, right):
    return lax.dot_general(
        left, right, (((1,), (1,)), ((), ())), preferred_element_type=jnp.float32
    )


def mixed(form, left, right):
    return jnp.einsum(form, left, right, preferred_element_type=jnp.float32)


def widths(
    bloch_real, bloch_imag, modes, vectors, levels, filled, energy_k, occupation_k, omega, bose
):
    mode_real = modes[:, 0]
    mode_imag = modes[:, 1]
    moded_real = (
        mixed("kqnm,qmv->kqnv", bloch_real, mode_real)
        - mixed("kqnm,qmv->kqnv", bloch_imag, mode_imag)
    ).astype(jnp.bfloat16)
    moded_imag = (
        mixed("kqnm,qmv->kqnv", bloch_real, mode_imag)
        + mixed("kqnm,qmv->kqnv", bloch_imag, mode_real)
    ).astype(jnp.bfloat16)
    vector_real = vectors[:, :, 0]
    vector_imag = vectors[:, :, 1]
    band_real = mixed("qknb,kqnv->kqbv", vector_real, moded_real) + mixed(
        "qknb,kqnv->kqbv", vector_imag, moded_imag
    )
    band_imag = mixed("qknb,kqnv->kqbv", vector_real, moded_imag) - mixed(
        "qknb,kqnv->kqbv", vector_imag, moded_real
    )
    weight = band_real * band_real + band_imag * band_imag
    level_kq = jnp.transpose(levels, (1, 0, 2))[..., None]
    filled_kq = jnp.transpose(filled, (1, 0, 2))[..., None]
    offset = energy_k[:, None, None, None] - level_kq
    freq = omega[None, :, None, :]
    boson = bose[None, :, None, :]
    absorb = gaussian(offset + freq)
    emit = gaussian(offset - freq)
    electron = jnp.sum(
        weight * ((boson + filled_kq) * absorb + (boson + 1.0 - filled_kq) * emit), axis=(1, 2)
    )
    phonon = jnp.sum(weight * (occupation_k[:, None, None, None] - filled_kq) * absorb, axis=(0, 2))
    return (electron, phonon)


MESH = pl.DeviceIdType.MESH
LANES = 128


def bloch_kernel(
    cells_block, tile, last, wq_ref, wk_ref, x_ref, out_ref,
    half, parts, recv, send_sem, recv_sem,
):
    pairs_step = pl.program_id(0)
    cell_step = pl.program_id(1)
    tiles = pl.num_programs(0)
    cell_steps = pl.num_programs(1)
    bands, kas = lax.axis_size("pb"), lax.axis_size("ka")
    devices = bands * kas
    me = lax.axis_index("pb") * kas + lax.axis_index("ka")
    columns = wq_ref.shape[0]
    cells = half.shape[1] // columns
    groups = parts.shape[2]
    mine = groups // bands
    rows = parts.shape[3] // 2
    barrier = pltpu.get_barrier_semaphore()

    @pl.when((pairs_step == 0) & (cell_step == 0))
    def _():
        def greet(step, carry):
            peer = lax.rem(me + step, devices)
            pl.semaphore_signal(
                barrier, inc=1, device_id={"pb": peer // kas, "ka": lax.rem(peer, kas)},
                device_id_type=MESH,
            )
            return carry

        lax.fori_loop(1, devices, greet, 0)

    for cell in range(cells_block):
        right = jnp.concatenate([x_ref[0, cell], x_ref[1, cell]], axis=0)
        product = jnp.dot(wq_ref[...], right, preferred_element_type=jnp.float32)
        row = cell_step * cells_block + cell
        for lane in range(tile // LANES):
            half[lane, pl.ds(row, columns, stride=cells), :] = product[
                :, lane * LANES : (lane + 1) * LANES
            ]

    def strip(index):
        start = pl.multiple_of(index * cells, cells)
        return jnp.concatenate(
            [half[lane, pl.ds(start, cells), :] for lane in range(tile // LANES)], axis=1
        ).astype(jnp.bfloat16)

    @pl.when(cell_step == cell_steps - 1)
    def _():
        def contract(group, carry):
            sums = []
            for member in range(2):
                q = group * 2 + member
                right = jnp.concatenate([strip(q), strip(columns // 2 + q)], axis=0)
                sums.append(
                    jnp.dot(wk_ref[...], right, preferred_element_type=jnp.float32)
                )
            for ka in range(kas):
                block = slice(ka * rows, (ka + 1) * rows)
                parts[pairs_step, ka, group] = jnp.concatenate(
                    [sums[0][block], sums[1][block]], axis=0
                ).astype(jnp.bfloat16)
            return carry

        lax.fori_loop(0, groups, contract, 0, unroll=4)

    @pl.when((cell_step == cell_steps - 1) & (pairs_step == 0))
    def _():
        pl.semaphore_wait(barrier, devices - 1)

    def send(index, width):
        def one(step, carry):
            peer = lax.rem(me + step, devices)
            to_pb, to_ka = peer // kas, lax.rem(peer, kas)
            pltpu.make_async_remote_copy(
                src_ref=parts.at[index, to_ka, pl.ds(to_pb * mine, mine), :, pl.ds(0, width)],
                dst_ref=recv.at[index, me, :, :, pl.ds(0, width)],
                send_sem=send_sem.at[index],
                recv_sem=recv_sem.at[index],
                device_id={"pb": to_pb, "ka": to_ka},
                device_id_type=MESH,
            ).start()
            return carry

        lax.fori_loop(1, devices, one, 0)

    @pl.when((cell_step == cell_steps - 1) & (pairs_step < tiles - 1))
    def _():
        send(pairs_step, tile)

    @pl.when((cell_step == cell_steps - 1) & (pairs_step == tiles - 1))
    def _():
        count = recv.shape[0]
        send(count - 1, last)
        my_pb, my_ka = lax.axis_index("pb"), lax.axis_index("ka")
        for index in range(count):
            recv[index, me] = parts[index, my_ka, pl.ds(my_pb * mine, mine)]
        for index in range(count):
            width = tile if index < count - 1 else last
            window = recv.at[index, pl.ds(1, devices - 1), :, :, pl.ds(0, width)]
            pltpu.make_async_copy(window, window, send_sem.at[index]).wait()
            pltpu.make_async_copy(window, window, recv_sem.at[index]).wait()
            for band in range(bands):
                total = recv[index, band * kas, :, :, :width].astype(jnp.float32)
                for ka in range(1, kas):
                    total = total + recv[index, band * kas + ka, :, :, :width].astype(jnp.float32)
                out_ref[band, :, :, index * tile : index * tile + width] = total.astype(
                    jnp.bfloat16
                )


def bloch(coupling, wq, wk, q_local, k_local):
    bands, kas = lax.axis_size("pb"), lax.axis_size("ka")
    devices = bands * kas
    parts_count, cells, pairs, phonons = coupling.shape
    moved = jnp.transpose(coupling, (0, 1, 3, 2))
    padded = -(-pairs // LANES) * LANES
    if pairs < LANES:
        moved = jnp.pad(moved, ((0, 0), (0, 0), (0, 0), (0, LANES - pairs)))
    tile = min(2 * LANES, padded)
    tiles = -(-padded // tile)
    last = padded - (tiles - 1) * tile
    cells_block = 16
    columns = wq.shape[0]
    groups = columns // 4
    mine = q_local // 2
    rows = 4 * k_local
    result = pl.pallas_call(
        functools.partial(bloch_kernel, cells_block, tile, last),
        grid=(tiles, cells // cells_block),
        in_specs=[
            pl.BlockSpec(wq.shape, lambda t, e: (0, 0)),
            pl.BlockSpec(wk.shape, lambda t, e: (0, 0)),
            pl.BlockSpec((parts_count, cells_block, phonons, tile), lambda t, e: (0, e, 0, t)),
        ],
        out_specs=pl.BlockSpec((bands, mine, rows, padded), lambda t, e: (0, 0, 0, 0)),
        out_shape=jax.ShapeDtypeStruct((bands, mine, rows, padded), jnp.bfloat16),
        scratch_shapes=[
            pltpu.VMEM((tile // LANES, columns * cells, LANES), jnp.float32),
            pltpu.VMEM((tiles, kas, groups, rows, tile), jnp.bfloat16),
            pltpu.VMEM((tiles, devices, mine, rows, tile), jnp.bfloat16),
            pltpu.SemaphoreType.DMA((tiles,)),
            pltpu.SemaphoreType.DMA((tiles,)),
        ],
        compiler_params=pltpu.CompilerParams(
            collective_id=0,
            has_side_effects=True,
            dimension_semantics=("arbitrary", "arbitrary"),
            vmem_limit_bytes=60 * 1024 * 1024,
        ),
        name="bloch",
    )(wq, wk, moved)
    return result[..., :pairs]


def sums_kernel(electron_ref, phonon_ref, electron_out, phonon_out, got_e, got_p, send, recv_e, recv_p):
    bands, kas = lax.axis_size("pb"), lax.axis_size("ka")
    my_pb, my_ka = lax.axis_index("pb"), lax.axis_index("ka")
    barrier = pltpu.get_barrier_semaphore()
    for step in range(1, bands):
        pl.semaphore_signal(
            barrier, inc=1, device_id={"pb": lax.rem(my_pb + step, bands), "ka": my_ka},
            device_id_type=MESH,
        )
    for step in range(1, kas):
        pl.semaphore_signal(
            barrier, inc=1, device_id={"pb": my_pb, "ka": lax.rem(my_ka + step, kas)},
            device_id_type=MESH,
        )
    pl.semaphore_wait(barrier, bands + kas - 2)
    copies = []
    for step in range(1, bands):
        copies.append(pltpu.make_async_remote_copy(
            electron_ref, got_e.at[my_pb], send.at[step - 1], recv_e.at[step - 1],
            device_id={"pb": lax.rem(my_pb + step, bands), "ka": my_ka}, device_id_type=MESH,
        ))
    for step in range(1, kas):
        copies.append(pltpu.make_async_remote_copy(
            phonon_ref, got_p.at[my_ka], send.at[bands + step - 2], recv_p.at[step - 1],
            device_id={"pb": my_pb, "ka": lax.rem(my_ka + step, kas)}, device_id_type=MESH,
        ))
    for copy in copies:
        copy.start()
    got_e[my_pb] = electron_ref[...]
    got_p[my_ka] = phonon_ref[...]
    for copy in copies:
        copy.wait()
    total = got_e[0]
    for step in range(1, bands):
        total = total + got_e[step]
    electron_out[...] = total
    total = got_p[0]
    for step in range(1, kas):
        total = total + got_p[step]
    phonon_out[...] = total


def exchange(electron, phonon):
    bands, kas = lax.axis_size("pb"), lax.axis_size("ka")
    whole = pl.BlockSpec(memory_space=pltpu.VMEM)
    return pl.pallas_call(
        sums_kernel,
        in_specs=[whole, whole],
        out_specs=[whole, whole],
        out_shape=[
            jax.ShapeDtypeStruct(electron.shape, electron.dtype),
            jax.ShapeDtypeStruct(phonon.shape, phonon.dtype),
        ],
        scratch_shapes=[
            pltpu.VMEM((bands, *electron.shape), jnp.float32),
            pltpu.VMEM((kas, *phonon.shape), jnp.float32),
            pltpu.SemaphoreType.DMA((bands + kas - 2,)),
            pltpu.SemaphoreType.DMA((bands - 1,)),
            pltpu.SemaphoreType.DMA((kas - 1,)),
        ],
        compiler_params=pltpu.CompilerParams(collective_id=1, has_side_effects=True),
        name="sums",
    )(electron, phonon)


def angles(points, cells):
    product = lax.dot_general(
        points.astype(jnp.float32).astype(jnp.bfloat16),
        cells.astype(jnp.float32).astype(jnp.bfloat16),
        (((0,), (0,)), ((), ())),
        preferred_element_type=jnp.float32,
    )
    turns = jnp.floor((product + 0.5) * (1.0 / NG))
    angle = (product - turns * NG) * (2.0 * math.pi / NG)
    return jnp.cos(angle), jnp.sin(angle)


def ring_kernel(
    pairs, kpoints, qpoints, electron_cells, phonon_cells, modes, vectors,
    levels, filled, energy_k, occupation_k, omega, bose, edge_ref, x_hbm, out_ref,
    wq, wk, half, ring, parts, from_plane, from_line, outer_in, inner_in, table, lifted,
    rows_ref, turned, emission, absorption, vectors_all, levels_all, filled_all, scalars_own,
    scalars_all, totals_e, totals_p, got_e, got_p,
    ring_sem, input_sem, input_send, input_recv, outer_send, outer_recv, inner_send, inner_recv,
    plane_send, plane_recv, line_send, line_recv, send_e, recv_e, send_p, recv_p,
):
    step = pl.program_id(0)
    steps = pl.num_programs(0)
    bands, kas = lax.axis_size("pb"), lax.axis_size("ka")
    devices = bands * kas
    my_pb, my_ka = lax.axis_index("pb"), lax.axis_index("ka")
    me = my_pb * kas + my_ka
    columns = wq.shape[0]
    q_total = columns // 2
    cells = half.shape[0] // columns
    slots, unit = ring.shape[0], ring.shape[2]
    chunks = cells // unit
    tiles = parts.shape[0]
    q_local, k_local = vectors.shape[0], vectors.shape[1]
    k_side = 2 * k_local
    rows = 2 * k_side
    chips = bands // 2
    bands_n = vectors.shape[3]
    bands_own = bands_n // bands
    side = my_ka // 2
    far = 1 - side
    owner = side * (kas - 1)
    outer = my_ka == owner
    inner = jnp.logical_not(outer)
    partner = side * kas // 2 + lax.rem(my_ka + 1, 2)
    middle = kas - 1 - my_ka
    place = lax.rem(my_ka, 2)
    barrier = pltpu.get_barrier_semaphore()
    overlaps = []
    for tile in range(tiles):
        for n in range(bands_own):
            low = max(tile * LANES, n * MODES)
            high = min((tile + 1) * LANES, (n + 1) * MODES)
            if low < high:
                overlaps.append((tile, n, low - tile * LANES, low - n * MODES, high - low))

    def fetch(index, slot):
        tile, chunk = index // chunks, lax.rem(index, chunks)
        return pltpu.make_async_copy(
            x_hbm.at[
                :, pl.ds(chunk * unit, unit), :, pl.ds(pl.multiple_of(tile * LANES, LANES), LANES)
            ],
            ring.at[slot],
            ring_sem.at[slot],
        )

    def project(real, imag, row):
        right = jnp.concatenate([real, imag], axis=0)
        product = jnp.dot(wq[...], right, preferred_element_type=jnp.float32)
        half[pl.ds(row, columns, stride=cells), :] = product

    def strip(index):
        return half[index * cells : (index + 1) * cells, :].astype(jnp.bfloat16)

    def contract(order):
        for q in range(q_total):
            right = jnp.concatenate([strip(q), strip(q_total + q)], axis=0)
            product = jnp.dot(wk[...], right, preferred_element_type=jnp.float32)
            for way in range(2):
                parts[order, way, q // q_local, q % q_local] = product[
                    way * rows : (way + 1) * rows
                ].astype(jnp.bfloat16)

    def put(source, target, send_sem, recv_sem, to_pb, to_ka):
        pltpu.make_async_remote_copy(
            src_ref=source, dst_ref=target, send_sem=send_sem, recv_sem=recv_sem,
            device_id={"pb": to_pb, "ka": to_ka}, device_id_type=MESH,
        ).start()

    def settle(window, sem):
        pltpu.make_async_copy(window, window, sem).wait()

    def chunk_of(index):
        return pl.ds(2 * lax.rem(my_pb // 2 + 1 + index, chips), 2)

    def send(order):
        @pl.when(outer)
        def _():
            def chunk(index, carry):
                span = chunk_of(index)
                put(parts.at[order, far, span], outer_in.at[order, span],
                    outer_send.at[order, index], outer_recv.at[order, index], my_pb, partner)
                return carry

            lax.fori_loop(0, chips, chunk, 0)

            def plane(index, carry):
                to = lax.rem(my_pb + index, bands)
                put(parts.at[order, side, to], from_plane.at[order, my_pb],
                    plane_send.at[order], plane_recv.at[order], to, my_ka)
                return carry

            lax.fori_loop(1, bands, plane, 0)

    def added(order, way, span, arrived):
        own = parts[order, way, span].astype(jnp.float32)
        parts[order, way, span] = (own + arrived.astype(jnp.float32)).astype(jnp.bfloat16)

    def pass_far(order):
        def chunk(index, carry):
            span = chunk_of(index)
            settle(outer_in.at[order, span], outer_recv.at[order, index])
            added(order, far, span, outer_in[order, span])
            put(parts.at[order, far, span], inner_in.at[order, span],
                inner_send.at[order, index], inner_recv.at[order, index], my_pb, middle)
            return carry

        lax.fori_loop(0, chips, chunk, 0)

    def pass_near(order):
        def chunk(index, carry):
            span = chunk_of(index)
            settle(inner_in.at[order, span], inner_recv.at[order, index])
            added(order, side, span, inner_in[order, span])
            for core in range(2):
                to = 2 * lax.rem(my_pb // 2 + 1 + index, chips) + core
                put(parts.at[order, side, to], from_line.at[order, my_pb],
                    line_send.at[order], line_recv.at[order], to, partner)
            return carry

        lax.fori_loop(0, chips, chunk, 0)

    inputs = (
        (vectors, vectors_all), (levels, levels_all), (filled, filled_all),
        (scalars_own, scalars_all),
    )

    edge_cells = edge_ref.shape[1]

    def edge(index, carry):
        for inner in range(unit):
            cell = index * unit + inner
            project(edge_ref[0, cell], edge_ref[1, cell], step * edge_cells + cell)
        return carry

    @pl.when(step == 0)
    def _():
        def greet(index, carry):
            peer = lax.rem(me + index, devices)
            pl.semaphore_signal(
                barrier, inc=1, device_id={"pb": peer // kas, "ka": lax.rem(peer, kas)},
                device_id_type=MESH,
            )
            return carry

        lax.fori_loop(1, devices, greet, 0)

        def first(index, carry):
            fetch(index, index).start()
            return carry

        lax.fori_loop(0, slots, first, 0)
        cos, sin = angles(qpoints[...], phonon_cells[...])
        wq[...] = jnp.concatenate(
            [jnp.concatenate([cos, -sin], 1), jnp.concatenate([sin, cos], 1)], 0
        ).astype(jnp.bfloat16)
        cells_all = electron_cells[...]
        own = cells_all[:, :cells]
        for ka in range(1, kas):
            own = jnp.where(my_ka == ka, cells_all[:, ka * cells : (ka + 1) * cells], own)
        cos, sin = angles(kpoints[...], own)
        blocks = []
        for way in range(2):
            c = cos[way * k_side : (way + 1) * k_side]
            s = sin[way * k_side : (way + 1) * k_side]
            blocks += [jnp.concatenate([c, -s], 1), jnp.concatenate([s, c], 1)]
        wk[...] = jnp.concatenate(blocks, 0).astype(jnp.bfloat16)
        for k in range(k_local):
            scalars_own[0, k : k + 1, :] = jnp.full((1, LANES), energy_k[k], jnp.float32)
            scalars_own[1, k : k + 1, :] = jnp.full((1, LANES), occupation_k[k], jnp.float32)

    lax.fori_loop(0, edge_cells // unit, edge, 0)

    @pl.when(step == 0)
    def _():
        for q in range(q_local):
            for part in range(2):
                mode = modes[q, part].astype(jnp.float32)
                for index, (tile, n, row, start, count) in enumerate(overlaps):
                    pieces = []
                    if row:
                        pieces.append(jnp.zeros((row, MODES), jnp.float32))
                    pieces.append(mode[start : start + count])
                    if row + count < LANES:
                        pieces.append(jnp.zeros((LANES - row - count, MODES), jnp.float32))
                    placed = jnp.concatenate(pieces, 0) if len(pieces) > 1 else pieces[0]
                    table[q, index, :, part * LANES : part * LANES + MODES] = placed.astype(
                        jnp.bfloat16
                    )

    def prepare(block, q):
        freq = omega[pl.ds(q, 1), :]
        boson = bose[pl.ds(q, 1), :]
        level_q = jnp.transpose(levels_all[block, q])
        filled_q = jnp.transpose(filled_all[block, q])
        for k in range(k_local):
            f = filled_q[:, k : k + 1]
            offset = scalars_all[block, 0, k : k + 1, :1] - level_q[:, k : k + 1]
            absorb = gaussian(offset + freq)
            emit = gaussian(offset - freq)
            spot = block * k_local + k
            emission[q, spot] = (boson + f) * absorb + (boson + 1.0 - f) * emit
            absorption[q, spot] = (scalars_all[block, 1, k : k + 1, :1] - f) * absorb
            for part in range(2):
                rows_ref[k, part, :, :bands_n] = vectors_all[block, q, k, part].astype(jnp.float32)
            real, imag = (
                jnp.concatenate(
                    [
                        rows_ref[k, part, pl.ds(n, bands, stride=bands_own), :]
                        for n in range(bands_own)
                    ],
                    axis=0,
                )[:, :bands_n]
                for part in range(2)
            )
            both = jnp.concatenate(
                [jnp.concatenate([real, -imag], 1), jnp.concatenate([imag, real], 1)], 0
            )
            turned[q, spot] = jnp.transpose(both).astype(jnp.bfloat16)

    def finish():
        for number, (_, target) in enumerate(inputs):
            settle(target.at[0], input_recv.at[number])
        for number, (source, target) in enumerate(inputs):
            pltpu.make_async_copy(source, target.at[place], input_sem.at[number]).wait()
        for block in range(2):
            for q in range(q_local):
                prepare(block, q)
        for order in range(tiles):
            from_plane[order, my_pb] = parts[order, side, my_pb]
        lane = lax.broadcasted_iota(jnp.int32, (1, LANES), 1)
        started = set()
        for order in range(tiles):
            tile = tiles - 1 if order == 0 else order - 1
            settle(from_plane.at[order, pl.ds(1, bands - 1)], plane_recv.at[order])
            settle(from_line.at[order], line_recv.at[order])
            for q in range(q_local):
                left = jnp.concatenate(
                    [
                        from_plane[order, band, q].astype(jnp.float32)
                        + from_line[order, band, q].astype(jnp.float32)
                        for band in range(bands)
                    ],
                    axis=0,
                )
                if pairs < (tile + 1) * LANES:
                    left = jnp.where(lane < pairs - tile * LANES, left, 0.0)
                left = left.astype(jnp.bfloat16)
                for index, (other, n, _, _, _) in enumerate(overlaps):
                    if other != tile:
                        continue
                    product = jnp.dot(left, table[q, index], preferred_element_type=jnp.float32)
                    for half_of in range(2):
                        value = product[:, half_of * LANES : (half_of + 1) * LANES]
                        if (q, n) in started:
                            value = value + lifted[q, n, half_of]
                        lifted[q, n, half_of] = value
                    started.add((q, n))
        electron = [None] * k_side
        for q in range(q_local):
            phonon = None
            for k in range(k_side):
                real, imag = [], []
                for n in range(bands_own):
                    rr, ri, ir, ii = (
                        lifted[q, n, half_of, pl.ds(part * k_side + k, bands, stride=rows), :]
                        for part in range(2)
                        for half_of in range(2)
                    )
                    real.append(rr - ii)
                    imag.append(ri + ir)
                right = jnp.concatenate(real + imag, axis=0).astype(jnp.bfloat16)
                band = jnp.dot(turned[q, k], right, preferred_element_type=jnp.float32)
                band_real = band[:bands_n, :MODES]
                band_imag = band[bands_n:, :MODES]
                weight = band_real * band_real + band_imag * band_imag
                e_term = weight * emission[q, k]
                p_term = weight * absorption[q, k]
                electron[k] = e_term if q == 0 else electron[k] + e_term
                phonon = p_term if k == 0 else phonon + p_term
            totals_p[q : q + 1, :] = jnp.sum(phonon, axis=0, keepdims=True)
        for k in range(k_side):
            totals_e[k // k_local, k % k_local : k % k_local + 1, :] = jnp.sum(
                electron[k], axis=0, keepdims=True
            )
        copies = []
        for shift in range(1, kas):
            copies.append(pltpu.make_async_remote_copy(
                totals_p, got_p.at[side], send_p.at[shift - 1], recv_p.at[side],
                device_id={"pb": my_pb, "ka": lax.rem(my_ka + shift, kas)}, device_id_type=MESH,
            ))
        for shift in range(bands):
            copies.append(pltpu.make_async_remote_copy(
                totals_e.at[1 - place], got_e.at[my_pb], send_e.at[0, shift], recv_e.at[my_pb],
                device_id={"pb": lax.rem(my_pb + shift, bands), "ka": partner},
                device_id_type=MESH,
            ))
        for shift in range(1, bands):
            copies.append(pltpu.make_async_remote_copy(
                totals_e.at[place], got_e.at[my_pb], send_e.at[1, shift], recv_e.at[my_pb],
                device_id={"pb": lax.rem(my_pb + shift, bands), "ka": my_ka}, device_id_type=MESH,
            ))
        for copy in copies:
            copy.start()
        got_e[my_pb] = totals_e[place]
        got_p[side] = totals_p[...]
        for order in range(tiles):
            settle(from_plane.at[order, pl.ds(1, bands - 1)], plane_send.at[order])
            for index in range(chips):
                settle(outer_in.at[order, pl.ds(0, 2)], outer_send.at[order, index])
        for copy in copies:
            copy.wait_send()
        settle(got_p.at[far], recv_p.at[far])

    def relay():
        pass_near(tiles - 2)
        pass_far(tiles - 1)
        pass_near(tiles - 1)
        for number, (source, _) in enumerate(inputs):
            settle(source, input_send.at[number])
        for order in range(tiles):
            settle(from_line.at[order], line_send.at[order])
            for index in range(chips):
                settle(inner_in.at[order, pl.ds(0, 2)], inner_send.at[order, index])
        for way in range(2):
            settle(got_p.at[way], recv_p.at[way])
        settle(got_e.at[my_pb], recv_e.at[my_pb])

    @pl.when(step == steps - 1)
    def _():
        pl.semaphore_wait(barrier, devices - 1)

        @pl.when(outer)
        def _():
            for number, (source, target) in enumerate(inputs):
                pltpu.make_async_copy(source, target.at[place], input_sem.at[number]).start()

        @pl.when(inner)
        def _():
            for number, (source, target) in enumerate(inputs):
                put(source, target.at[place], input_send.at[number], input_recv.at[number],
                    my_pb, partner)

        contract(0)
        send(0)

        def one_tile(tile, carry):
            def one_chunk(chunk, inner_carry):
                index = tile * chunks + chunk
                slot = lax.rem(index, slots)
                fetch(index, slot).wait()
                for inside in range(unit):
                    project(ring[slot, 0, inside], ring[slot, 1, inside], chunk * unit + inside)

                @pl.when(index + slots < (tiles - 1) * chunks)
                def _():
                    fetch(index + slots, slot).start()

                return inner_carry

            lax.fori_loop(0, chunks, one_chunk, 0)
            contract(tile + 1)
            send(tile + 1)

            @pl.when(inner)
            def _():
                pass_far(tile)

            @pl.when(inner & (tile >= 1))
            def _():
                pass_near(tile - 1)

            return carry

        lax.fori_loop(0, tiles - 1, one_tile, 0)
        pl.when(inner)(relay)
        pl.when(outer)(finish)
        total = None
        for shift in range(1, bands):
            other = lax.rem(my_pb + shift, bands)
            settle(got_e.at[other], recv_e.at[other])
        for other in range(bands):
            total = got_e[other] if other == 0 else total + got_e[other]
        out_ref[0] = total
        out_ref[1] = got_p[0] + got_p[1]


def everything(
    coupling, kpoints, qpoints, electron_cells, phonon_cells, phonon_modes, band_vectors,
    energies_kq, occupations_kq, energy_k, occupation_k, frequencies, bose_factors,
):
    bands, kas = lax.axis_size("pb"), lax.axis_size("ka")
    parts_count, cells, pairs, phonons = coupling.shape
    moved = jnp.transpose(coupling, (0, 1, 3, 2))
    tiles = -(-pairs // LANES)
    unit = cells // 4
    slots = 8
    q_local, k_local = band_vectors.shape[0], band_vectors.shape[1]
    bands_n = band_vectors.shape[3]
    columns = 2 * qpoints.shape[1]
    k_side = 2 * k_local
    rows = 2 * k_side
    chips = bands // 2
    bands_own = bands_n // bands
    overlaps = sum(
        max(t * LANES, n * MODES) < min((t + 1) * LANES, (n + 1) * MODES)
        for t in range(tiles)
        for n in range(bands_own)
    )
    small = pl.BlockSpec(memory_space=pltpu.VMEM)
    scalars = pl.BlockSpec(memory_space=pltpu.SMEM)
    dma = pltpu.SemaphoreType.DMA
    bf16, f32 = jnp.bfloat16, jnp.float32
    return pl.pallas_call(
        functools.partial(ring_kernel, pairs),
        grid=(2,),
        in_specs=[small] * 8
        + [scalars] * 2
        + [small] * 2
        + [
            pl.BlockSpec((parts_count, cells // 2, phonons, LANES), lambda e: (0, e, 0, tiles - 1)),
            pl.BlockSpec(memory_space=pl.ANY),
        ],
        out_specs=small,
        out_shape=jax.ShapeDtypeStruct((2, k_local, MODES), f32),
        scratch_shapes=[
            pltpu.VMEM((columns, 2 * phonons), bf16),
            pltpu.VMEM((2 * k_local * kas, 2 * cells), bf16),
            pltpu.VMEM((columns * cells, LANES), f32),
            pltpu.VMEM((slots, parts_count, unit, phonons, LANES), bf16),
            pltpu.VMEM((tiles, 2, bands, q_local, rows, LANES), bf16),
            pltpu.VMEM((tiles, bands, q_local, rows, LANES), bf16),
            pltpu.VMEM((tiles, bands, q_local, rows, LANES), bf16),
            pltpu.VMEM((tiles, bands, q_local, rows, LANES), bf16),
            pltpu.VMEM((tiles, bands, q_local, rows, LANES), bf16),
            pltpu.VMEM((q_local, overlaps, LANES, 2 * LANES), bf16),
            pltpu.VMEM((q_local, bands_own, 2, bands * rows, LANES), f32),
            pltpu.VMEM((k_local, 2, bands_n, LANES), f32),
            pltpu.VMEM((q_local, k_side, 2 * bands_n, 2 * bands_n), bf16),
            pltpu.VMEM((q_local, k_side, bands_n, MODES), f32),
            pltpu.VMEM((q_local, k_side, bands_n, MODES), f32),
            pltpu.VMEM((2, *band_vectors.shape), bf16),
            pltpu.VMEM((2, *energies_kq.shape), f32),
            pltpu.VMEM((2, *occupations_kq.shape), f32),
            pltpu.VMEM((2, k_local, LANES), f32),
            pltpu.VMEM((2, 2, k_local, LANES), f32),
            pltpu.VMEM((2, k_local, MODES), f32),
            pltpu.VMEM((q_local, MODES), f32),
            pltpu.VMEM((bands, k_local, MODES), f32),
            pltpu.VMEM((2, q_local, MODES), f32),
            dma((slots,)),
            dma((4,)),
            dma((4,)),
            dma((4,)),
            dma((tiles, chips)),
            dma((tiles, chips)),
            dma((tiles, chips)),
            dma((tiles, chips)),
            dma((tiles,)),
            dma((tiles,)),
            dma((tiles,)),
            dma((tiles,)),
            dma((2, bands)),
            dma((bands,)),
            dma((kas - 1,)),
            dma((2,)),
        ],
        compiler_params=pltpu.CompilerParams(
            collective_id=2,
            has_side_effects=True,
            dimension_semantics=("arbitrary",),
            vmem_limit_bytes=60 * 1024 * 1024,
        ),
        name="widths",
    )(
        kpoints, qpoints, electron_cells, phonon_cells, phonon_modes, band_vectors, energies_kq,
        occupations_kq, energy_k, occupation_k, frequencies, bose_factors, moved, moved,
    )


def on_device(
    coupling,
    kpoints,
    qpoints,
    electron_cells,
    phonon_cells,
    phonon_modes,
    band_vectors,
    energies_kq,
    occupations_kq,
    energy_k,
    occupation_k,
    frequencies,
    bose_factors,
):
    k_local = energy_k.shape[0]
    q_local = frequencies.shape[0]
    cells_local = coupling.shape[1]
    bands, kas = lax.axis_size("pb"), lax.axis_size("ka")
    q_total = q_local * bands
    k_total = k_local * kas
    whole_bands = coupling.shape[2] % MODES == 0 and coupling.shape[2] > LANES
    even = bands % 2 == 0 and cells_local % 16 == 0
    if kas == 4 and whole_bands and even and k_local == q_local:
        sums = everything(
            coupling, kpoints, qpoints, electron_cells, phonon_cells, phonon_modes, band_vectors,
            energies_kq, occupations_kq, energy_k, occupation_k, frequencies, bose_factors,
        )
        return (sums[0] / (q_total * NB), sums[1] / (k_total * NB))
    cos_q, sin_q = phase_table(qpoints, phonon_cells)
    own_cells = lax.dynamic_slice_in_dim(
        electron_cells, lax.axis_index("ka") * cells_local, cells_local, 1
    )
    cos_k, sin_k = phase_table(kpoints, own_cells)
    wq = jnp.concatenate(
        [jnp.concatenate([cos_q, -sin_q], 1), jnp.concatenate([sin_q, cos_q], 1)], 0
    )
    wk = jnp.stack(
        [jnp.concatenate([cos_k, -sin_k], 1), jnp.concatenate([sin_k, cos_k], 1)], 1
    ).reshape(2 * k_total, 2 * cells_local)
    values = bloch(coupling, wq, wk, q_local, k_local)
    values = values.reshape(bands, q_local // 2, 2, k_local, 2, -1)
    values = jnp.transpose(values, (4, 3, 1, 2, 0, 5)).reshape(2, k_local, q_local, NB, MODES)
    electron, phonon = widths(
        values[0],
        values[1],
        phonon_modes,
        band_vectors,
        energies_kq,
        occupations_kq,
        energy_k,
        occupation_k,
        frequencies,
        bose_factors,
    )
    electron_width, phonon_width = exchange(electron / (q_total * NB), phonon / (k_total * NB))
    return (electron_width, phonon_width)


def solution(mesh):
    in_specs = (
        P(None, "ka", "pb", None),
        P(),
        P(),
        P(),
        P(),
        P("pb", None, None, None),
        P("pb", "ka", None, None, None),
        P("pb", "ka", None),
        P("pb", "ka", None),
        P("ka"),
        P("ka"),
        P("pb", None),
        P("pb", None),
    )
    out_specs = (P("ka", None), P("pb", None))
    return jax.shard_map(
        on_device, mesh=mesh, in_specs=in_specs, out_specs=out_specs, check_vma=False
    )
```

```python
import functools
import math

import jax
import jax.numpy as jnp
from jax import lax
from jax.experimental import pallas as pl
from jax.experimental.pallas import tpu as pltpu
from jax.sharding import PartitionSpec as P

NB = 40
MODES = 120
NG = 100


smearing = 0.05


def phase_table(points, cells):
    product = (
        points[0][:, None] * cells[0][None, :]
        + points[1][:, None] * cells[1][None, :]
        + points[2][:, None] * cells[2][None, :]
    )
    angle = jnp.mod(product, NG).astype(jnp.float32) * (2.0 * math.pi / NG)
    return (jnp.cos(angle).astype(jnp.bfloat16), jnp.sin(angle).astype(jnp.bfloat16))


def gaussian(offset):
    return jnp.exp(-0.5 * (offset / smearing) ** 2) / (smearing * math.sqrt(2.0 * math.pi))


def contract_last(left, right):
    return lax.dot_general(
        left, right, (((1,), (1,)), ((), ())), preferred_element_type=jnp.float32
    )


def mixed(form, left, right):
    return jnp.einsum(form, left, right, preferred_element_type=jnp.float32)


def widths(
    bloch_real, bloch_imag, modes, vectors, levels, filled, energy_k, occupation_k, omega, bose
):
    mode_real = modes[:, 0]
    mode_imag = modes[:, 1]
    moded_real = (
        mixed("kqnm,qmv->kqnv", bloch_real, mode_real)
        - mixed("kqnm,qmv->kqnv", bloch_imag, mode_imag)
    ).astype(jnp.bfloat16)
    moded_imag = (
        mixed("kqnm,qmv->kqnv", bloch_real, mode_imag)
        + mixed("kqnm,qmv->kqnv", bloch_imag, mode_real)
    ).astype(jnp.bfloat16)
    vector_real = vectors[:, :, 0]
    vector_imag = vectors[:, :, 1]
    band_real = mixed("qknb,kqnv->kqbv", vector_real, moded_real) + mixed(
        "qknb,kqnv->kqbv", vector_imag, moded_imag
    )
    band_imag = mixed("qknb,kqnv->kqbv", vector_real, moded_imag) - mixed(
        "qknb,kqnv->kqbv", vector_imag, moded_real
    )
    weight = band_real * band_real + band_imag * band_imag
    level_kq = jnp.transpose(levels, (1, 0, 2))[..., None]
    filled_kq = jnp.transpose(filled, (1, 0, 2))[..., None]
    offset = energy_k[:, None, None, None] - level_kq
    freq = omega[None, :, None, :]
    boson = bose[None, :, None, :]
    absorb = gaussian(offset + freq)
    emit = gaussian(offset - freq)
    electron = jnp.sum(
        weight * ((boson + filled_kq) * absorb + (boson + 1.0 - filled_kq) * emit), axis=(1, 2)
    )
    phonon = jnp.sum(weight * (occupation_k[:, None, None, None] - filled_kq) * absorb, axis=(0, 2))
    return (electron, phonon)


MESH = pl.DeviceIdType.MESH
LANES = 128


def bloch_kernel(
    cells_block, tile, last, wq_ref, wk_ref, x_ref, out_ref,
    half, parts, recv, send_sem, recv_sem,
):
    pairs_step = pl.program_id(0)
    cell_step = pl.program_id(1)
    tiles = pl.num_programs(0)
    cell_steps = pl.num_programs(1)
    bands, kas = lax.axis_size("pb"), lax.axis_size("ka")
    devices = bands * kas
    me = lax.axis_index("pb") * kas + lax.axis_index("ka")
    columns = wq_ref.shape[0]
    cells = half.shape[1] // columns
    groups = parts.shape[2]
    mine = groups // bands
    rows = parts.shape[3] // 2
    barrier = pltpu.get_barrier_semaphore()

    @pl.when((pairs_step == 0) & (cell_step == 0))
    def _():
        def greet(step, carry):
            peer = lax.rem(me + step, devices)
            pl.semaphore_signal(
                barrier, inc=1, device_id={"pb": peer // kas, "ka": lax.rem(peer, kas)},
                device_id_type=MESH,
            )
            return carry

        lax.fori_loop(1, devices, greet, 0)

    for cell in range(cells_block):
        right = jnp.concatenate([x_ref[0, cell], x_ref[1, cell]], axis=0)
        product = jnp.dot(wq_ref[...], right, preferred_element_type=jnp.float32)
        row = cell_step * cells_block + cell
        for lane in range(tile // LANES):
            half[lane, pl.ds(row, columns, stride=cells), :] = product[
                :, lane * LANES : (lane + 1) * LANES
            ]

    def strip(index):
        start = pl.multiple_of(index * cells, cells)
        return jnp.concatenate(
            [half[lane, pl.ds(start, cells), :] for lane in range(tile // LANES)], axis=1
        ).astype(jnp.bfloat16)

    @pl.when(cell_step == cell_steps - 1)
    def _():
        def contract(group, carry):
            sums = []
            for member in range(2):
                q = group * 2 + member
                right = jnp.concatenate([strip(q), strip(columns // 2 + q)], axis=0)
                sums.append(
                    jnp.dot(wk_ref[...], right, preferred_element_type=jnp.float32)
                )
            for ka in range(kas):
                block = slice(ka * rows, (ka + 1) * rows)
                parts[pairs_step, ka, group] = jnp.concatenate(
                    [sums[0][block], sums[1][block]], axis=0
                ).astype(jnp.bfloat16)
            return carry

        lax.fori_loop(0, groups, contract, 0, unroll=4)

    @pl.when((cell_step == cell_steps - 1) & (pairs_step == 0))
    def _():
        pl.semaphore_wait(barrier, devices - 1)

    def send(index, width):
        def one(step, carry):
            peer = lax.rem(me + step, devices)
            to_pb, to_ka = peer // kas, lax.rem(peer, kas)
            pltpu.make_async_remote_copy(
                src_ref=parts.at[index, to_ka, pl.ds(to_pb * mine, mine), :, pl.ds(0, width)],
                dst_ref=recv.at[index, me, :, :, pl.ds(0, width)],
                send_sem=send_sem.at[index],
                recv_sem=recv_sem.at[index],
                device_id={"pb": to_pb, "ka": to_ka},
                device_id_type=MESH,
            ).start()
            return carry

        lax.fori_loop(1, devices, one, 0)

    @pl.when((cell_step == cell_steps - 1) & (pairs_step < tiles - 1))
    def _():
        send(pairs_step, tile)

    @pl.when((cell_step == cell_steps - 1) & (pairs_step == tiles - 1))
    def _():
        count = recv.shape[0]
        send(count - 1, last)
        my_pb, my_ka = lax.axis_index("pb"), lax.axis_index("ka")
        for index in range(count):
            recv[index, me] = parts[index, my_ka, pl.ds(my_pb * mine, mine)]
        for index in range(count):
            width = tile if index < count - 1 else last
            window = recv.at[index, pl.ds(1, devices - 1), :, :, pl.ds(0, width)]
            pltpu.make_async_copy(window, window, send_sem.at[index]).wait()
            pltpu.make_async_copy(window, window, recv_sem.at[index]).wait()
            for band in range(bands):
                total = recv[index, band * kas, :, :, :width].astype(jnp.float32)
                for ka in range(1, kas):
                    total = total + recv[index, band * kas + ka, :, :, :width].astype(jnp.float32)
                out_ref[band, :, :, index * tile : index * tile + width] = total.astype(
                    jnp.bfloat16
                )


def bloch(coupling, wq, wk, q_local, k_local):
    bands, kas = lax.axis_size("pb"), lax.axis_size("ka")
    devices = bands * kas
    parts_count, cells, pairs, phonons = coupling.shape
    moved = jnp.transpose(coupling, (0, 1, 3, 2))
    padded = -(-pairs // LANES) * LANES
    if pairs < LANES:
        moved = jnp.pad(moved, ((0, 0), (0, 0), (0, 0), (0, LANES - pairs)))
    tile = min(2 * LANES, padded)
    tiles = -(-padded // tile)
    last = padded - (tiles - 1) * tile
    cells_block = 16
    columns = wq.shape[0]
    groups = columns // 4
    mine = q_local // 2
    rows = 4 * k_local
    result = pl.pallas_call(
        functools.partial(bloch_kernel, cells_block, tile, last),
        grid=(tiles, cells // cells_block),
        in_specs=[
            pl.BlockSpec(wq.shape, lambda t, e: (0, 0)),
            pl.BlockSpec(wk.shape, lambda t, e: (0, 0)),
            pl.BlockSpec((parts_count, cells_block, phonons, tile), lambda t, e: (0, e, 0, t)),
        ],
        out_specs=pl.BlockSpec((bands, mine, rows, padded), lambda t, e: (0, 0, 0, 0)),
        out_shape=jax.ShapeDtypeStruct((bands, mine, rows, padded), jnp.bfloat16),
        scratch_shapes=[
            pltpu.VMEM((tile // LANES, columns * cells, LANES), jnp.float32),
            pltpu.VMEM((tiles, kas, groups, rows, tile), jnp.bfloat16),
            pltpu.VMEM((tiles, devices, mine, rows, tile), jnp.bfloat16),
            pltpu.SemaphoreType.DMA((tiles,)),
            pltpu.SemaphoreType.DMA((tiles,)),
        ],
        compiler_params=pltpu.CompilerParams(
            collective_id=0,
            has_side_effects=True,
            dimension_semantics=("arbitrary", "arbitrary"),
            vmem_limit_bytes=60 * 1024 * 1024,
        ),
        name="bloch",
    )(wq, wk, moved)
    return result[..., :pairs]


def sums_kernel(electron_ref, phonon_ref, electron_out, phonon_out, got_e, got_p, send, recv_e, recv_p):
    bands, kas = lax.axis_size("pb"), lax.axis_size("ka")
    my_pb, my_ka = lax.axis_index("pb"), lax.axis_index("ka")
    barrier = pltpu.get_barrier_semaphore()
    for step in range(1, bands):
        pl.semaphore_signal(
            barrier, inc=1, device_id={"pb": lax.rem(my_pb + step, bands), "ka": my_ka},
            device_id_type=MESH,
        )
    for step in range(1, kas):
        pl.semaphore_signal(
            barrier, inc=1, device_id={"pb": my_pb, "ka": lax.rem(my_ka + step, kas)},
            device_id_type=MESH,
        )
    pl.semaphore_wait(barrier, bands + kas - 2)
    copies = []
    for step in range(1, bands):
        copies.append(pltpu.make_async_remote_copy(
            electron_ref, got_e.at[my_pb], send.at[step - 1], recv_e.at[step - 1],
            device_id={"pb": lax.rem(my_pb + step, bands), "ka": my_ka}, device_id_type=MESH,
        ))
    for step in range(1, kas):
        copies.append(pltpu.make_async_remote_copy(
            phonon_ref, got_p.at[my_ka], send.at[bands + step - 2], recv_p.at[step - 1],
            device_id={"pb": my_pb, "ka": lax.rem(my_ka + step, kas)}, device_id_type=MESH,
        ))
    for copy in copies:
        copy.start()
    got_e[my_pb] = electron_ref[...]
    got_p[my_ka] = phonon_ref[...]
    for copy in copies:
        copy.wait()
    total = got_e[0]
    for step in range(1, bands):
        total = total + got_e[step]
    electron_out[...] = total
    total = got_p[0]
    for step in range(1, kas):
        total = total + got_p[step]
    phonon_out[...] = total


def exchange(electron, phonon):
    bands, kas = lax.axis_size("pb"), lax.axis_size("ka")
    whole = pl.BlockSpec(memory_space=pltpu.VMEM)
    return pl.pallas_call(
        sums_kernel,
        in_specs=[whole, whole],
        out_specs=[whole, whole],
        out_shape=[
            jax.ShapeDtypeStruct(electron.shape, electron.dtype),
            jax.ShapeDtypeStruct(phonon.shape, phonon.dtype),
        ],
        scratch_shapes=[
            pltpu.VMEM((bands, *electron.shape), jnp.float32),
            pltpu.VMEM((kas, *phonon.shape), jnp.float32),
            pltpu.SemaphoreType.DMA((bands + kas - 2,)),
            pltpu.SemaphoreType.DMA((bands - 1,)),
            pltpu.SemaphoreType.DMA((kas - 1,)),
        ],
        compiler_params=pltpu.CompilerParams(collective_id=1, has_side_effects=True),
        name="sums",
    )(electron, phonon)


def angles(points, cells):
    product = lax.dot_general(
        points.astype(jnp.float32).astype(jnp.bfloat16),
        cells.astype(jnp.float32).astype(jnp.bfloat16),
        (((0,), (0,)), ((), ())),
        preferred_element_type=jnp.float32,
    )
    turns = jnp.floor((product + 0.5) * (1.0 / NG))
    angle = (product - turns * NG) * (2.0 * math.pi / NG)
    return jnp.cos(angle), jnp.sin(angle)


def ring_kernel(
    pairs, kpoints, qpoints, electron_cells, phonon_cells, modes, vectors,
    levels, filled, energy_k, occupation_k, omega, bose, edge_ref, x_hbm, out_ref,
    wq, wk, half, ring, parts, recv, relay, sums, table, lifted, rows_ref, turned,
    emission, absorption, totals, got_e, got_p,
    ring_sem, relay_send, relay_recv, plane_send, plane_recv, raw_send, raw_recv,
    sum_send, sum_recv, send_e, recv_e, send_p, recv_p,
):
    step = pl.program_id(0)
    steps = pl.num_programs(0)
    bands, kas = lax.axis_size("pb"), lax.axis_size("ka")
    devices = bands * kas
    my_pb, my_ka = lax.axis_index("pb"), lax.axis_index("ka")
    me = my_pb * kas + my_ka
    columns = wq.shape[0]
    q_total = columns // 2
    pitch = half.shape[0] // columns
    cells = wk.shape[1] // 2
    slots, unit = ring.shape[0], ring.shape[2]
    chunks = cells // unit
    tiles = parts.shape[0]
    halves = parts.shape[3]
    mine = 2 * halves
    q_local, k_local = vectors.shape[0], vectors.shape[1]
    rows = 2 * k_local
    bands_n = vectors.shape[3]
    bands_own = bands_n // bands
    up, down = lax.rem(my_ka + 1, kas), lax.rem(my_ka + kas - 1, kas)
    across = lax.rem(my_ka + 2, kas)
    barrier = pltpu.get_barrier_semaphore()
    overlaps = []
    for tile in range(tiles):
        for n in range(bands_own):
            low = max(tile * LANES, n * MODES)
            high = min((tile + 1) * LANES, (n + 1) * MODES)
            if low < high:
                overlaps.append((tile, n, low - tile * LANES, low - n * MODES, high - low))

    def fetch(index, slot):
        tile, chunk = index // chunks, lax.rem(index, chunks)
        return pltpu.make_async_copy(
            x_hbm.at[
                :, pl.ds(chunk * unit, unit), :, pl.ds(pl.multiple_of(tile * LANES, LANES), LANES)
            ],
            ring.at[slot],
            ring_sem.at[slot],
        )

    def project(real, imag, row):
        right = jnp.concatenate([real, imag], axis=0)
        product = jnp.dot(wq[...], right, preferred_element_type=jnp.float32)
        half[pl.ds(row, columns, stride=pitch), :] = product

    def strip(index):
        return half[index * pitch : index * pitch + cells, :].astype(jnp.bfloat16)

    def contract(order):
        for group in range(q_total // 2):
            products = []
            for member in range(2):
                q = group * 2 + member
                right = jnp.concatenate([strip(q), strip(q_total + q)], axis=0)
                products.append(jnp.dot(wk[...], right, preferred_element_type=jnp.float32))
            m = group % mine
            for ka in range(kas):
                block = slice(ka * rows, (ka + 1) * rows)
                parts[order, ka, m // halves, m % halves, group // mine] = jnp.concatenate(
                    [products[0][block], products[1][block]], axis=0
                ).astype(jnp.bfloat16)

    def put(source, target, send_sem, recv_sem, to_pb, to_ka):
        pltpu.make_async_remote_copy(
            src_ref=source, dst_ref=target, send_sem=send_sem, recv_sem=recv_sem,
            device_id={"pb": to_pb, "ka": to_ka}, device_id_type=MESH,
        ).start()

    def settle(window, sem):
        pltpu.make_async_copy(window, window, sem).wait()

    def send(order):
        put(parts.at[order, across, 0], relay.at[order, 0], relay_send.at[0, order],
            relay_recv.at[0, order], my_pb, up)
        put(parts.at[order, across, 1], relay.at[order, 1], relay_send.at[1, order],
            relay_recv.at[1, order], my_pb, down)

        def raw(index, carry):
            to = lax.rem(my_pb + index, bands)
            put(parts.at[order, up, 1, :, to], recv.at[order, 1, 1, :, my_pb],
                raw_send.at[0, order], raw_recv.at[0, order], to, up)
            put(parts.at[order, down, 0, :, to], recv.at[order, 2, 0, :, my_pb],
                raw_send.at[1, order], raw_recv.at[1, order], to, down)
            return carry

        lax.fori_loop(0, bands, raw, 0)

        def plane(index, carry):
            to = lax.rem(my_pb + index, bands)
            put(parts.at[order, my_ka, :, :, to], recv.at[order, 0, :, :, my_pb],
                plane_send.at[order], plane_recv.at[order], to, my_ka)
            return carry

        lax.fori_loop(1, bands, plane, 0)

    def pass_on(order):
        for way, (target, place) in enumerate(((up, 1), (down, 2))):
            settle(relay.at[order, way], relay_recv.at[way, order])
            own = parts[order, target, way].astype(jnp.float32)
            sums[order, way] = (own + relay[order, way].astype(jnp.float32)).astype(jnp.bfloat16)

            def one(index, carry, way=way, target=target, place=place):
                to = lax.rem(my_pb + index, bands)
                put(sums.at[order, way, :, to], recv.at[order, place, way, :, my_pb],
                    sum_send.at[way, order], sum_recv.at[way, order], to, target)
                return carry

            lax.fori_loop(0, bands, one, 0)

    edge_cells = edge_ref.shape[1]

    def edge(index, carry):
        for inner in range(unit):
            cell = index * unit + inner
            project(edge_ref[0, cell], edge_ref[1, cell], step * edge_cells + cell)
        return carry

    @pl.when(step == 0)
    def _():
        def greet(index, carry):
            peer = lax.rem(me + index, devices)
            pl.semaphore_signal(
                barrier, inc=1, device_id={"pb": peer // kas, "ka": lax.rem(peer, kas)},
                device_id_type=MESH,
            )
            return carry

        lax.fori_loop(1, devices, greet, 0)

        def first(index, carry):
            fetch(index, index).start()
            return carry

        lax.fori_loop(0, slots, first, 0)
        cos, sin = angles(qpoints[...], phonon_cells[...])
        wq[...] = jnp.concatenate(
            [jnp.concatenate([cos, -sin], 1), jnp.concatenate([sin, cos], 1)], 0
        ).astype(jnp.bfloat16)
        cells_all = electron_cells[...]
        own = cells_all[:, :cells]
        for ka in range(1, kas):
            own = jnp.where(my_ka == ka, cells_all[:, ka * cells : (ka + 1) * cells], own)
        cos, sin = angles(kpoints[...], own)
        blocks = []
        for ka in range(kas):
            c = cos[ka * k_local : (ka + 1) * k_local]
            s = sin[ka * k_local : (ka + 1) * k_local]
            blocks += [jnp.concatenate([c, -s], 1), jnp.concatenate([s, c], 1)]
        wk[...] = jnp.concatenate(blocks, 0).astype(jnp.bfloat16)

    lax.fori_loop(0, edge_cells // unit, edge, 0)

    @pl.when(step == 0)
    def _():
        for q in range(q_local):
            freq = omega[q : q + 1, :]
            boson = bose[q : q + 1, :]
            level_q = jnp.transpose(levels[q])
            filled_q = jnp.transpose(filled[q])
            for k in range(k_local):
                f = filled_q[:, k : k + 1]
                offset = energy_k[k] - level_q[:, k : k + 1]
                absorb = gaussian(offset + freq)
                emit = gaussian(offset - freq)
                emission[q, k] = (boson + f) * absorb + (boson + 1.0 - f) * emit
                absorption[q, k] = (occupation_k[k] - f) * absorb
                for part in range(2):
                    rows_ref[part, :, :bands_n] = vectors[q, k, part].astype(jnp.float32)
                real, imag = (
                    jnp.concatenate(
                        [
                            rows_ref[part, pl.ds(n, bands, stride=bands_own), :]
                            for n in range(bands_own)
                        ],
                        axis=0,
                    )[:, :bands_n]
                    for part in range(2)
                )
                both = jnp.concatenate(
                    [jnp.concatenate([real, -imag], 1), jnp.concatenate([imag, real], 1)], 0
                )
                turned[q, k] = jnp.transpose(both).astype(jnp.bfloat16)
            for part in range(2):
                mode = modes[q, part].astype(jnp.float32)
                for index, (tile, n, row, start, count) in enumerate(overlaps):
                    pieces = []
                    if row:
                        pieces.append(jnp.zeros((row, MODES), jnp.float32))
                    pieces.append(mode[start : start + count])
                    if row + count < LANES:
                        pieces.append(jnp.zeros((LANES - row - count, MODES), jnp.float32))
                    placed = jnp.concatenate(pieces, 0) if len(pieces) > 1 else pieces[0]
                    table[q, index, :, part * LANES : part * LANES + MODES] = placed.astype(
                        jnp.bfloat16
                    )

    @pl.when(step == steps - 1)
    def _():
        contract(0)
        pl.semaphore_wait(barrier, devices - 1)
        send(0)

        def one_tile(tile, carry):
            def one_chunk(chunk, inner_carry):
                index = tile * chunks + chunk
                slot = lax.rem(index, slots)
                fetch(index, slot).wait()
                for inner in range(unit):
                    project(ring[slot, 0, inner], ring[slot, 1, inner], chunk * unit + inner)

                @pl.when(index + slots < (tiles - 1) * chunks)
                def _():
                    fetch(index + slots, slot).start()

                return inner_carry

            lax.fori_loop(0, chunks, one_chunk, 0)
            contract(tile + 1)
            send(tile + 1)

            @pl.when(tile >= 1)
            def _():
                pass_on(tile - 1)

            return carry

        lax.fori_loop(0, tiles - 1, one_tile, 0)
        for order in range(tiles):
            recv[order, 0, :, :, my_pb] = parts[order, my_ka, :, :, my_pb]
        pass_on(tiles - 2)
        pass_on(tiles - 1)
        lane = lax.broadcasted_iota(jnp.int32, (1, LANES), 1)
        started = set()
        for order in range(tiles):
            tile = tiles - 1 if order == 0 else order - 1
            settle(recv.at[order, 0, :, :, pl.ds(1, bands - 1)], plane_recv.at[order])
            for way in range(2):
                settle(recv.at[order, 1 + way, 1 - way], raw_recv.at[way, order])
            for way in range(2):
                settle(recv.at[order, 1 + way, way], sum_recv.at[way, order])
            for m in range(mine):
                spot = (m // halves, m % halves)
                total = [
                    recv[order, 0, *spot, band].astype(jnp.float32)
                    + recv[order, 1, *spot, band].astype(jnp.float32)
                    + recv[order, 2, *spot, band].astype(jnp.float32)
                    for band in range(bands)
                ]
                for member in range(2):
                    q = 2 * m + member
                    left = jnp.concatenate(
                        [one[member * rows : (member + 1) * rows] for one in total], axis=0
                    )
                    if pairs < (tile + 1) * LANES:
                        left = jnp.where(lane < pairs - tile * LANES, left, 0.0)
                    left = left.astype(jnp.bfloat16)
                    for index, (other, n, _, _, _) in enumerate(overlaps):
                        if other != tile:
                            continue
                        product = jnp.dot(
                            left, table[q, index], preferred_element_type=jnp.float32
                        )
                        for side in range(2):
                            value = product[:, side * LANES : (side + 1) * LANES]
                            if (q, n) in started:
                                value = value + lifted[q, n, side]
                            lifted[q, n, side] = value
                        started.add((q, n))
        electron = [None] * k_local
        for q in range(q_local):
            phonon = None
            for k in range(k_local):
                real, imag = [], []
                for n in range(bands_own):
                    rr, ri, ir, ii = (
                        lifted[q, n, side, pl.ds(part * k_local + k, bands, stride=rows), :]
                        for part in range(2)
                        for side in range(2)
                    )
                    real.append(rr - ii)
                    imag.append(ri + ir)
                right = jnp.concatenate(real + imag, axis=0).astype(jnp.bfloat16)
                band = jnp.dot(turned[q, k], right, preferred_element_type=jnp.float32)
                band_real = band[:bands_n, :MODES]
                band_imag = band[bands_n:, :MODES]
                weight = band_real * band_real + band_imag * band_imag
                e_term = weight * emission[q, k]
                p_term = weight * absorption[q, k]
                electron[k] = e_term if q == 0 else electron[k] + e_term
                phonon = p_term if k == 0 else phonon + p_term
            totals[1, q : q + 1, :] = jnp.sum(phonon, axis=0, keepdims=True)
        for k in range(k_local):
            totals[0, k : k + 1, :] = jnp.sum(electron[k], axis=0, keepdims=True)
        copies = []
        for shift in range(1, bands):
            copies.append(pltpu.make_async_remote_copy(
                totals.at[0], got_e.at[my_pb], send_e.at[shift - 1], recv_e.at[shift - 1],
                device_id={"pb": lax.rem(my_pb + shift, bands), "ka": my_ka}, device_id_type=MESH,
            ))
        for shift in range(1, kas):
            copies.append(pltpu.make_async_remote_copy(
                totals.at[1], got_p.at[my_ka], send_p.at[shift - 1], recv_p.at[shift - 1],
                device_id={"pb": my_pb, "ka": lax.rem(my_ka + shift, kas)}, device_id_type=MESH,
            ))
        for copy in copies:
            copy.start()
        got_e[my_pb] = totals[0]
        got_p[my_ka] = totals[1]
        for order in range(tiles):
            settle(recv.at[order, 0, :, :, pl.ds(1, bands - 1)], plane_send.at[order])
            for way in range(2):
                settle(relay.at[order, way], relay_send.at[way, order])
                settle(recv.at[order, 1 + way, 1 - way], raw_send.at[way, order])
                settle(recv.at[order, 1 + way, way], sum_send.at[way, order])
        for copy in copies:
            copy.wait()
        total = got_e[0]
        for other in range(1, bands):
            total = total + got_e[other]
        out_ref[0] = total
        total = got_p[0]
        for other in range(1, kas):
            total = total + got_p[other]
        out_ref[1] = total


def everything(
    coupling, kpoints, qpoints, electron_cells, phonon_cells, phonon_modes, band_vectors,
    energies_kq, occupations_kq, energy_k, occupation_k, frequencies, bose_factors,
):
    bands, kas = lax.axis_size("pb"), lax.axis_size("ka")
    parts_count, cells, pairs, phonons = coupling.shape
    moved = jnp.transpose(coupling, (0, 1, 3, 2))
    tiles = -(-pairs // LANES)
    unit = cells // 4
    pitch = 8 * (-(-cells // 8) | 1)
    slots = 8
    q_local, k_local = band_vectors.shape[0], band_vectors.shape[1]
    bands_n = band_vectors.shape[3]
    columns = 2 * qpoints.shape[1]
    halves = q_local // 4
    rows = 4 * k_local
    bands_own = bands_n // bands
    overlaps = sum(
        max(t * LANES, n * MODES) < min((t + 1) * LANES, (n + 1) * MODES)
        for t in range(tiles)
        for n in range(bands_own)
    )
    small = pl.BlockSpec(memory_space=pltpu.VMEM)
    scalars = pl.BlockSpec(memory_space=pltpu.SMEM)
    dma = pltpu.SemaphoreType.DMA
    bf16, f32 = jnp.bfloat16, jnp.float32
    return pl.pallas_call(
        functools.partial(ring_kernel, pairs),
        grid=(2,),
        in_specs=[small] * 8
        + [scalars] * 2
        + [small] * 2
        + [
            pl.BlockSpec((parts_count, cells // 2, phonons, LANES), lambda e: (0, e, 0, tiles - 1)),
            pl.BlockSpec(memory_space=pl.ANY),
        ],
        out_specs=small,
        out_shape=jax.ShapeDtypeStruct((2, k_local, MODES), f32),
        scratch_shapes=[
            pltpu.VMEM((columns, 2 * phonons), bf16),
            pltpu.VMEM((2 * k_local * kas, 2 * cells), bf16),
            pltpu.VMEM((columns * pitch, LANES), f32),
            pltpu.VMEM((slots, parts_count, unit, phonons, LANES), bf16),
            pltpu.VMEM((tiles, kas, 2, halves, bands, rows, LANES), bf16),
            pltpu.VMEM((tiles, 3, 2, halves, bands, rows, LANES), bf16),
            pltpu.VMEM((tiles, 2, halves, bands, rows, LANES), bf16),
            pltpu.VMEM((tiles, 2, halves, bands, rows, LANES), bf16),
            pltpu.VMEM((q_local, overlaps, LANES, 2 * LANES), bf16),
            pltpu.VMEM((q_local, bands_own, 2, bands * 2 * k_local, LANES), f32),
            pltpu.VMEM((2, bands_n, LANES), f32),
            pltpu.VMEM((q_local, k_local, 2 * bands_n, 2 * bands_n), bf16),
            pltpu.VMEM((q_local, k_local, bands_n, MODES), f32),
            pltpu.VMEM((q_local, k_local, bands_n, MODES), f32),
            pltpu.VMEM((2, k_local, MODES), f32),
            pltpu.VMEM((bands, k_local, MODES), f32),
            pltpu.VMEM((kas, k_local, MODES), f32),
            dma((slots,)),
            dma((2, tiles)),
            dma((2, tiles)),
            dma((tiles,)),
            dma((tiles,)),
            dma((2, tiles)),
            dma((2, tiles)),
            dma((2, tiles)),
            dma((2, tiles)),
            dma((bands - 1,)),
            dma((bands - 1,)),
            dma((kas - 1,)),
            dma((kas - 1,)),
        ],
        compiler_params=pltpu.CompilerParams(
            collective_id=2,
            has_side_effects=True,
            dimension_semantics=("arbitrary",),
            vmem_limit_bytes=60 * 1024 * 1024,
        ),
        name="widths",
    )(
        kpoints, qpoints, electron_cells, phonon_cells, phonon_modes, band_vectors, energies_kq,
        occupations_kq, energy_k, occupation_k, frequencies, bose_factors, moved, moved,
    )


def on_device(
    coupling,
    kpoints,
    qpoints,
    electron_cells,
    phonon_cells,
    phonon_modes,
    band_vectors,
    energies_kq,
    occupations_kq,
    energy_k,
    occupation_k,
    frequencies,
    bose_factors,
):
    k_local = energy_k.shape[0]
    q_local = frequencies.shape[0]
    cells_local = coupling.shape[1]
    bands, kas = lax.axis_size("pb"), lax.axis_size("ka")
    q_total = q_local * bands
    k_total = k_local * kas
    whole_bands = coupling.shape[2] % MODES == 0 and coupling.shape[2] > LANES
    even = q_local % 4 == 0 and cells_local % 16 == 0
    if kas == 4 and whole_bands and even and k_local == q_local:
        sums = everything(
            coupling, kpoints, qpoints, electron_cells, phonon_cells, phonon_modes, band_vectors,
            energies_kq, occupations_kq, energy_k, occupation_k, frequencies, bose_factors,
        )
        return (sums[0] / (q_total * NB), sums[1] / (k_total * NB))
    cos_q, sin_q = phase_table(qpoints, phonon_cells)
    own_cells = lax.dynamic_slice_in_dim(
        electron_cells, lax.axis_index("ka") * cells_local, cells_local, 1
    )
    cos_k, sin_k = phase_table(kpoints, own_cells)
    wq = jnp.concatenate(
        [jnp.concatenate([cos_q, -sin_q], 1), jnp.concatenate([sin_q, cos_q], 1)], 0
    )
    wk = jnp.stack(
        [jnp.concatenate([cos_k, -sin_k], 1), jnp.concatenate([sin_k, cos_k], 1)], 1
    ).reshape(2 * k_total, 2 * cells_local)
    values = bloch(coupling, wq, wk, q_local, k_local)
    values = values.reshape(bands, q_local // 2, 2, k_local, 2, -1)
    values = jnp.transpose(values, (4, 3, 1, 2, 0, 5)).reshape(2, k_local, q_local, NB, MODES)
    electron, phonon = widths(
        values[0],
        values[1],
        phonon_modes,
        band_vectors,
        energies_kq,
        occupations_kq,
        energy_k,
        occupation_k,
        frequencies,
        bose_factors,
    )
    electron_width, phonon_width = exchange(electron / (q_total * NB), phonon / (k_total * NB))
    return (electron_width, phonon_width)


def solution(mesh):
    in_specs = (
        P(None, "ka", "pb", None),
        P(),
        P(),
        P(),
        P(),
        P("pb", None, None, None),
        P("pb", "ka", None, None, None),
        P("pb", "ka", None),
        P("pb", "ka", None),
        P("ka"),
        P("ka"),
        P("pb", None),
        P("pb", None),
    )
    out_specs = (P("ka", None), P("pb", None))
    return jax.shard_map(
        on_device, mesh=mesh, in_specs=in_specs, out_specs=out_specs, check_vma=False
    )
```

```python
import functools
import math

import jax
import jax.numpy as jnp
from jax import lax
from jax.experimental import pallas as pl
from jax.experimental.pallas import tpu as pltpu
from jax.sharding import PartitionSpec as P

NB = 40
MODES = 120
NG = 100


smearing = 0.05


def phase_table(points, cells):
    product = (
        points[0][:, None] * cells[0][None, :]
        + points[1][:, None] * cells[1][None, :]
        + points[2][:, None] * cells[2][None, :]
    )
    angle = jnp.mod(product, NG).astype(jnp.float32) * (2.0 * math.pi / NG)
    return (jnp.cos(angle).astype(jnp.bfloat16), jnp.sin(angle).astype(jnp.bfloat16))


def gaussian(offset):
    return jnp.exp(-0.5 * (offset / smearing) ** 2) / (smearing * math.sqrt(2.0 * math.pi))


def contract_last(left, right):
    return lax.dot_general(
        left, right, (((1,), (1,)), ((), ())), preferred_element_type=jnp.float32
    )


def mixed(form, left, right):
    return jnp.einsum(form, left, right, preferred_element_type=jnp.float32)


def widths(
    bloch_real, bloch_imag, modes, vectors, levels, filled, energy_k, occupation_k, omega, bose
):
    mode_real = modes[:, 0]
    mode_imag = modes[:, 1]
    moded_real = (
        mixed("kqnm,qmv->kqnv", bloch_real, mode_real)
        - mixed("kqnm,qmv->kqnv", bloch_imag, mode_imag)
    ).astype(jnp.bfloat16)
    moded_imag = (
        mixed("kqnm,qmv->kqnv", bloch_real, mode_imag)
        + mixed("kqnm,qmv->kqnv", bloch_imag, mode_real)
    ).astype(jnp.bfloat16)
    vector_real = vectors[:, :, 0]
    vector_imag = vectors[:, :, 1]
    band_real = mixed("qknb,kqnv->kqbv", vector_real, moded_real) + mixed(
        "qknb,kqnv->kqbv", vector_imag, moded_imag
    )
    band_imag = mixed("qknb,kqnv->kqbv", vector_real, moded_imag) - mixed(
        "qknb,kqnv->kqbv", vector_imag, moded_real
    )
    weight = band_real * band_real + band_imag * band_imag
    level_kq = jnp.transpose(levels, (1, 0, 2))[..., None]
    filled_kq = jnp.transpose(filled, (1, 0, 2))[..., None]
    offset = energy_k[:, None, None, None] - level_kq
    freq = omega[None, :, None, :]
    boson = bose[None, :, None, :]
    absorb = gaussian(offset + freq)
    emit = gaussian(offset - freq)
    electron = jnp.sum(
        weight * ((boson + filled_kq) * absorb + (boson + 1.0 - filled_kq) * emit), axis=(1, 2)
    )
    phonon = jnp.sum(weight * (occupation_k[:, None, None, None] - filled_kq) * absorb, axis=(0, 2))
    return (electron, phonon)


MESH = pl.DeviceIdType.MESH
LANES = 128


def bloch_kernel(
    cells_block, tile, last, wq_ref, wk_ref, x_ref, out_ref,
    half, parts, recv, send_sem, recv_sem,
):
    pairs_step = pl.program_id(0)
    cell_step = pl.program_id(1)
    tiles = pl.num_programs(0)
    cell_steps = pl.num_programs(1)
    bands, kas = lax.axis_size("pb"), lax.axis_size("ka")
    devices = bands * kas
    me = lax.axis_index("pb") * kas + lax.axis_index("ka")
    columns = wq_ref.shape[0]
    cells = half.shape[1] // columns
    groups = parts.shape[2]
    mine = groups // bands
    rows = parts.shape[3] // 2
    barrier = pltpu.get_barrier_semaphore()

    @pl.when((pairs_step == 0) & (cell_step == 0))
    def _():
        def greet(step, carry):
            peer = lax.rem(me + step, devices)
            pl.semaphore_signal(
                barrier, inc=1, device_id={"pb": peer // kas, "ka": lax.rem(peer, kas)},
                device_id_type=MESH,
            )
            return carry

        lax.fori_loop(1, devices, greet, 0)

    for cell in range(cells_block):
        right = jnp.concatenate([x_ref[0, cell], x_ref[1, cell]], axis=0)
        product = jnp.dot(wq_ref[...], right, preferred_element_type=jnp.float32)
        row = cell_step * cells_block + cell
        for lane in range(tile // LANES):
            half[lane, pl.ds(row, columns, stride=cells), :] = product[
                :, lane * LANES : (lane + 1) * LANES
            ]

    def strip(index):
        start = pl.multiple_of(index * cells, cells)
        return jnp.concatenate(
            [half[lane, pl.ds(start, cells), :] for lane in range(tile // LANES)], axis=1
        ).astype(jnp.bfloat16)

    @pl.when(cell_step == cell_steps - 1)
    def _():
        def contract(group, carry):
            sums = []
            for member in range(2):
                q = group * 2 + member
                right = jnp.concatenate([strip(q), strip(columns // 2 + q)], axis=0)
                sums.append(
                    jnp.dot(wk_ref[...], right, preferred_element_type=jnp.float32)
                )
            for ka in range(kas):
                block = slice(ka * rows, (ka + 1) * rows)
                parts[pairs_step, ka, group] = jnp.concatenate(
                    [sums[0][block], sums[1][block]], axis=0
                ).astype(jnp.bfloat16)
            return carry

        lax.fori_loop(0, groups, contract, 0, unroll=4)

    @pl.when((cell_step == cell_steps - 1) & (pairs_step == 0))
    def _():
        pl.semaphore_wait(barrier, devices - 1)

    def send(index, width):
        def one(step, carry):
            peer = lax.rem(me + step, devices)
            to_pb, to_ka = peer // kas, lax.rem(peer, kas)
            pltpu.make_async_remote_copy(
                src_ref=parts.at[index, to_ka, pl.ds(to_pb * mine, mine), :, pl.ds(0, width)],
                dst_ref=recv.at[index, me, :, :, pl.ds(0, width)],
                send_sem=send_sem.at[index],
                recv_sem=recv_sem.at[index],
                device_id={"pb": to_pb, "ka": to_ka},
                device_id_type=MESH,
            ).start()
            return carry

        lax.fori_loop(1, devices, one, 0)

    @pl.when((cell_step == cell_steps - 1) & (pairs_step < tiles - 1))
    def _():
        send(pairs_step, tile)

    @pl.when((cell_step == cell_steps - 1) & (pairs_step == tiles - 1))
    def _():
        count = recv.shape[0]
        send(count - 1, last)
        my_pb, my_ka = lax.axis_index("pb"), lax.axis_index("ka")
        for index in range(count):
            recv[index, me] = parts[index, my_ka, pl.ds(my_pb * mine, mine)]
        for index in range(count):
            width = tile if index < count - 1 else last
            window = recv.at[index, pl.ds(1, devices - 1), :, :, pl.ds(0, width)]
            pltpu.make_async_copy(window, window, send_sem.at[index]).wait()
            pltpu.make_async_copy(window, window, recv_sem.at[index]).wait()
            for band in range(bands):
                total = recv[index, band * kas, :, :, :width].astype(jnp.float32)
                for ka in range(1, kas):
                    total = total + recv[index, band * kas + ka, :, :, :width].astype(jnp.float32)
                out_ref[band, :, :, index * tile : index * tile + width] = total.astype(
                    jnp.bfloat16
                )


def bloch(coupling, wq, wk, q_local, k_local):
    bands, kas = lax.axis_size("pb"), lax.axis_size("ka")
    devices = bands * kas
    parts_count, cells, pairs, phonons = coupling.shape
    moved = jnp.transpose(coupling, (0, 1, 3, 2))
    padded = -(-pairs // LANES) * LANES
    if pairs < LANES:
        moved = jnp.pad(moved, ((0, 0), (0, 0), (0, 0), (0, LANES - pairs)))
    tile = min(2 * LANES, padded)
    tiles = -(-padded // tile)
    last = padded - (tiles - 1) * tile
    cells_block = 16
    columns = wq.shape[0]
    groups = columns // 4
    mine = q_local // 2
    rows = 4 * k_local
    result = pl.pallas_call(
        functools.partial(bloch_kernel, cells_block, tile, last),
        grid=(tiles, cells // cells_block),
        in_specs=[
            pl.BlockSpec(wq.shape, lambda t, e: (0, 0)),
            pl.BlockSpec(wk.shape, lambda t, e: (0, 0)),
            pl.BlockSpec((parts_count, cells_block, phonons, tile), lambda t, e: (0, e, 0, t)),
        ],
        out_specs=pl.BlockSpec((bands, mine, rows, padded), lambda t, e: (0, 0, 0, 0)),
        out_shape=jax.ShapeDtypeStruct((bands, mine, rows, padded), jnp.bfloat16),
        scratch_shapes=[
            pltpu.VMEM((tile // LANES, columns * cells, LANES), jnp.float32),
            pltpu.VMEM((tiles, kas, groups, rows, tile), jnp.bfloat16),
            pltpu.VMEM((tiles, devices, mine, rows, tile), jnp.bfloat16),
            pltpu.SemaphoreType.DMA((tiles,)),
            pltpu.SemaphoreType.DMA((tiles,)),
        ],
        compiler_params=pltpu.CompilerParams(
            collective_id=0,
            has_side_effects=True,
            dimension_semantics=("arbitrary", "arbitrary"),
            vmem_limit_bytes=60 * 1024 * 1024,
        ),
        name="bloch",
    )(wq, wk, moved)
    return result[..., :pairs]


def sums_kernel(electron_ref, phonon_ref, electron_out, phonon_out, got_e, got_p, send, recv_e, recv_p):
    bands, kas = lax.axis_size("pb"), lax.axis_size("ka")
    my_pb, my_ka = lax.axis_index("pb"), lax.axis_index("ka")
    barrier = pltpu.get_barrier_semaphore()
    for step in range(1, bands):
        pl.semaphore_signal(
            barrier, inc=1, device_id={"pb": lax.rem(my_pb + step, bands), "ka": my_ka},
            device_id_type=MESH,
        )
    for step in range(1, kas):
        pl.semaphore_signal(
            barrier, inc=1, device_id={"pb": my_pb, "ka": lax.rem(my_ka + step, kas)},
            device_id_type=MESH,
        )
    pl.semaphore_wait(barrier, bands + kas - 2)
    copies = []
    for step in range(1, bands):
        copies.append(pltpu.make_async_remote_copy(
            electron_ref, got_e.at[my_pb], send.at[step - 1], recv_e.at[step - 1],
            device_id={"pb": lax.rem(my_pb + step, bands), "ka": my_ka}, device_id_type=MESH,
        ))
    for step in range(1, kas):
        copies.append(pltpu.make_async_remote_copy(
            phonon_ref, got_p.at[my_ka], send.at[bands + step - 2], recv_p.at[step - 1],
            device_id={"pb": my_pb, "ka": lax.rem(my_ka + step, kas)}, device_id_type=MESH,
        ))
    for copy in copies:
        copy.start()
    got_e[my_pb] = electron_ref[...]
    got_p[my_ka] = phonon_ref[...]
    for copy in copies:
        copy.wait()
    total = got_e[0]
    for step in range(1, bands):
        total = total + got_e[step]
    electron_out[...] = total
    total = got_p[0]
    for step in range(1, kas):
        total = total + got_p[step]
    phonon_out[...] = total


def exchange(electron, phonon):
    bands, kas = lax.axis_size("pb"), lax.axis_size("ka")
    whole = pl.BlockSpec(memory_space=pltpu.VMEM)
    return pl.pallas_call(
        sums_kernel,
        in_specs=[whole, whole],
        out_specs=[whole, whole],
        out_shape=[
            jax.ShapeDtypeStruct(electron.shape, electron.dtype),
            jax.ShapeDtypeStruct(phonon.shape, phonon.dtype),
        ],
        scratch_shapes=[
            pltpu.VMEM((bands, *electron.shape), jnp.float32),
            pltpu.VMEM((kas, *phonon.shape), jnp.float32),
            pltpu.SemaphoreType.DMA((bands + kas - 2,)),
            pltpu.SemaphoreType.DMA((bands - 1,)),
            pltpu.SemaphoreType.DMA((kas - 1,)),
        ],
        compiler_params=pltpu.CompilerParams(collective_id=1, has_side_effects=True),
        name="sums",
    )(electron, phonon)


def angles(points, cells):
    product = lax.dot_general(
        points.astype(jnp.float32).astype(jnp.bfloat16),
        cells.astype(jnp.float32).astype(jnp.bfloat16),
        (((0,), (0,)), ((), ())),
        preferred_element_type=jnp.float32,
    )
    turns = jnp.floor((product + 0.5) * (1.0 / NG))
    angle = (product - turns * NG) * (2.0 * math.pi / NG)
    return jnp.cos(angle), jnp.sin(angle)


def ring_kernel(
    pairs, kpoints, qpoints, electron_cells, phonon_cells, modes, vectors,
    levels, filled, energy_k, occupation_k, omega, bose, edge_ref, x_hbm, out_ref,
    wq, wk, half, ring, parts, recv, relay, sums, table, lifted, rows_ref, turned,
    emission, absorption, totals, got_e, got_p,
    ring_sem, relay_send, relay_recv, plane_send, plane_recv, raw_send, raw_recv,
    sum_send, sum_recv, send_e, recv_e, send_p, recv_p,
):
    step = pl.program_id(0)
    steps = pl.num_programs(0)
    bands, kas = lax.axis_size("pb"), lax.axis_size("ka")
    devices = bands * kas
    my_pb, my_ka = lax.axis_index("pb"), lax.axis_index("ka")
    me = my_pb * kas + my_ka
    columns = wq.shape[0]
    q_total = columns // 2
    pitch = half.shape[0] // columns
    cells = wk.shape[1] // 2
    slots, unit = ring.shape[0], ring.shape[2]
    chunks = cells // unit
    tiles = parts.shape[0]
    halves = parts.shape[3]
    mine = 2 * halves
    q_local, k_local = vectors.shape[0], vectors.shape[1]
    rows = 2 * k_local
    bands_n = vectors.shape[3]
    bands_own = bands_n // bands
    up, down = lax.rem(my_ka + 1, kas), lax.rem(my_ka + kas - 1, kas)
    across = lax.rem(my_ka + 2, kas)
    barrier = pltpu.get_barrier_semaphore()
    overlaps = []
    for tile in range(tiles):
        for n in range(bands_own):
            low = max(tile * LANES, n * MODES)
            high = min((tile + 1) * LANES, (n + 1) * MODES)
            if low < high:
                overlaps.append((tile, n, low - tile * LANES, low - n * MODES, high - low))

    def fetch(index, slot):
        tile, chunk = index // chunks, lax.rem(index, chunks)
        return pltpu.make_async_copy(
            x_hbm.at[
                :, pl.ds(chunk * unit, unit), :, pl.ds(pl.multiple_of(tile * LANES, LANES), LANES)
            ],
            ring.at[slot],
            ring_sem.at[slot],
        )

    def project(real, imag, row):
        right = jnp.concatenate([real, imag], axis=0)
        product = jnp.dot(wq[...], right, preferred_element_type=jnp.float32)
        half[pl.ds(row, columns, stride=pitch), :] = product

    def strip(index):
        return half[index * pitch : index * pitch + cells, :].astype(jnp.bfloat16)

    def contract(order):
        for group in range(q_total // 2):
            right = jnp.concatenate(
                [
                    jnp.concatenate([strip(q), strip(q_total + q)], axis=0)
                    for q in (group * 2, group * 2 + 1)
                ],
                axis=1,
            )
            product = jnp.dot(wk[...], right, preferred_element_type=jnp.float32)
            m = group % mine
            for ka in range(kas):
                block = slice(ka * rows, (ka + 1) * rows)
                parts[order, ka, m // halves, m % halves, group // mine] = jnp.concatenate(
                    [product[block, :LANES], product[block, LANES:]], axis=0
                ).astype(jnp.bfloat16)

    def put(source, target, send_sem, recv_sem, to_pb, to_ka):
        pltpu.make_async_remote_copy(
            src_ref=source, dst_ref=target, send_sem=send_sem, recv_sem=recv_sem,
            device_id={"pb": to_pb, "ka": to_ka}, device_id_type=MESH,
        ).start()

    def settle(window, sem):
        pltpu.make_async_copy(window, window, sem).wait()

    def send(order):
        put(parts.at[order, across, 0], relay.at[order, 0], relay_send.at[0, order],
            relay_recv.at[0, order], my_pb, up)
        put(parts.at[order, across, 1], relay.at[order, 1], relay_send.at[1, order],
            relay_recv.at[1, order], my_pb, down)

        def raw(index, carry):
            to = lax.rem(my_pb + index, bands)
            put(parts.at[order, up, 1, :, to], recv.at[order, 1, 1, :, my_pb],
                raw_send.at[0, order], raw_recv.at[0, order], to, up)
            put(parts.at[order, down, 0, :, to], recv.at[order, 2, 0, :, my_pb],
                raw_send.at[1, order], raw_recv.at[1, order], to, down)
            return carry

        lax.fori_loop(0, bands, raw, 0)

        def plane(index, carry):
            to = lax.rem(my_pb + index, bands)
            put(parts.at[order, my_ka, :, :, to], recv.at[order, 0, :, :, my_pb],
                plane_send.at[order], plane_recv.at[order], to, my_ka)
            return carry

        lax.fori_loop(1, bands, plane, 0)

    def pass_on(order):
        for way, (target, place) in enumerate(((up, 1), (down, 2))):
            settle(relay.at[order, way], relay_recv.at[way, order])
            own = parts[order, target, way].astype(jnp.float32)
            sums[order, way] = (own + relay[order, way].astype(jnp.float32)).astype(jnp.bfloat16)

            def one(index, carry, way=way, target=target, place=place):
                to = lax.rem(my_pb + index, bands)
                put(sums.at[order, way, :, to], recv.at[order, place, way, :, my_pb],
                    sum_send.at[way, order], sum_recv.at[way, order], to, target)
                return carry

            lax.fori_loop(0, bands, one, 0)

    edge_cells = edge_ref.shape[1]

    def edge(index, carry):
        for inner in range(unit):
            cell = index * unit + inner
            project(edge_ref[0, cell], edge_ref[1, cell], step * edge_cells + cell)
        return carry

    @pl.when(step == 0)
    def _():
        def greet(index, carry):
            peer = lax.rem(me + index, devices)
            pl.semaphore_signal(
                barrier, inc=1, device_id={"pb": peer // kas, "ka": lax.rem(peer, kas)},
                device_id_type=MESH,
            )
            return carry

        lax.fori_loop(1, devices, greet, 0)

        def first(index, carry):
            fetch(index, index).start()
            return carry

        lax.fori_loop(0, slots, first, 0)
        cos, sin = angles(qpoints[...], phonon_cells[...])
        wq[...] = jnp.concatenate(
            [jnp.concatenate([cos, -sin], 1), jnp.concatenate([sin, cos], 1)], 0
        ).astype(jnp.bfloat16)
        cells_all = electron_cells[...]
        own = cells_all[:, :cells]
        for ka in range(1, kas):
            own = jnp.where(my_ka == ka, cells_all[:, ka * cells : (ka + 1) * cells], own)
        cos, sin = angles(kpoints[...], own)
        blocks = []
        for ka in range(kas):
            c = cos[ka * k_local : (ka + 1) * k_local]
            s = sin[ka * k_local : (ka + 1) * k_local]
            blocks += [jnp.concatenate([c, -s], 1), jnp.concatenate([s, c], 1)]
        wk[...] = jnp.concatenate(blocks, 0).astype(jnp.bfloat16)

    lax.fori_loop(0, edge_cells // unit, edge, 0)

    def prepare():
        for q in range(q_local):
            freq = omega[q : q + 1, :]
            boson = bose[q : q + 1, :]
            level_q = jnp.transpose(levels[q])
            filled_q = jnp.transpose(filled[q])
            for k in range(k_local):
                f = filled_q[:, k : k + 1]
                offset = energy_k[k] - level_q[:, k : k + 1]
                absorb = gaussian(offset + freq)
                emit = gaussian(offset - freq)
                emission[q, k] = (boson + f) * absorb + (boson + 1.0 - f) * emit
                absorption[q, k] = (occupation_k[k] - f) * absorb
                for part in range(2):
                    rows_ref[part, :, :bands_n] = vectors[q, k, part].astype(jnp.float32)
                real, imag = (
                    jnp.concatenate(
                        [
                            rows_ref[part, pl.ds(n, bands, stride=bands_own), :]
                            for n in range(bands_own)
                        ],
                        axis=0,
                    )[:, :bands_n]
                    for part in range(2)
                )
                both = jnp.concatenate(
                    [jnp.concatenate([real, -imag], 1), jnp.concatenate([imag, real], 1)], 0
                )
                turned[q, k] = jnp.transpose(both).astype(jnp.bfloat16)
            for part in range(2):
                mode = modes[q, part].astype(jnp.float32)
                for index, (tile, n, row, start, count) in enumerate(overlaps):
                    pieces = []
                    if row:
                        pieces.append(jnp.zeros((row, MODES), jnp.float32))
                    pieces.append(mode[start : start + count])
                    if row + count < LANES:
                        pieces.append(jnp.zeros((LANES - row - count, MODES), jnp.float32))
                    placed = jnp.concatenate(pieces, 0) if len(pieces) > 1 else pieces[0]
                    table[q, index, :, part * LANES : part * LANES + MODES] = placed.astype(
                        jnp.bfloat16
                    )

    @pl.when(step == steps - 1)
    def _():
        contract(0)
        pl.semaphore_wait(barrier, devices - 1)
        send(0)

        def one_tile(tile, carry):
            def one_chunk(chunk, inner_carry):
                index = tile * chunks + chunk
                slot = lax.rem(index, slots)
                fetch(index, slot).wait()
                for inner in range(unit):
                    project(ring[slot, 0, inner], ring[slot, 1, inner], chunk * unit + inner)

                @pl.when(index + slots < (tiles - 1) * chunks)
                def _():
                    fetch(index + slots, slot).start()

                return inner_carry

            lax.fori_loop(0, chunks, one_chunk, 0)
            contract(tile + 1)
            send(tile + 1)

            @pl.when(tile >= 1)
            def _():
                pass_on(tile - 1)

            return carry

        lax.fori_loop(0, tiles - 1, one_tile, 0)
        for order in range(tiles):
            recv[order, 0, :, :, my_pb] = parts[order, my_ka, :, :, my_pb]
        pass_on(tiles - 2)
        pass_on(tiles - 1)
        prepare()
        lane = lax.broadcasted_iota(jnp.int32, (1, LANES), 1)
        started = set()
        for order in range(tiles):
            tile = tiles - 1 if order == 0 else order - 1
            settle(recv.at[order, 0, :, :, pl.ds(1, bands - 1)], plane_recv.at[order])
            for way in range(2):
                settle(recv.at[order, 1 + way, 1 - way], raw_recv.at[way, order])
            for way in range(2):
                settle(recv.at[order, 1 + way, way], sum_recv.at[way, order])
            for m in range(mine):
                spot = (m // halves, m % halves)
                total = [
                    recv[order, 0, *spot, band].astype(jnp.float32)
                    + recv[order, 1, *spot, band].astype(jnp.float32)
                    + recv[order, 2, *spot, band].astype(jnp.float32)
                    for band in range(bands)
                ]
                for member in range(2):
                    q = 2 * m + member
                    left = jnp.concatenate(
                        [one[member * rows : (member + 1) * rows] for one in total], axis=0
                    )
                    if pairs < (tile + 1) * LANES:
                        left = jnp.where(lane < pairs - tile * LANES, left, 0.0)
                    left = left.astype(jnp.bfloat16)
                    for index, (other, n, _, _, _) in enumerate(overlaps):
                        if other != tile:
                            continue
                        product = jnp.dot(
                            left, table[q, index], preferred_element_type=jnp.float32
                        )
                        for side in range(2):
                            value = product[:, side * LANES : (side + 1) * LANES]
                            if (q, n) in started:
                                value = value + lifted[q, n, side]
                            lifted[q, n, side] = value
                        started.add((q, n))
        electron = [None] * k_local
        for q in range(q_local):
            phonon = None
            for k in range(k_local):
                real, imag = [], []
                for n in range(bands_own):
                    rr, ri, ir, ii = (
                        lifted[q, n, side, pl.ds(part * k_local + k, bands, stride=rows), :]
                        for part in range(2)
                        for side in range(2)
                    )
                    real.append(rr - ii)
                    imag.append(ri + ir)
                right = jnp.concatenate(real + imag, axis=0).astype(jnp.bfloat16)
                band = jnp.dot(turned[q, k], right, preferred_element_type=jnp.float32)
                band_real = band[:bands_n, :MODES]
                band_imag = band[bands_n:, :MODES]
                weight = band_real * band_real + band_imag * band_imag
                e_term = weight * emission[q, k]
                p_term = weight * absorption[q, k]
                electron[k] = e_term if q == 0 else electron[k] + e_term
                phonon = p_term if k == 0 else phonon + p_term
            totals[1, q : q + 1, :] = jnp.sum(phonon, axis=0, keepdims=True)
        for k in range(k_local):
            totals[0, k : k + 1, :] = jnp.sum(electron[k], axis=0, keepdims=True)
        copies = []
        for shift in range(1, bands):
            copies.append(pltpu.make_async_remote_copy(
                totals.at[0], got_e.at[my_pb], send_e.at[shift - 1], recv_e.at[shift - 1],
                device_id={"pb": lax.rem(my_pb + shift, bands), "ka": my_ka}, device_id_type=MESH,
            ))
        for shift in range(1, kas):
            copies.append(pltpu.make_async_remote_copy(
                totals.at[1], got_p.at[my_ka], send_p.at[shift - 1], recv_p.at[shift - 1],
                device_id={"pb": my_pb, "ka": lax.rem(my_ka + shift, kas)}, device_id_type=MESH,
            ))
        for copy in copies:
            copy.start()
        got_e[my_pb] = totals[0]
        got_p[my_ka] = totals[1]
        for order in range(tiles):
            settle(recv.at[order, 0, :, :, pl.ds(1, bands - 1)], plane_send.at[order])
            for way in range(2):
                settle(relay.at[order, way], relay_send.at[way, order])
                settle(recv.at[order, 1 + way, 1 - way], raw_send.at[way, order])
                settle(recv.at[order, 1 + way, way], sum_send.at[way, order])
        for copy in copies:
            copy.wait()
        total = got_e[0]
        for other in range(1, bands):
            total = total + got_e[other]
        out_ref[0] = total
        total = got_p[0]
        for other in range(1, kas):
            total = total + got_p[other]
        out_ref[1] = total


def everything(
    coupling, kpoints, qpoints, electron_cells, phonon_cells, phonon_modes, band_vectors,
    energies_kq, occupations_kq, energy_k, occupation_k, frequencies, bose_factors,
):
    bands, kas = lax.axis_size("pb"), lax.axis_size("ka")
    parts_count, cells, pairs, phonons = coupling.shape
    moved = jnp.transpose(coupling, (0, 1, 3, 2))
    tiles = -(-pairs // LANES)
    unit = cells // 2
    pitch = 8 * (-(-cells // 8) | 1)
    slots = 4
    q_local, k_local = band_vectors.shape[0], band_vectors.shape[1]
    bands_n = band_vectors.shape[3]
    columns = 2 * qpoints.shape[1]
    halves = q_local // 4
    rows = 4 * k_local
    bands_own = bands_n // bands
    overlaps = sum(
        max(t * LANES, n * MODES) < min((t + 1) * LANES, (n + 1) * MODES)
        for t in range(tiles)
        for n in range(bands_own)
    )
    small = pl.BlockSpec(memory_space=pltpu.VMEM)
    scalars = pl.BlockSpec(memory_space=pltpu.SMEM)
    dma = pltpu.SemaphoreType.DMA
    bf16, f32 = jnp.bfloat16, jnp.float32
    return pl.pallas_call(
        functools.partial(ring_kernel, pairs),
        grid=(2,),
        in_specs=[small] * 8
        + [scalars] * 2
        + [small] * 2
        + [
            pl.BlockSpec((parts_count, cells // 2, phonons, LANES), lambda e: (0, e, 0, tiles - 1)),
            pl.BlockSpec(memory_space=pl.ANY),
        ],
        out_specs=small,
        out_shape=jax.ShapeDtypeStruct((2, k_local, MODES), f32),
        scratch_shapes=[
            pltpu.VMEM((columns, 2 * phonons), bf16),
            pltpu.VMEM((2 * k_local * kas, 2 * cells), bf16),
            pltpu.VMEM((columns * pitch, LANES), f32),
            pltpu.VMEM((slots, parts_count, unit, phonons, LANES), bf16),
            pltpu.VMEM((tiles, kas, 2, halves, bands, rows, LANES), bf16),
            pltpu.VMEM((tiles, 3, 2, halves, bands, rows, LANES), bf16),
            pltpu.VMEM((tiles, 2, halves, bands, rows, LANES), bf16),
            pltpu.VMEM((tiles, 2, halves, bands, rows, LANES), bf16),
            pltpu.VMEM((q_local, overlaps, LANES, 2 * LANES), bf16),
            pltpu.VMEM((q_local, bands_own, 2, bands * 2 * k_local, LANES), f32),
            pltpu.VMEM((2, bands_n, LANES), f32),
            pltpu.VMEM((q_local, k_local, 2 * bands_n, 2 * bands_n), bf16),
            pltpu.VMEM((q_local, k_local, bands_n, MODES), f32),
            pltpu.VMEM((q_local, k_local, bands_n, MODES), f32),
            pltpu.VMEM((2, k_local, MODES), f32),
            pltpu.VMEM((bands, k_local, MODES), f32),
            pltpu.VMEM((kas, k_local, MODES), f32),
            dma((slots,)),
            dma((2, tiles)),
            dma((2, tiles)),
            dma((tiles,)),
            dma((tiles,)),
            dma((2, tiles)),
            dma((2, tiles)),
            dma((2, tiles)),
            dma((2, tiles)),
            dma((bands - 1,)),
            dma((bands - 1,)),
            dma((kas - 1,)),
            dma((kas - 1,)),
        ],
        compiler_params=pltpu.CompilerParams(
            collective_id=2,
            has_side_effects=True,
            dimension_semantics=("arbitrary",),
            vmem_limit_bytes=60 * 1024 * 1024,
        ),
        name="widths",
    )(
        kpoints, qpoints, electron_cells, phonon_cells, phonon_modes, band_vectors, energies_kq,
        occupations_kq, energy_k, occupation_k, frequencies, bose_factors, moved, moved,
    )


def on_device(
    coupling,
    kpoints,
    qpoints,
    electron_cells,
    phonon_cells,
    phonon_modes,
    band_vectors,
    energies_kq,
    occupations_kq,
    energy_k,
    occupation_k,
    frequencies,
    bose_factors,
):
    k_local = energy_k.shape[0]
    q_local = frequencies.shape[0]
    cells_local = coupling.shape[1]
    bands, kas = lax.axis_size("pb"), lax.axis_size("ka")
    q_total = q_local * bands
    k_total = k_local * kas
    whole_bands = coupling.shape[2] % MODES == 0 and coupling.shape[2] > LANES
    even = q_local % 4 == 0 and cells_local % 16 == 0
    if kas == 4 and whole_bands and even and k_local == q_local:
        sums = everything(
            coupling, kpoints, qpoints, electron_cells, phonon_cells, phonon_modes, band_vectors,
            energies_kq, occupations_kq, energy_k, occupation_k, frequencies, bose_factors,
        )
        return (sums[0] / (q_total * NB), sums[1] / (k_total * NB))
    cos_q, sin_q = phase_table(qpoints, phonon_cells)
    own_cells = lax.dynamic_slice_in_dim(
        electron_cells, lax.axis_index("ka") * cells_local, cells_local, 1
    )
    cos_k, sin_k = phase_table(kpoints, own_cells)
    wq = jnp.concatenate(
        [jnp.concatenate([cos_q, -sin_q], 1), jnp.concatenate([sin_q, cos_q], 1)], 0
    )
    wk = jnp.stack(
        [jnp.concatenate([cos_k, -sin_k], 1), jnp.concatenate([sin_k, cos_k], 1)], 1
    ).reshape(2 * k_total, 2 * cells_local)
    values = bloch(coupling, wq, wk, q_local, k_local)
    values = values.reshape(bands, q_local // 2, 2, k_local, 2, -1)
    values = jnp.transpose(values, (4, 3, 1, 2, 0, 5)).reshape(2, k_local, q_local, NB, MODES)
    electron, phonon = widths(
        values[0],
        values[1],
        phonon_modes,
        band_vectors,
        energies_kq,
        occupations_kq,
        energy_k,
        occupation_k,
        frequencies,
        bose_factors,
    )
    electron_width, phonon_width = exchange(electron / (q_total * NB), phonon / (k_total * NB))
    return (electron_width, phonon_width)


def solution(mesh):
    in_specs = (
        P(None, "ka", "pb", None),
        P(),
        P(),
        P(),
        P(),
        P("pb", None, None, None),
        P("pb", "ka", None, None, None),
        P("pb", "ka", None),
        P("pb", "ka", None),
        P("ka"),
        P("ka"),
        P("pb", None),
        P("pb", None),
    )
    out_specs = (P("ka", None), P("pb", None))
    return jax.shard_map(
        on_device, mesh=mesh, in_specs=in_specs, out_specs=out_specs, check_vma=False
    )
```

```python
import functools
import math

import jax
import jax.numpy as jnp
from jax import lax
from jax.experimental import pallas as pl
from jax.experimental.pallas import tpu as pltpu
from jax.sharding import PartitionSpec as P

NB = 40
MODES = 120
NG = 100


smearing = 0.05


def phase_table(points, cells):
    product = (
        points[0][:, None] * cells[0][None, :]
        + points[1][:, None] * cells[1][None, :]
        + points[2][:, None] * cells[2][None, :]
    )
    angle = jnp.mod(product, NG).astype(jnp.float32) * (2.0 * math.pi / NG)
    return (jnp.cos(angle).astype(jnp.bfloat16), jnp.sin(angle).astype(jnp.bfloat16))


def gaussian(offset):
    return jnp.exp(-0.5 * (offset / smearing) ** 2) / (smearing * math.sqrt(2.0 * math.pi))


def contract_last(left, right):
    return lax.dot_general(
        left, right, (((1,), (1,)), ((), ())), preferred_element_type=jnp.float32
    )


def mixed(form, left, right):
    return jnp.einsum(form, left, right, preferred_element_type=jnp.float32)


def widths(
    bloch_real, bloch_imag, modes, vectors, levels, filled, energy_k, occupation_k, omega, bose
):
    mode_real = modes[:, 0]
    mode_imag = modes[:, 1]
    moded_real = (
        mixed("kqnm,qmv->kqnv", bloch_real, mode_real)
        - mixed("kqnm,qmv->kqnv", bloch_imag, mode_imag)
    ).astype(jnp.bfloat16)
    moded_imag = (
        mixed("kqnm,qmv->kqnv", bloch_real, mode_imag)
        + mixed("kqnm,qmv->kqnv", bloch_imag, mode_real)
    ).astype(jnp.bfloat16)
    vector_real = vectors[:, :, 0]
    vector_imag = vectors[:, :, 1]
    band_real = mixed("qknb,kqnv->kqbv", vector_real, moded_real) + mixed(
        "qknb,kqnv->kqbv", vector_imag, moded_imag
    )
    band_imag = mixed("qknb,kqnv->kqbv", vector_real, moded_imag) - mixed(
        "qknb,kqnv->kqbv", vector_imag, moded_real
    )
    weight = band_real * band_real + band_imag * band_imag
    level_kq = jnp.transpose(levels, (1, 0, 2))[..., None]
    filled_kq = jnp.transpose(filled, (1, 0, 2))[..., None]
    offset = energy_k[:, None, None, None] - level_kq
    freq = omega[None, :, None, :]
    boson = bose[None, :, None, :]
    absorb = gaussian(offset + freq)
    emit = gaussian(offset - freq)
    electron = jnp.sum(
        weight * ((boson + filled_kq) * absorb + (boson + 1.0 - filled_kq) * emit), axis=(1, 2)
    )
    phonon = jnp.sum(weight * (occupation_k[:, None, None, None] - filled_kq) * absorb, axis=(0, 2))
    return (electron, phonon)


MESH = pl.DeviceIdType.MESH
LANES = 128


def bloch_kernel(
    cells_block, tile, last, wq_ref, wk_ref, x_ref, out_ref,
    half, parts, recv, send_sem, recv_sem,
):
    pairs_step = pl.program_id(0)
    cell_step = pl.program_id(1)
    tiles = pl.num_programs(0)
    cell_steps = pl.num_programs(1)
    bands, kas = lax.axis_size("pb"), lax.axis_size("ka")
    devices = bands * kas
    me = lax.axis_index("pb") * kas + lax.axis_index("ka")
    columns = wq_ref.shape[0]
    cells = half.shape[1] // columns
    groups = parts.shape[2]
    mine = groups // bands
    rows = parts.shape[3] // 2
    barrier = pltpu.get_barrier_semaphore()

    @pl.when((pairs_step == 0) & (cell_step == 0))
    def _():
        def greet(step, carry):
            peer = lax.rem(me + step, devices)
            pl.semaphore_signal(
                barrier, inc=1, device_id={"pb": peer // kas, "ka": lax.rem(peer, kas)},
                device_id_type=MESH,
            )
            return carry

        lax.fori_loop(1, devices, greet, 0)

    for cell in range(cells_block):
        right = jnp.concatenate([x_ref[0, cell], x_ref[1, cell]], axis=0)
        product = jnp.dot(wq_ref[...], right, preferred_element_type=jnp.float32)
        row = cell_step * cells_block + cell
        for lane in range(tile // LANES):
            half[lane, pl.ds(row, columns, stride=cells), :] = product[
                :, lane * LANES : (lane + 1) * LANES
            ]

    def strip(index):
        start = pl.multiple_of(index * cells, cells)
        return jnp.concatenate(
            [half[lane, pl.ds(start, cells), :] for lane in range(tile // LANES)], axis=1
        ).astype(jnp.bfloat16)

    @pl.when(cell_step == cell_steps - 1)
    def _():
        def contract(group, carry):
            sums = []
            for member in range(2):
                q = group * 2 + member
                right = jnp.concatenate([strip(q), strip(columns // 2 + q)], axis=0)
                sums.append(
                    jnp.dot(wk_ref[...], right, preferred_element_type=jnp.float32)
                )
            for ka in range(kas):
                block = slice(ka * rows, (ka + 1) * rows)
                parts[pairs_step, ka, group] = jnp.concatenate(
                    [sums[0][block], sums[1][block]], axis=0
                ).astype(jnp.bfloat16)
            return carry

        lax.fori_loop(0, groups, contract, 0, unroll=4)

    @pl.when((cell_step == cell_steps - 1) & (pairs_step == 0))
    def _():
        pl.semaphore_wait(barrier, devices - 1)

    def send(index, width):
        def one(step, carry):
            peer = lax.rem(me + step, devices)
            to_pb, to_ka = peer // kas, lax.rem(peer, kas)
            pltpu.make_async_remote_copy(
                src_ref=parts.at[index, to_ka, pl.ds(to_pb * mine, mine), :, pl.ds(0, width)],
                dst_ref=recv.at[index, me, :, :, pl.ds(0, width)],
                send_sem=send_sem.at[index],
                recv_sem=recv_sem.at[index],
                device_id={"pb": to_pb, "ka": to_ka},
                device_id_type=MESH,
            ).start()
            return carry

        lax.fori_loop(1, devices, one, 0)

    @pl.when((cell_step == cell_steps - 1) & (pairs_step < tiles - 1))
    def _():
        send(pairs_step, tile)

    @pl.when((cell_step == cell_steps - 1) & (pairs_step == tiles - 1))
    def _():
        count = recv.shape[0]
        send(count - 1, last)
        my_pb, my_ka = lax.axis_index("pb"), lax.axis_index("ka")
        for index in range(count):
            recv[index, me] = parts[index, my_ka, pl.ds(my_pb * mine, mine)]
        for index in range(count):
            width = tile if index < count - 1 else last
            window = recv.at[index, pl.ds(1, devices - 1), :, :, pl.ds(0, width)]
            pltpu.make_async_copy(window, window, send_sem.at[index]).wait()
            pltpu.make_async_copy(window, window, recv_sem.at[index]).wait()
            for band in range(bands):
                total = recv[index, band * kas, :, :, :width].astype(jnp.float32)
                for ka in range(1, kas):
                    total = total + recv[index, band * kas + ka, :, :, :width].astype(jnp.float32)
                out_ref[band, :, :, index * tile : index * tile + width] = total.astype(
                    jnp.bfloat16
                )


def bloch(coupling, wq, wk, q_local, k_local):
    bands, kas = lax.axis_size("pb"), lax.axis_size("ka")
    devices = bands * kas
    parts_count, cells, pairs, phonons = coupling.shape
    moved = jnp.transpose(coupling, (0, 1, 3, 2))
    padded = -(-pairs // LANES) * LANES
    if pairs < LANES:
        moved = jnp.pad(moved, ((0, 0), (0, 0), (0, 0), (0, LANES - pairs)))
    tile = min(2 * LANES, padded)
    tiles = -(-padded // tile)
    last = padded - (tiles - 1) * tile
    cells_block = 16
    columns = wq.shape[0]
    groups = columns // 4
    mine = q_local // 2
    rows = 4 * k_local
    result = pl.pallas_call(
        functools.partial(bloch_kernel, cells_block, tile, last),
        grid=(tiles, cells // cells_block),
        in_specs=[
            pl.BlockSpec(wq.shape, lambda t, e: (0, 0)),
            pl.BlockSpec(wk.shape, lambda t, e: (0, 0)),
            pl.BlockSpec((parts_count, cells_block, phonons, tile), lambda t, e: (0, e, 0, t)),
        ],
        out_specs=pl.BlockSpec((bands, mine, rows, padded), lambda t, e: (0, 0, 0, 0)),
        out_shape=jax.ShapeDtypeStruct((bands, mine, rows, padded), jnp.bfloat16),
        scratch_shapes=[
            pltpu.VMEM((tile // LANES, columns * cells, LANES), jnp.float32),
            pltpu.VMEM((tiles, kas, groups, rows, tile), jnp.bfloat16),
            pltpu.VMEM((tiles, devices, mine, rows, tile), jnp.bfloat16),
            pltpu.SemaphoreType.DMA((tiles,)),
            pltpu.SemaphoreType.DMA((tiles,)),
        ],
        compiler_params=pltpu.CompilerParams(
            collective_id=0,
            has_side_effects=True,
            dimension_semantics=("arbitrary", "arbitrary"),
            vmem_limit_bytes=60 * 1024 * 1024,
        ),
        name="bloch",
    )(wq, wk, moved)
    return result[..., :pairs]


def sums_kernel(electron_ref, phonon_ref, electron_out, phonon_out, got_e, got_p, send, recv_e, recv_p):
    bands, kas = lax.axis_size("pb"), lax.axis_size("ka")
    my_pb, my_ka = lax.axis_index("pb"), lax.axis_index("ka")
    barrier = pltpu.get_barrier_semaphore()
    for step in range(1, bands):
        pl.semaphore_signal(
            barrier, inc=1, device_id={"pb": lax.rem(my_pb + step, bands), "ka": my_ka},
            device_id_type=MESH,
        )
    for step in range(1, kas):
        pl.semaphore_signal(
            barrier, inc=1, device_id={"pb": my_pb, "ka": lax.rem(my_ka + step, kas)},
            device_id_type=MESH,
        )
    pl.semaphore_wait(barrier, bands + kas - 2)
    copies = []
    for step in range(1, bands):
        copies.append(pltpu.make_async_remote_copy(
            electron_ref, got_e.at[my_pb], send.at[step - 1], recv_e.at[step - 1],
            device_id={"pb": lax.rem(my_pb + step, bands), "ka": my_ka}, device_id_type=MESH,
        ))
    for step in range(1, kas):
        copies.append(pltpu.make_async_remote_copy(
            phonon_ref, got_p.at[my_ka], send.at[bands + step - 2], recv_p.at[step - 1],
            device_id={"pb": my_pb, "ka": lax.rem(my_ka + step, kas)}, device_id_type=MESH,
        ))
    for copy in copies:
        copy.start()
    got_e[my_pb] = electron_ref[...]
    got_p[my_ka] = phonon_ref[...]
    for copy in copies:
        copy.wait()
    total = got_e[0]
    for step in range(1, bands):
        total = total + got_e[step]
    electron_out[...] = total
    total = got_p[0]
    for step in range(1, kas):
        total = total + got_p[step]
    phonon_out[...] = total


def exchange(electron, phonon):
    bands, kas = lax.axis_size("pb"), lax.axis_size("ka")
    whole = pl.BlockSpec(memory_space=pltpu.VMEM)
    return pl.pallas_call(
        sums_kernel,
        in_specs=[whole, whole],
        out_specs=[whole, whole],
        out_shape=[
            jax.ShapeDtypeStruct(electron.shape, electron.dtype),
            jax.ShapeDtypeStruct(phonon.shape, phonon.dtype),
        ],
        scratch_shapes=[
            pltpu.VMEM((bands, *electron.shape), jnp.float32),
            pltpu.VMEM((kas, *phonon.shape), jnp.float32),
            pltpu.SemaphoreType.DMA((bands + kas - 2,)),
            pltpu.SemaphoreType.DMA((bands - 1,)),
            pltpu.SemaphoreType.DMA((kas - 1,)),
        ],
        compiler_params=pltpu.CompilerParams(collective_id=1, has_side_effects=True),
        name="sums",
    )(electron, phonon)


def angles(points, cells):
    product = lax.dot_general(
        points.astype(jnp.float32).astype(jnp.bfloat16),
        cells.astype(jnp.float32).astype(jnp.bfloat16),
        (((0,), (0,)), ((), ())),
        preferred_element_type=jnp.float32,
    )
    turns = jnp.floor((product + 0.5) * (1.0 / NG))
    angle = (product - turns * NG) * (2.0 * math.pi / NG)
    return jnp.cos(angle), jnp.sin(angle)


def ring_kernel(
    pairs, kpoints, qpoints, electron_cells, phonon_cells, modes, vectors,
    levels, filled, energy_k, occupation_k, omega, bose, edge_ref, x_hbm, out_ref,
    wq, wk, half, ring, parts, recv, relay, sums, table, lifted, rows_ref, turned,
    emission, absorption, totals, got_e, got_p,
    ring_sem, relay_send, relay_recv, plane_send, plane_recv, raw_send, raw_recv,
    sum_send, sum_recv, send_e, recv_e, send_p, recv_p,
):
    step = pl.program_id(0)
    steps = pl.num_programs(0)
    bands, kas = lax.axis_size("pb"), lax.axis_size("ka")
    devices = bands * kas
    my_pb, my_ka = lax.axis_index("pb"), lax.axis_index("ka")
    me = my_pb * kas + my_ka
    columns = wq.shape[0]
    q_total = columns // 2
    pitch = half.shape[0] // columns
    cells = wk.shape[1] // 2
    slots, unit = ring.shape[0], ring.shape[2]
    chunks = cells // unit
    tiles = parts.shape[0]
    halves = parts.shape[3]
    mine = 2 * halves
    q_local, k_local = vectors.shape[0], vectors.shape[1]
    rows = 2 * k_local
    bands_n = vectors.shape[3]
    bands_own = bands_n // bands
    up, down = lax.rem(my_ka + 1, kas), lax.rem(my_ka + kas - 1, kas)
    across = lax.rem(my_ka + 2, kas)
    barrier = pltpu.get_barrier_semaphore()
    valid = pairs - (tiles - 1) * LANES
    spare = LANES - valid
    packed = q_local == 4 and valid <= 3 * spare
    lane = lax.broadcasted_iota(jnp.int32, (1, LANES), 1)
    overlaps = []
    for tile in range(tiles):
        for n in range(bands_own):
            low = max(tile * LANES, n * MODES)
            high = min((tile + 1) * LANES, (n + 1) * MODES)
            if low < high:
                overlaps.append((tile, n, low - tile * LANES, low - n * MODES, high - low))

    def fetch(index, slot):
        tile, chunk = index // chunks, lax.rem(index, chunks)
        return pltpu.make_async_copy(
            x_hbm.at[
                :, pl.ds(chunk * unit, unit), :, pl.ds(pl.multiple_of(tile * LANES, LANES), LANES)
            ],
            ring.at[slot],
            ring_sem.at[slot],
        )

    def project(real, imag, row):
        right = jnp.concatenate([real, imag], axis=0)
        product = jnp.dot(wq[...], right, preferred_element_type=jnp.float32)
        half[pl.ds(row, columns, stride=pitch), :] = product

    def strip(index):
        return half[index * pitch : index * pitch + cells, :].astype(jnp.bfloat16)

    def contract(order, pack=False):
        waiting = []
        for group in range(q_total // 2):
            right = jnp.concatenate(
                [
                    jnp.concatenate([strip(q), strip(q_total + q)], axis=0)
                    for q in (group * 2, group * 2 + 1)
                ],
                axis=1,
            )
            product = jnp.dot(wk[...], right, preferred_element_type=jnp.float32)
            waiting += [product[:, :LANES], product[:, LANES:]]
            if len(waiting) < q_local:
                continue
            if pack:
                for host in range(3):
                    moved = pltpu.roll(waiting[3], (valid - host * spare) % LANES, 1)
                    waiting[host] = jnp.where(lane < valid, waiting[host], moved)
            for q in range(q_local):
                m = q // 2
                for ka in range(kas):
                    parts[order, ka, m // halves, m % halves, group // mine, q % 2] = waiting[q][
                        ka * rows : (ka + 1) * rows
                    ].astype(jnp.bfloat16)
            waiting = []

    def put(source, target, send_sem, recv_sem, to_pb, to_ka):
        pltpu.make_async_remote_copy(
            src_ref=source, dst_ref=target, send_sem=send_sem, recv_sem=recv_sem,
            device_id={"pb": to_pb, "ka": to_ka}, device_id_type=MESH,
        ).start()

    def settle(window, sem):
        pltpu.make_async_copy(window, window, sem).wait()

    def lot(ref, way, pack):
        return ref.at[:, :, 0] if pack and way == 1 else ref

    def item(ref, way, to, pack):
        return ref.at[:, to, 0] if pack and way == 1 else ref.at[:, to]

    def send(order, pack=False):
        for way, target in enumerate((up, down)):
            put(lot(parts.at[order, across, way], way, pack), lot(relay.at[order, way], way, pack),
                relay_send.at[way, order], relay_recv.at[way, order], my_pb, target)

        def raw(index, carry):
            to = lax.rem(my_pb + index, bands)
            for way, target in enumerate((down, up)):
                put(item(parts.at[order, target, way], way, to, pack),
                    item(recv.at[order, 2 - way, way], way, my_pb, pack),
                    raw_send.at[1 - way, order], raw_recv.at[1 - way, order], to, target)
            return carry

        lax.fori_loop(0, bands, raw, 0)

        def plane(index, carry):
            to = lax.rem(my_pb + index, bands)
            put(parts.at[order, my_ka, :, :, to], recv.at[order, 0, :, :, my_pb],
                plane_send.at[order], plane_recv.at[order], to, my_ka)
            return carry

        lax.fori_loop(1, bands, plane, 0)

    def pass_on(order, pack=False):
        for way, (target, place) in enumerate(((up, 1), (down, 2))):
            settle(lot(relay.at[order, way], way, pack), relay_recv.at[way, order])
            for member in range(1 if pack and way == 1 else 2):
                own = parts[order, target, way, :, :, member].astype(jnp.float32)
                arrived = relay[order, way, :, :, member].astype(jnp.float32)
                sums[order, way, :, :, member] = (own + arrived).astype(jnp.bfloat16)

            def one(index, carry, way=way, target=target, place=place):
                to = lax.rem(my_pb + index, bands)
                put(item(sums.at[order, way], way, to, pack),
                    item(recv.at[order, place, way], way, my_pb, pack),
                    sum_send.at[way, order], sum_recv.at[way, order], to, target)
                return carry

            lax.fori_loop(0, bands, one, 0)

    edge_cells = edge_ref.shape[1]

    def edge(index, carry):
        for inner in range(unit):
            cell = index * unit + inner
            project(edge_ref[0, cell], edge_ref[1, cell], step * edge_cells + cell)
        return carry

    @pl.when(step == 0)
    def _():
        def greet(index, carry):
            peer = lax.rem(me + index, devices)
            pl.semaphore_signal(
                barrier, inc=1, device_id={"pb": peer // kas, "ka": lax.rem(peer, kas)},
                device_id_type=MESH,
            )
            return carry

        lax.fori_loop(1, devices, greet, 0)

        def first(index, carry):
            fetch(index, index).start()
            return carry

        lax.fori_loop(0, slots, first, 0)
        cos, sin = angles(qpoints[...], phonon_cells[...])
        wq[...] = jnp.concatenate(
            [jnp.concatenate([cos, -sin], 1), jnp.concatenate([sin, cos], 1)], 0
        ).astype(jnp.bfloat16)
        cells_all = electron_cells[...]
        own = cells_all[:, :cells]
        for ka in range(1, kas):
            own = jnp.where(my_ka == ka, cells_all[:, ka * cells : (ka + 1) * cells], own)
        cos, sin = angles(kpoints[...], own)
        blocks = []
        for ka in range(kas):
            c = cos[ka * k_local : (ka + 1) * k_local]
            s = sin[ka * k_local : (ka + 1) * k_local]
            blocks += [jnp.concatenate([c, -s], 1), jnp.concatenate([s, c], 1)]
        wk[...] = jnp.concatenate(blocks, 0).astype(jnp.bfloat16)

    lax.fori_loop(0, edge_cells // unit, edge, 0)

    def prepare():
        for q in range(q_local):
            freq = omega[q : q + 1, :]
            boson = bose[q : q + 1, :]
            level_q = jnp.transpose(levels[q])
            filled_q = jnp.transpose(filled[q])
            for k in range(k_local):
                f = filled_q[:, k : k + 1]
                offset = energy_k[k] - level_q[:, k : k + 1]
                absorb = gaussian(offset + freq)
                emit = gaussian(offset - freq)
                emission[q, k] = (boson + f) * absorb + (boson + 1.0 - f) * emit
                absorption[q, k] = (occupation_k[k] - f) * absorb
                for part in range(2):
                    rows_ref[part, :, :bands_n] = vectors[q, k, part].astype(jnp.float32)
                real, imag = (
                    jnp.concatenate(
                        [
                            rows_ref[part, pl.ds(n, bands, stride=bands_own), :]
                            for n in range(bands_own)
                        ],
                        axis=0,
                    )[:, :bands_n]
                    for part in range(2)
                )
                both = jnp.concatenate(
                    [jnp.concatenate([real, -imag], 1), jnp.concatenate([imag, real], 1)], 0
                )
                turned[q, k] = jnp.transpose(both).astype(jnp.bfloat16)
            for part in range(2):
                mode = modes[q, part].astype(jnp.float32)
                for index, (tile, n, row, start, count) in enumerate(overlaps):
                    pieces = []
                    if row:
                        pieces.append(jnp.zeros((row, MODES), jnp.float32))
                    pieces.append(mode[start : start + count])
                    if row + count < LANES:
                        pieces.append(jnp.zeros((LANES - row - count, MODES), jnp.float32))
                    placed = jnp.concatenate(pieces, 0) if len(pieces) > 1 else pieces[0]
                    table[q, index, :, part * LANES : part * LANES + MODES] = placed.astype(
                        jnp.bfloat16
                    )

    @pl.when(step == steps - 1)
    def _():
        contract(0, packed)
        pl.semaphore_wait(barrier, devices - 1)
        send(0, packed)

        def one_tile(tile, carry):
            for chunk in range(chunks):
                index = tile * chunks + chunk
                slot = lax.rem(index, slots)
                fetch(index, slot).wait()
                for inner in range(unit):
                    project(ring[slot, 0, inner], ring[slot, 1, inner], chunk * unit + inner)

                @pl.when(index + slots < (tiles - 1) * chunks)
                def _(index=index, slot=slot):
                    fetch(index + slots, slot).start()

                if chunk == 0:

                    @pl.when(tile == 1)
                    def _():
                        pass_on(0, packed)

                    @pl.when(tile > 1)
                    def _():
                        pass_on(tile - 1)

            contract(tile + 1)
            send(tile + 1)


            return carry

        lax.fori_loop(0, tiles - 1, one_tile, 0)
        for order in range(tiles):
            recv[order, 0, :, :, my_pb] = parts[order, my_ka, :, :, my_pb]
        pass_on(tiles - 2, packed and tiles == 2)
        pass_on(tiles - 1)
        prepare()
        started = set()
        for order in range(tiles):
            tile = tiles - 1 if order == 0 else order - 1
            settle(recv.at[order, 0, :, :, pl.ds(1, bands - 1)], plane_recv.at[order])
            pack = packed and order == 0
            for way in range(2):
                window = recv.at[order, 1 + way, 1 - way]
                settle(lot(window, 1 - way, pack), raw_recv.at[way, order])
            for way in range(2):
                settle(lot(recv.at[order, 1 + way, way], way, pack), sum_recv.at[way, order])
            lefts = []
            for q in range(q_local - 1 if pack else q_local):
                m = q // 2
                spot = (m // halves, m % halves)
                lefts.append(jnp.concatenate(
                    [
                        recv[order, 0, *spot, band, q % 2].astype(jnp.float32)
                        + recv[order, 1, *spot, band, q % 2].astype(jnp.float32)
                        + recv[order, 2, *spot, band, q % 2].astype(jnp.float32)
                        for band in range(bands)
                    ],
                    axis=0,
                ))
            if pack:
                back = [
                    pltpu.roll(lefts[host], (host * spare - valid) % LANES, 1) for host in range(3)
                ]
                lefts.append(
                    jnp.where(lane < spare, back[0], jnp.where(lane < 2 * spare, back[1], back[2]))
                )
            for m in range(mine):
                for member in range(2):
                    q = 2 * m + member
                    left = lefts[q]
                    if pairs < (tile + 1) * LANES:
                        left = jnp.where(lane < pairs - tile * LANES, left, 0.0)
                    left = left.astype(jnp.bfloat16)
                    for index, (other, n, _, _, _) in enumerate(overlaps):
                        if other != tile:
                            continue
                        product = jnp.dot(
                            left, table[q, index], preferred_element_type=jnp.float32
                        )
                        for side in range(2):
                            value = product[:, side * LANES : (side + 1) * LANES]
                            if (q, n) in started:
                                value = value + lifted[q, n, side]
                            lifted[q, n, side] = value
                        started.add((q, n))
        electron = [None] * k_local
        for q in range(q_local):
            phonon = None
            for k in range(k_local):
                real, imag = [], []
                for n in range(bands_own):
                    rr, ri, ir, ii = (
                        lifted[q, n, side, pl.ds(part * k_local + k, bands, stride=rows), :]
                        for part in range(2)
                        for side in range(2)
                    )
                    real.append(rr - ii)
                    imag.append(ri + ir)
                right = jnp.concatenate(real + imag, axis=0).astype(jnp.bfloat16)
                band = jnp.dot(turned[q, k], right, preferred_element_type=jnp.float32)
                band_real = band[:bands_n, :MODES]
                band_imag = band[bands_n:, :MODES]
                weight = band_real * band_real + band_imag * band_imag
                e_term = weight * emission[q, k]
                p_term = weight * absorption[q, k]
                electron[k] = e_term if q == 0 else electron[k] + e_term
                phonon = p_term if k == 0 else phonon + p_term
            totals[1, q : q + 1, :] = jnp.sum(phonon, axis=0, keepdims=True)
        for k in range(k_local):
            totals[0, k : k + 1, :] = jnp.sum(electron[k], axis=0, keepdims=True)
        copies = []
        for shift in range(1, bands):
            copies.append(pltpu.make_async_remote_copy(
                totals.at[0], got_e.at[my_pb], send_e.at[shift - 1], recv_e.at[shift - 1],
                device_id={"pb": lax.rem(my_pb + shift, bands), "ka": my_ka}, device_id_type=MESH,
            ))
        for shift in range(1, kas):
            copies.append(pltpu.make_async_remote_copy(
                totals.at[1], got_p.at[my_ka], send_p.at[shift - 1], recv_p.at[shift - 1],
                device_id={"pb": my_pb, "ka": lax.rem(my_ka + shift, kas)}, device_id_type=MESH,
            ))
        for copy in copies:
            copy.start()
        got_e[my_pb] = totals[0]
        got_p[my_ka] = totals[1]
        for order in range(tiles):
            settle(recv.at[order, 0, :, :, pl.ds(1, bands - 1)], plane_send.at[order])
            pack = packed and order == 0
            for way in range(2):
                settle(lot(relay.at[order, way], way, pack), relay_send.at[way, order])
                window = recv.at[order, 1 + way, 1 - way]
                settle(lot(window, 1 - way, pack), raw_send.at[way, order])
                settle(lot(recv.at[order, 1 + way, way], way, pack), sum_send.at[way, order])
        for copy in copies:
            copy.wait()
        total = got_e[0]
        for other in range(1, bands):
            total = total + got_e[other]
        out_ref[0] = total
        total = got_p[0]
        for other in range(1, kas):
            total = total + got_p[other]
        out_ref[1] = total


def everything(
    coupling, kpoints, qpoints, electron_cells, phonon_cells, phonon_modes, band_vectors,
    energies_kq, occupations_kq, energy_k, occupation_k, frequencies, bose_factors,
):
    bands, kas = lax.axis_size("pb"), lax.axis_size("ka")
    parts_count, cells, pairs, phonons = coupling.shape
    moved = jnp.transpose(coupling, (0, 1, 3, 2))
    tiles = -(-pairs // LANES)
    unit = cells // 2
    pitch = 8 * (-(-cells // 8) | 1)
    slots = min(4, 2 * (tiles - 1))
    q_local, k_local = band_vectors.shape[0], band_vectors.shape[1]
    bands_n = band_vectors.shape[3]
    columns = 2 * qpoints.shape[1]
    halves = q_local // 4
    rows = 2 * k_local
    bands_own = bands_n // bands
    overlaps = sum(
        max(t * LANES, n * MODES) < min((t + 1) * LANES, (n + 1) * MODES)
        for t in range(tiles)
        for n in range(bands_own)
    )
    small = pl.BlockSpec(memory_space=pltpu.VMEM)
    scalars = pl.BlockSpec(memory_space=pltpu.SMEM)
    dma = pltpu.SemaphoreType.DMA
    bf16, f32 = jnp.bfloat16, jnp.float32
    return pl.pallas_call(
        functools.partial(ring_kernel, pairs),
        grid=(2,),
        in_specs=[small] * 8
        + [scalars] * 2
        + [small] * 2
        + [
            pl.BlockSpec((parts_count, cells // 2, phonons, LANES), lambda e: (0, e, 0, tiles - 1)),
            pl.BlockSpec(memory_space=pl.ANY),
        ],
        out_specs=small,
        out_shape=jax.ShapeDtypeStruct((2, k_local, MODES), f32),
        scratch_shapes=[
            pltpu.VMEM((columns, 2 * phonons), bf16),
            pltpu.VMEM((2 * k_local * kas, 2 * cells), bf16),
            pltpu.VMEM((columns * pitch, LANES), f32),
            pltpu.VMEM((slots, parts_count, unit, phonons, LANES), bf16),
            pltpu.VMEM((tiles, kas, 2, halves, bands, 2, rows, LANES), bf16),
            pltpu.VMEM((tiles, 3, 2, halves, bands, 2, rows, LANES), bf16),
            pltpu.VMEM((tiles, 2, halves, bands, 2, rows, LANES), bf16),
            pltpu.VMEM((tiles, 2, halves, bands, 2, rows, LANES), bf16),
            pltpu.VMEM((q_local, overlaps, LANES, 2 * LANES), bf16),
            pltpu.VMEM((q_local, bands_own, 2, bands * 2 * k_local, LANES), f32),
            pltpu.VMEM((2, bands_n, LANES), f32),
            pltpu.VMEM((q_local, k_local, 2 * bands_n, 2 * bands_n), bf16),
            pltpu.VMEM((q_local, k_local, bands_n, MODES), f32),
            pltpu.VMEM((q_local, k_local, bands_n, MODES), f32),
            pltpu.VMEM((2, k_local, MODES), f32),
            pltpu.VMEM((bands, k_local, MODES), f32),
            pltpu.VMEM((kas, k_local, MODES), f32),
            dma((slots,)),
            dma((2, tiles)),
            dma((2, tiles)),
            dma((tiles,)),
            dma((tiles,)),
            dma((2, tiles)),
            dma((2, tiles)),
            dma((2, tiles)),
            dma((2, tiles)),
            dma((bands - 1,)),
            dma((bands - 1,)),
            dma((kas - 1,)),
            dma((kas - 1,)),
        ],
        compiler_params=pltpu.CompilerParams(
            collective_id=2,
            has_side_effects=True,
            dimension_semantics=("arbitrary",),
            vmem_limit_bytes=60 * 1024 * 1024,
        ),
        name="widths",
    )(
        kpoints, qpoints, electron_cells, phonon_cells, phonon_modes, band_vectors, energies_kq,
        occupations_kq, energy_k, occupation_k, frequencies, bose_factors, moved, moved,
    )


def on_device(
    coupling,
    kpoints,
    qpoints,
    electron_cells,
    phonon_cells,
    phonon_modes,
    band_vectors,
    energies_kq,
    occupations_kq,
    energy_k,
    occupation_k,
    frequencies,
    bose_factors,
):
    k_local = energy_k.shape[0]
    q_local = frequencies.shape[0]
    cells_local = coupling.shape[1]
    bands, kas = lax.axis_size("pb"), lax.axis_size("ka")
    q_total = q_local * bands
    k_total = k_local * kas
    whole_bands = coupling.shape[2] % MODES == 0 and coupling.shape[2] > LANES
    even = q_local % 4 == 0 and cells_local % 16 == 0
    if kas == 4 and whole_bands and even and k_local == q_local:
        sums = everything(
            coupling, kpoints, qpoints, electron_cells, phonon_cells, phonon_modes, band_vectors,
            energies_kq, occupations_kq, energy_k, occupation_k, frequencies, bose_factors,
        )
        return (sums[0] / (q_total * NB), sums[1] / (k_total * NB))
    cos_q, sin_q = phase_table(qpoints, phonon_cells)
    own_cells = lax.dynamic_slice_in_dim(
        electron_cells, lax.axis_index("ka") * cells_local, cells_local, 1
    )
    cos_k, sin_k = phase_table(kpoints, own_cells)
    wq = jnp.concatenate(
        [jnp.concatenate([cos_q, -sin_q], 1), jnp.concatenate([sin_q, cos_q], 1)], 0
    )
    wk = jnp.stack(
        [jnp.concatenate([cos_k, -sin_k], 1), jnp.concatenate([sin_k, cos_k], 1)], 1
    ).reshape(2 * k_total, 2 * cells_local)
    values = bloch(coupling, wq, wk, q_local, k_local)
    values = values.reshape(bands, q_local // 2, 2, k_local, 2, -1)
    values = jnp.transpose(values, (4, 3, 1, 2, 0, 5)).reshape(2, k_local, q_local, NB, MODES)
    electron, phonon = widths(
        values[0],
        values[1],
        phonon_modes,
        band_vectors,
        energies_kq,
        occupations_kq,
        energy_k,
        occupation_k,
        frequencies,
        bose_factors,
    )
    electron_width, phonon_width = exchange(electron / (q_total * NB), phonon / (k_total * NB))
    return (electron_width, phonon_width)


def solution(mesh):
    in_specs = (
        P(None, "ka", "pb", None),
        P(),
        P(),
        P(),
        P(),
        P("pb", None, None, None),
        P("pb", "ka", None, None, None),
        P("pb", "ka", None),
        P("pb", "ka", None),
        P("ka"),
        P("ka"),
        P("pb", None),
        P("pb", None),
    )
    out_specs = (P("ka", None), P("pb", None))
    return jax.shard_map(
        on_device, mesh=mesh, in_specs=in_specs, out_specs=out_specs, check_vma=False
    )
```

```python
import functools
import math

import jax
import jax.numpy as jnp
from jax import lax
from jax.experimental import pallas as pl
from jax.experimental.pallas import tpu as pltpu
from jax.sharding import PartitionSpec as P

NB = 40
MODES = 120
NG = 100


smearing = 0.05


def phase_table(points, cells):
    product = (
        points[0][:, None] * cells[0][None, :]
        + points[1][:, None] * cells[1][None, :]
        + points[2][:, None] * cells[2][None, :]
    )
    angle = jnp.mod(product, NG).astype(jnp.float32) * (2.0 * math.pi / NG)
    return (jnp.cos(angle).astype(jnp.bfloat16), jnp.sin(angle).astype(jnp.bfloat16))


def gaussian(offset):
    return jnp.exp(-0.5 * (offset / smearing) ** 2) / (smearing * math.sqrt(2.0 * math.pi))


def contract_last(left, right):
    return lax.dot_general(
        left, right, (((1,), (1,)), ((), ())), preferred_element_type=jnp.float32
    )


def mixed(form, left, right):
    return jnp.einsum(form, left, right, preferred_element_type=jnp.float32)


def widths(
    bloch_real, bloch_imag, modes, vectors, levels, filled, energy_k, occupation_k, omega, bose
):
    mode_real = modes[:, 0]
    mode_imag = modes[:, 1]
    moded_real = (
        mixed("kqnm,qmv->kqnv", bloch_real, mode_real)
        - mixed("kqnm,qmv->kqnv", bloch_imag, mode_imag)
    ).astype(jnp.bfloat16)
    moded_imag = (
        mixed("kqnm,qmv->kqnv", bloch_real, mode_imag)
        + mixed("kqnm,qmv->kqnv", bloch_imag, mode_real)
    ).astype(jnp.bfloat16)
    vector_real = vectors[:, :, 0]
    vector_imag = vectors[:, :, 1]
    band_real = mixed("qknb,kqnv->kqbv", vector_real, moded_real) + mixed(
        "qknb,kqnv->kqbv", vector_imag, moded_imag
    )
    band_imag = mixed("qknb,kqnv->kqbv", vector_real, moded_imag) - mixed(
        "qknb,kqnv->kqbv", vector_imag, moded_real
    )
    weight = band_real * band_real + band_imag * band_imag
    level_kq = jnp.transpose(levels, (1, 0, 2))[..., None]
    filled_kq = jnp.transpose(filled, (1, 0, 2))[..., None]
    offset = energy_k[:, None, None, None] - level_kq
    freq = omega[None, :, None, :]
    boson = bose[None, :, None, :]
    absorb = gaussian(offset + freq)
    emit = gaussian(offset - freq)
    electron = jnp.sum(
        weight * ((boson + filled_kq) * absorb + (boson + 1.0 - filled_kq) * emit), axis=(1, 2)
    )
    phonon = jnp.sum(weight * (occupation_k[:, None, None, None] - filled_kq) * absorb, axis=(0, 2))
    return (electron, phonon)


MESH = pl.DeviceIdType.MESH
LANES = 128


def bloch_kernel(
    cells_block, tile, last, wq_ref, wk_ref, x_ref, out_ref,
    half, parts, recv, send_sem, recv_sem,
):
    pairs_step = pl.program_id(0)
    cell_step = pl.program_id(1)
    tiles = pl.num_programs(0)
    cell_steps = pl.num_programs(1)
    bands, kas = lax.axis_size("pb"), lax.axis_size("ka")
    devices = bands * kas
    me = lax.axis_index("pb") * kas + lax.axis_index("ka")
    columns = wq_ref.shape[0]
    cells = half.shape[1] // columns
    groups = parts.shape[2]
    mine = groups // bands
    rows = parts.shape[3] // 2
    barrier = pltpu.get_barrier_semaphore()

    @pl.when((pairs_step == 0) & (cell_step == 0))
    def _():
        def greet(step, carry):
            peer = lax.rem(me + step, devices)
            pl.semaphore_signal(
                barrier, inc=1, device_id={"pb": peer // kas, "ka": lax.rem(peer, kas)},
                device_id_type=MESH,
            )
            return carry

        lax.fori_loop(1, devices, greet, 0)

    for cell in range(cells_block):
        right = jnp.concatenate([x_ref[0, cell], x_ref[1, cell]], axis=0)
        product = jnp.dot(wq_ref[...], right, preferred_element_type=jnp.float32)
        row = cell_step * cells_block + cell
        for lane in range(tile // LANES):
            half[lane, pl.ds(row, columns, stride=cells), :] = product[
                :, lane * LANES : (lane + 1) * LANES
            ]

    def strip(index):
        start = pl.multiple_of(index * cells, cells)
        return jnp.concatenate(
            [half[lane, pl.ds(start, cells), :] for lane in range(tile // LANES)], axis=1
        ).astype(jnp.bfloat16)

    @pl.when(cell_step == cell_steps - 1)
    def _():
        def contract(group, carry):
            sums = []
            for member in range(2):
                q = group * 2 + member
                right = jnp.concatenate([strip(q), strip(columns // 2 + q)], axis=0)
                sums.append(
                    jnp.dot(wk_ref[...], right, preferred_element_type=jnp.float32)
                )
            for ka in range(kas):
                block = slice(ka * rows, (ka + 1) * rows)
                parts[pairs_step, ka, group] = jnp.concatenate(
                    [sums[0][block], sums[1][block]], axis=0
                ).astype(jnp.bfloat16)
            return carry

        lax.fori_loop(0, groups, contract, 0, unroll=4)

    @pl.when((cell_step == cell_steps - 1) & (pairs_step == 0))
    def _():
        pl.semaphore_wait(barrier, devices - 1)

    def send(index, width):
        def one(step, carry):
            peer = lax.rem(me + step, devices)
            to_pb, to_ka = peer // kas, lax.rem(peer, kas)
            pltpu.make_async_remote_copy(
                src_ref=parts.at[index, to_ka, pl.ds(to_pb * mine, mine), :, pl.ds(0, width)],
                dst_ref=recv.at[index, me, :, :, pl.ds(0, width)],
                send_sem=send_sem.at[index],
                recv_sem=recv_sem.at[index],
                device_id={"pb": to_pb, "ka": to_ka},
                device_id_type=MESH,
            ).start()
            return carry

        lax.fori_loop(1, devices, one, 0)

    @pl.when((cell_step == cell_steps - 1) & (pairs_step < tiles - 1))
    def _():
        send(pairs_step, tile)

    @pl.when((cell_step == cell_steps - 1) & (pairs_step == tiles - 1))
    def _():
        count = recv.shape[0]
        send(count - 1, last)
        my_pb, my_ka = lax.axis_index("pb"), lax.axis_index("ka")
        for index in range(count):
            recv[index, me] = parts[index, my_ka, pl.ds(my_pb * mine, mine)]
        for index in range(count):
            width = tile if index < count - 1 else last
            window = recv.at[index, pl.ds(1, devices - 1), :, :, pl.ds(0, width)]
            pltpu.make_async_copy(window, window, send_sem.at[index]).wait()
            pltpu.make_async_copy(window, window, recv_sem.at[index]).wait()
            for band in range(bands):
                total = recv[index, band * kas, :, :, :width].astype(jnp.float32)
                for ka in range(1, kas):
                    total = total + recv[index, band * kas + ka, :, :, :width].astype(jnp.float32)
                out_ref[band, :, :, index * tile : index * tile + width] = total.astype(
                    jnp.bfloat16
                )


def bloch(coupling, wq, wk, q_local, k_local):
    bands, kas = lax.axis_size("pb"), lax.axis_size("ka")
    devices = bands * kas
    parts_count, cells, pairs, phonons = coupling.shape
    moved = jnp.transpose(coupling, (0, 1, 3, 2))
    padded = -(-pairs // LANES) * LANES
    if pairs < LANES:
        moved = jnp.pad(moved, ((0, 0), (0, 0), (0, 0), (0, LANES - pairs)))
    tile = min(2 * LANES, padded)
    tiles = -(-padded // tile)
    last = padded - (tiles - 1) * tile
    cells_block = 16
    columns = wq.shape[0]
    groups = columns // 4
    mine = q_local // 2
    rows = 4 * k_local
    result = pl.pallas_call(
        functools.partial(bloch_kernel, cells_block, tile, last),
        grid=(tiles, cells // cells_block),
        in_specs=[
            pl.BlockSpec(wq.shape, lambda t, e: (0, 0)),
            pl.BlockSpec(wk.shape, lambda t, e: (0, 0)),
            pl.BlockSpec((parts_count, cells_block, phonons, tile), lambda t, e: (0, e, 0, t)),
        ],
        out_specs=pl.BlockSpec((bands, mine, rows, padded), lambda t, e: (0, 0, 0, 0)),
        out_shape=jax.ShapeDtypeStruct((bands, mine, rows, padded), jnp.bfloat16),
        scratch_shapes=[
            pltpu.VMEM((tile // LANES, columns * cells, LANES), jnp.float32),
            pltpu.VMEM((tiles, kas, groups, rows, tile), jnp.bfloat16),
            pltpu.VMEM((tiles, devices, mine, rows, tile), jnp.bfloat16),
            pltpu.SemaphoreType.DMA((tiles,)),
            pltpu.SemaphoreType.DMA((tiles,)),
        ],
        compiler_params=pltpu.CompilerParams(
            collective_id=0,
            has_side_effects=True,
            dimension_semantics=("arbitrary", "arbitrary"),
            vmem_limit_bytes=60 * 1024 * 1024,
        ),
        name="bloch",
    )(wq, wk, moved)
    return result[..., :pairs]


def sums_kernel(electron_ref, phonon_ref, electron_out, phonon_out, got_e, got_p, send, recv_e, recv_p):
    bands, kas = lax.axis_size("pb"), lax.axis_size("ka")
    my_pb, my_ka = lax.axis_index("pb"), lax.axis_index("ka")
    barrier = pltpu.get_barrier_semaphore()
    for step in range(1, bands):
        pl.semaphore_signal(
            barrier, inc=1, device_id={"pb": lax.rem(my_pb + step, bands), "ka": my_ka},
            device_id_type=MESH,
        )
    for step in range(1, kas):
        pl.semaphore_signal(
            barrier, inc=1, device_id={"pb": my_pb, "ka": lax.rem(my_ka + step, kas)},
            device_id_type=MESH,
        )
    pl.semaphore_wait(barrier, bands + kas - 2)
    copies = []
    for step in range(1, bands):
        copies.append(pltpu.make_async_remote_copy(
            electron_ref, got_e.at[my_pb], send.at[step - 1], recv_e.at[step - 1],
            device_id={"pb": lax.rem(my_pb + step, bands), "ka": my_ka}, device_id_type=MESH,
        ))
    for step in range(1, kas):
        copies.append(pltpu.make_async_remote_copy(
            phonon_ref, got_p.at[my_ka], send.at[bands + step - 2], recv_p.at[step - 1],
            device_id={"pb": my_pb, "ka": lax.rem(my_ka + step, kas)}, device_id_type=MESH,
        ))
    for copy in copies:
        copy.start()
    got_e[my_pb] = electron_ref[...]
    got_p[my_ka] = phonon_ref[...]
    for copy in copies:
        copy.wait()
    total = got_e[0]
    for step in range(1, bands):
        total = total + got_e[step]
    electron_out[...] = total
    total = got_p[0]
    for step in range(1, kas):
        total = total + got_p[step]
    phonon_out[...] = total


def exchange(electron, phonon):
    bands, kas = lax.axis_size("pb"), lax.axis_size("ka")
    whole = pl.BlockSpec(memory_space=pltpu.VMEM)
    return pl.pallas_call(
        sums_kernel,
        in_specs=[whole, whole],
        out_specs=[whole, whole],
        out_shape=[
            jax.ShapeDtypeStruct(electron.shape, electron.dtype),
            jax.ShapeDtypeStruct(phonon.shape, phonon.dtype),
        ],
        scratch_shapes=[
            pltpu.VMEM((bands, *electron.shape), jnp.float32),
            pltpu.VMEM((kas, *phonon.shape), jnp.float32),
            pltpu.SemaphoreType.DMA((bands + kas - 2,)),
            pltpu.SemaphoreType.DMA((bands - 1,)),
            pltpu.SemaphoreType.DMA((kas - 1,)),
        ],
        compiler_params=pltpu.CompilerParams(collective_id=1, has_side_effects=True),
        name="sums",
    )(electron, phonon)


def angles(points, cells):
    product = lax.dot_general(
        points.astype(jnp.float32).astype(jnp.bfloat16),
        cells.astype(jnp.float32).astype(jnp.bfloat16),
        (((0,), (0,)), ((), ())),
        preferred_element_type=jnp.float32,
    )
    turns = jnp.floor((product + 0.5) * (1.0 / NG))
    angle = (product - turns * NG) * (2.0 * math.pi / NG)
    return jnp.cos(angle), jnp.sin(angle)


def ring_kernel(
    pairs, kpoints, qpoints, electron_cells, phonon_cells, modes, vectors,
    levels, filled, energy_k, occupation_k, omega, bose, edge_ref, x_hbm, out_ref,
    wq, wk, half, ring, parts, recv, relay, sums, table, lifted, rows_ref, turned,
    emission, absorption, totals, got_e, got_p,
    ring_sem, relay_send, relay_recv, plane_send, plane_recv, raw_send, raw_recv,
    sum_send, sum_recv, send_e, recv_e, send_p, recv_p,
):
    step = pl.program_id(0)
    steps = pl.num_programs(0)
    bands, kas = lax.axis_size("pb"), lax.axis_size("ka")
    devices = bands * kas
    my_pb, my_ka = lax.axis_index("pb"), lax.axis_index("ka")
    me = my_pb * kas + my_ka
    columns = wq.shape[0]
    q_total = columns // 2
    pitch = half.shape[0] // columns
    cells = wk.shape[1] // 2
    slots, unit = ring.shape[0], ring.shape[2]
    chunks = cells // unit
    tiles = parts.shape[0]
    halves = parts.shape[3]
    mine = 2 * halves
    q_local, k_local = vectors.shape[0], vectors.shape[1]
    rows = 2 * k_local
    bands_n = vectors.shape[3]
    bands_own = bands_n // bands
    up, down = lax.rem(my_ka + 1, kas), lax.rem(my_ka + kas - 1, kas)
    across = lax.rem(my_ka + 2, kas)
    barrier = pltpu.get_barrier_semaphore()
    valid = pairs - (tiles - 1) * LANES
    spare = LANES - valid
    packed = q_local == 4 and valid <= 3 * spare
    lane = lax.broadcasted_iota(jnp.int32, (1, LANES), 1)
    overlaps = []
    for tile in range(tiles):
        for n in range(bands_own):
            low = max(tile * LANES, n * MODES)
            high = min((tile + 1) * LANES, (n + 1) * MODES)
            if low < high:
                overlaps.append((tile, n, low - tile * LANES, low - n * MODES, high - low))

    def fetch(index, slot):
        tile, chunk = index // chunks, lax.rem(index, chunks)
        return pltpu.make_async_copy(
            x_hbm.at[
                :, pl.ds(chunk * unit, unit), :, pl.ds(pl.multiple_of(tile * LANES, LANES), LANES)
            ],
            ring.at[slot],
            ring_sem.at[slot],
        )

    def project(real, imag, row):
        right = jnp.concatenate([real, imag], axis=0)
        product = jnp.dot(wq[...], right, preferred_element_type=jnp.float32)
        half[pl.ds(row, columns, stride=pitch), :] = product

    def strip(index):
        return half[index * pitch : index * pitch + cells, :].astype(jnp.bfloat16)

    def contract(order, pack=False):
        waiting = []
        for group in range(q_total // 2):
            right = jnp.concatenate(
                [
                    jnp.concatenate([strip(q), strip(q_total + q)], axis=0)
                    for q in (group * 2, group * 2 + 1)
                ],
                axis=1,
            )
            product = jnp.dot(wk[...], right, preferred_element_type=jnp.float32)
            waiting += [product[:, :LANES], product[:, LANES:]]
            if len(waiting) < q_local:
                continue
            if pack:
                for host in range(3):
                    moved = pltpu.roll(waiting[3], (valid - host * spare) % LANES, 1)
                    waiting[host] = jnp.where(lane < valid, waiting[host], moved)
            for q in range(q_local):
                m = q // 2
                for ka in range(kas):
                    parts[order, ka, m // halves, m % halves, group // mine, q % 2] = waiting[q][
                        ka * rows : (ka + 1) * rows
                    ].astype(jnp.bfloat16)
            waiting = []

    def put(source, target, send_sem, recv_sem, to_pb, to_ka):
        pltpu.make_async_remote_copy(
            src_ref=source, dst_ref=target, send_sem=send_sem, recv_sem=recv_sem,
            device_id={"pb": to_pb, "ka": to_ka}, device_id_type=MESH,
        ).start()

    def settle(window, sem):
        pltpu.make_async_copy(window, window, sem).wait()

    def lot(ref, way, pack):
        return ref.at[:, :, 0] if pack and way == 1 else ref

    def item(ref, way, to, pack):
        return ref.at[:, to, 0] if pack and way == 1 else ref.at[:, to]

    def start(order, way, pack=False):
        put(lot(parts.at[order, across, way], way, pack), lot(relay.at[order, way], way, pack),
            relay_send.at[way, order], relay_recv.at[way, order], my_pb, (up, down)[way])

    def contract_half(order, way):
        for band in range(bands):
            for inside in range(halves):
                m = way * halves + inside
                group = band * mine + m
                right = jnp.concatenate(
                    [
                        jnp.concatenate([strip(q), strip(q_total + q)], axis=0)
                        for q in (group * 2, group * 2 + 1)
                    ],
                    axis=1,
                )
                product = jnp.dot(wk[...], right, preferred_element_type=jnp.float32)
                for ka in range(kas):
                    block = product[ka * rows : (ka + 1) * rows]
                    for member in range(2):
                        parts[order, ka, way, inside, band, member] = block[
                            :, member * LANES : (member + 1) * LANES
                        ].astype(jnp.bfloat16)

    def send(order, pack=False):
        def raw(index, carry):
            to = lax.rem(my_pb + index, bands)
            for way, target in enumerate((down, up)):
                put(item(parts.at[order, target, way], way, to, pack),
                    item(recv.at[order, 2 - way, way], way, my_pb, pack),
                    raw_send.at[1 - way, order], raw_recv.at[1 - way, order], to, target)
            return carry

        lax.fori_loop(0, bands, raw, 0)

        def plane(index, carry):
            to = lax.rem(my_pb + index, bands)
            put(parts.at[order, my_ka, :, :, to], recv.at[order, 0, :, :, my_pb],
                plane_send.at[order], plane_recv.at[order], to, my_ka)
            return carry

        lax.fori_loop(1, bands, plane, 0)

    def pass_on(order, pack=False):
        for way, (target, place) in enumerate(((up, 1), (down, 2))):
            settle(lot(relay.at[order, way], way, pack), relay_recv.at[way, order])
            for member in range(1 if pack and way == 1 else 2):
                own = parts[order, target, way, :, :, member].astype(jnp.float32)
                arrived = relay[order, way, :, :, member].astype(jnp.float32)
                sums[order, way, :, :, member] = (own + arrived).astype(jnp.bfloat16)

            def one(index, carry, way=way, target=target, place=place):
                to = lax.rem(my_pb + index, bands)
                put(item(sums.at[order, way], way, to, pack),
                    item(recv.at[order, place, way], way, my_pb, pack),
                    sum_send.at[way, order], sum_recv.at[way, order], to, target)
                return carry

            lax.fori_loop(0, bands, one, 0)

    edge_cells = edge_ref.shape[1]

    def edge(index, carry):
        for inner in range(unit):
            cell = index * unit + inner
            project(edge_ref[0, cell], edge_ref[1, cell], step * edge_cells + cell)
        return carry

    @pl.when(step == 0)
    def _():
        def greet(index, carry):
            peer = lax.rem(me + index, devices)
            pl.semaphore_signal(
                barrier, inc=1, device_id={"pb": peer // kas, "ka": lax.rem(peer, kas)},
                device_id_type=MESH,
            )
            return carry

        lax.fori_loop(1, devices, greet, 0)

        def first(index, carry):
            fetch(index, index).start()
            return carry

        lax.fori_loop(0, slots, first, 0)
        cos, sin = angles(qpoints[...], phonon_cells[...])
        wq[...] = jnp.concatenate(
            [jnp.concatenate([cos, -sin], 1), jnp.concatenate([sin, cos], 1)], 0
        ).astype(jnp.bfloat16)
        cells_all = electron_cells[...]
        own = cells_all[:, :cells]
        for ka in range(1, kas):
            own = jnp.where(my_ka == ka, cells_all[:, ka * cells : (ka + 1) * cells], own)
        cos, sin = angles(kpoints[...], own)
        blocks = []
        for ka in range(kas):
            c = cos[ka * k_local : (ka + 1) * k_local]
            s = sin[ka * k_local : (ka + 1) * k_local]
            blocks += [jnp.concatenate([c, -s], 1), jnp.concatenate([s, c], 1)]
        wk[...] = jnp.concatenate(blocks, 0).astype(jnp.bfloat16)

    lax.fori_loop(0, edge_cells // unit, edge, 0)

    def prepare():
        for q in range(q_local):
            freq = omega[q : q + 1, :]
            boson = bose[q : q + 1, :]
            level_q = jnp.transpose(levels[q])
            filled_q = jnp.transpose(filled[q])
            for k in range(k_local):
                f = filled_q[:, k : k + 1]
                offset = energy_k[k] - level_q[:, k : k + 1]
                absorb = gaussian(offset + freq)
                emit = gaussian(offset - freq)
                emission[q, k] = (boson + f) * absorb + (boson + 1.0 - f) * emit
                absorption[q, k] = (occupation_k[k] - f) * absorb
                for part in range(2):
                    rows_ref[part, :, :bands_n] = vectors[q, k, part].astype(jnp.float32)
                real, imag = (
                    jnp.concatenate(
                        [
                            rows_ref[part, pl.ds(n, bands, stride=bands_own), :]
                            for n in range(bands_own)
                        ],
                        axis=0,
                    )[:, :bands_n]
                    for part in range(2)
                )
                both = jnp.concatenate(
                    [jnp.concatenate([real, -imag], 1), jnp.concatenate([imag, real], 1)], 0
                )
                turned[q, k] = jnp.transpose(both).astype(jnp.bfloat16)
            for part in range(2):
                mode = modes[q, part].astype(jnp.float32)
                for index, (tile, n, row, start, count) in enumerate(overlaps):
                    pieces = []
                    if row:
                        pieces.append(jnp.zeros((row, MODES), jnp.float32))
                    pieces.append(mode[start : start + count])
                    if row + count < LANES:
                        pieces.append(jnp.zeros((LANES - row - count, MODES), jnp.float32))
                    placed = jnp.concatenate(pieces, 0) if len(pieces) > 1 else pieces[0]
                    table[q, index, :, part * LANES : part * LANES + MODES] = placed.astype(
                        jnp.bfloat16
                    )

    @pl.when(step == steps - 1)
    def _():
        contract(0, packed)
        pl.semaphore_wait(barrier, devices - 1)
        start(0, 0, packed)
        start(0, 1, packed)
        send(0, packed)

        def one_tile(tile, carry):
            for chunk in range(chunks):
                index = tile * chunks + chunk
                slot = lax.rem(index, slots)
                fetch(index, slot).wait()
                for inner in range(unit):
                    project(ring[slot, 0, inner], ring[slot, 1, inner], chunk * unit + inner)

                @pl.when(index + slots < (tiles - 1) * chunks)
                def _(index=index, slot=slot):
                    fetch(index + slots, slot).start()

                if chunk == 0:

                    @pl.when(tile == 1)
                    def _():
                        pass_on(0, packed)

                    @pl.when(tile > 1)
                    def _():
                        pass_on(tile - 1)

            for way in range(2):
                contract_half(tile + 1, way)
                start(tile + 1, way)
            send(tile + 1)


            return carry

        lax.fori_loop(0, tiles - 1, one_tile, 0)
        for order in range(tiles):
            recv[order, 0, :, :, my_pb] = parts[order, my_ka, :, :, my_pb]
        pass_on(tiles - 2, packed and tiles == 2)
        pl.when(my_ka < kas - 1)(prepare)
        pass_on(tiles - 1)
        pl.when(my_ka == kas - 1)(prepare)
        started = set()
        for order in range(tiles):
            tile = tiles - 1 if order == 0 else order - 1
            settle(recv.at[order, 0, :, :, pl.ds(1, bands - 1)], plane_recv.at[order])
            pack = packed and order == 0
            for way in range(2):
                window = recv.at[order, 1 + way, 1 - way]
                settle(lot(window, 1 - way, pack), raw_recv.at[way, order])
            for way in range(2):
                settle(lot(recv.at[order, 1 + way, way], way, pack), sum_recv.at[way, order])
            lefts = []
            for q in range(q_local - 1 if pack else q_local):
                m = q // 2
                spot = (m // halves, m % halves)
                lefts.append(jnp.concatenate(
                    [
                        recv[order, 0, *spot, band, q % 2].astype(jnp.float32)
                        + recv[order, 1, *spot, band, q % 2].astype(jnp.float32)
                        + recv[order, 2, *spot, band, q % 2].astype(jnp.float32)
                        for band in range(bands)
                    ],
                    axis=0,
                ))
            if pack:
                back = [
                    pltpu.roll(lefts[host], (host * spare - valid) % LANES, 1) for host in range(3)
                ]
                lefts.append(
                    jnp.where(lane < spare, back[0], jnp.where(lane < 2 * spare, back[1], back[2]))
                )
            for m in range(mine):
                for member in range(2):
                    q = 2 * m + member
                    left = lefts[q]
                    if pairs < (tile + 1) * LANES:
                        left = jnp.where(lane < pairs - tile * LANES, left, 0.0)
                    left = left.astype(jnp.bfloat16)
                    for index, (other, n, _, _, _) in enumerate(overlaps):
                        if other != tile:
                            continue
                        product = jnp.dot(
                            left, table[q, index], preferred_element_type=jnp.float32
                        )
                        for side in range(2):
                            value = product[:, side * LANES : (side + 1) * LANES]
                            if (q, n) in started:
                                value = value + lifted[q, n, side]
                            lifted[q, n, side] = value
                        started.add((q, n))
        electron = [None] * k_local
        for q in range(q_local):
            phonon = None
            for k in range(k_local):
                real, imag = [], []
                for n in range(bands_own):
                    rr, ri, ir, ii = (
                        lifted[q, n, side, pl.ds(part * k_local + k, bands, stride=rows), :]
                        for part in range(2)
                        for side in range(2)
                    )
                    real.append(rr - ii)
                    imag.append(ri + ir)
                right = jnp.concatenate(real + imag, axis=0).astype(jnp.bfloat16)
                band = jnp.dot(turned[q, k], right, preferred_element_type=jnp.float32)
                band_real = band[:bands_n, :MODES]
                band_imag = band[bands_n:, :MODES]
                weight = band_real * band_real + band_imag * band_imag
                e_term = weight * emission[q, k]
                p_term = weight * absorption[q, k]
                electron[k] = e_term if q == 0 else electron[k] + e_term
                phonon = p_term if k == 0 else phonon + p_term
            totals[1, q : q + 1, :] = jnp.sum(phonon, axis=0, keepdims=True)
        for k in range(k_local):
            totals[0, k : k + 1, :] = jnp.sum(electron[k], axis=0, keepdims=True)
        copies = []
        for shift in range(1, bands):
            copies.append(pltpu.make_async_remote_copy(
                totals.at[0], got_e.at[my_pb], send_e.at[shift - 1], recv_e.at[shift - 1],
                device_id={"pb": lax.rem(my_pb + shift, bands), "ka": my_ka}, device_id_type=MESH,
            ))
        for shift in range(1, kas):
            copies.append(pltpu.make_async_remote_copy(
                totals.at[1], got_p.at[my_ka], send_p.at[shift - 1], recv_p.at[shift - 1],
                device_id={"pb": my_pb, "ka": lax.rem(my_ka + shift, kas)}, device_id_type=MESH,
            ))
        for copy in copies:
            copy.start()
        got_e[my_pb] = totals[0]
        got_p[my_ka] = totals[1]
        for order in range(tiles):
            settle(recv.at[order, 0, :, :, pl.ds(1, bands - 1)], plane_send.at[order])
            pack = packed and order == 0
            for way in range(2):
                settle(lot(relay.at[order, way], way, pack), relay_send.at[way, order])
                window = recv.at[order, 1 + way, 1 - way]
                settle(lot(window, 1 - way, pack), raw_send.at[way, order])
                settle(lot(recv.at[order, 1 + way, way], way, pack), sum_send.at[way, order])
        for copy in copies:
            copy.wait()
        total = got_e[0]
        for other in range(1, bands):
            total = total + got_e[other]
        out_ref[0] = total
        total = got_p[0]
        for other in range(1, kas):
            total = total + got_p[other]
        out_ref[1] = total


def everything(
    coupling, kpoints, qpoints, electron_cells, phonon_cells, phonon_modes, band_vectors,
    energies_kq, occupations_kq, energy_k, occupation_k, frequencies, bose_factors,
):
    bands, kas = lax.axis_size("pb"), lax.axis_size("ka")
    parts_count, cells, pairs, phonons = coupling.shape
    moved = jnp.transpose(coupling, (0, 1, 3, 2))
    tiles = -(-pairs // LANES)
    unit = cells // 2
    pitch = 8 * (-(-cells // 8) | 1)
    slots = min(4, 2 * (tiles - 1))
    q_local, k_local = band_vectors.shape[0], band_vectors.shape[1]
    bands_n = band_vectors.shape[3]
    columns = 2 * qpoints.shape[1]
    halves = q_local // 4
    rows = 2 * k_local
    bands_own = bands_n // bands
    overlaps = sum(
        max(t * LANES, n * MODES) < min((t + 1) * LANES, (n + 1) * MODES)
        for t in range(tiles)
        for n in range(bands_own)
    )
    small = pl.BlockSpec(memory_space=pltpu.VMEM)
    scalars = pl.BlockSpec(memory_space=pltpu.SMEM)
    dma = pltpu.SemaphoreType.DMA
    bf16, f32 = jnp.bfloat16, jnp.float32
    return pl.pallas_call(
        functools.partial(ring_kernel, pairs),
        grid=(2,),
        in_specs=[small] * 8
        + [scalars] * 2
        + [small] * 2
        + [
            pl.BlockSpec((parts_count, cells // 2, phonons, LANES), lambda e: (0, e, 0, tiles - 1)),
            pl.BlockSpec(memory_space=pl.ANY),
        ],
        out_specs=small,
        out_shape=jax.ShapeDtypeStruct((2, k_local, MODES), f32),
        scratch_shapes=[
            pltpu.VMEM((columns, 2 * phonons), bf16),
            pltpu.VMEM((2 * k_local * kas, 2 * cells), bf16),
            pltpu.VMEM((columns * pitch, LANES), f32),
            pltpu.VMEM((slots, parts_count, unit, phonons, LANES), bf16),
            pltpu.VMEM((tiles, kas, 2, halves, bands, 2, rows, LANES), bf16),
            pltpu.VMEM((tiles, 3, 2, halves, bands, 2, rows, LANES), bf16),
            pltpu.VMEM((tiles, 2, halves, bands, 2, rows, LANES), bf16),
            pltpu.VMEM((tiles, 2, halves, bands, 2, rows, LANES), bf16),
            pltpu.VMEM((q_local, overlaps, LANES, 2 * LANES), bf16),
            pltpu.VMEM((q_local, bands_own, 2, bands * 2 * k_local, LANES), f32),
            pltpu.VMEM((2, bands_n, LANES), f32),
            pltpu.VMEM((q_local, k_local, 2 * bands_n, 2 * bands_n), bf16),
            pltpu.VMEM((q_local, k_local, bands_n, MODES), f32),
            pltpu.VMEM((q_local, k_local, bands_n, MODES), f32),
            pltpu.VMEM((2, k_local, MODES), f32),
            pltpu.VMEM((bands, k_local, MODES), f32),
            pltpu.VMEM((kas, k_local, MODES), f32),
            dma((slots,)),
            dma((2, tiles)),
            dma((2, tiles)),
            dma((tiles,)),
            dma((tiles,)),
            dma((2, tiles)),
            dma((2, tiles)),
            dma((2, tiles)),
            dma((2, tiles)),
            dma((bands - 1,)),
            dma((bands - 1,)),
            dma((kas - 1,)),
            dma((kas - 1,)),
        ],
        compiler_params=pltpu.CompilerParams(
            collective_id=2,
            has_side_effects=True,
            dimension_semantics=("arbitrary",),
            vmem_limit_bytes=60 * 1024 * 1024,
        ),
        name="widths",
    )(
        kpoints, qpoints, electron_cells, phonon_cells, phonon_modes, band_vectors, energies_kq,
        occupations_kq, energy_k, occupation_k, frequencies, bose_factors, moved, moved,
    )


def on_device(
    coupling,
    kpoints,
    qpoints,
    electron_cells,
    phonon_cells,
    phonon_modes,
    band_vectors,
    energies_kq,
    occupations_kq,
    energy_k,
    occupation_k,
    frequencies,
    bose_factors,
):
    k_local = energy_k.shape[0]
    q_local = frequencies.shape[0]
    cells_local = coupling.shape[1]
    bands, kas = lax.axis_size("pb"), lax.axis_size("ka")
    q_total = q_local * bands
    k_total = k_local * kas
    whole_bands = coupling.shape[2] % MODES == 0 and coupling.shape[2] > LANES
    even = q_local % 4 == 0 and cells_local % 16 == 0
    if kas == 4 and whole_bands and even and k_local == q_local:
        sums = everything(
            coupling, kpoints, qpoints, electron_cells, phonon_cells, phonon_modes, band_vectors,
            energies_kq, occupations_kq, energy_k, occupation_k, frequencies, bose_factors,
        )
        return (sums[0] / (q_total * NB), sums[1] / (k_total * NB))
    cos_q, sin_q = phase_table(qpoints, phonon_cells)
    own_cells = lax.dynamic_slice_in_dim(
        electron_cells, lax.axis_index("ka") * cells_local, cells_local, 1
    )
    cos_k, sin_k = phase_table(kpoints, own_cells)
    wq = jnp.concatenate(
        [jnp.concatenate([cos_q, -sin_q], 1), jnp.concatenate([sin_q, cos_q], 1)], 0
    )
    wk = jnp.stack(
        [jnp.concatenate([cos_k, -sin_k], 1), jnp.concatenate([sin_k, cos_k], 1)], 1
    ).reshape(2 * k_total, 2 * cells_local)
    values = bloch(coupling, wq, wk, q_local, k_local)
    values = values.reshape(bands, q_local // 2, 2, k_local, 2, -1)
    values = jnp.transpose(values, (4, 3, 1, 2, 0, 5)).reshape(2, k_local, q_local, NB, MODES)
    electron, phonon = widths(
        values[0],
        values[1],
        phonon_modes,
        band_vectors,
        energies_kq,
        occupations_kq,
        energy_k,
        occupation_k,
        frequencies,
        bose_factors,
    )
    electron_width, phonon_width = exchange(electron / (q_total * NB), phonon / (k_total * NB))
    return (electron_width, phonon_width)


def solution(mesh):
    in_specs = (
        P(None, "ka", "pb", None),
        P(),
        P(),
        P(),
        P(),
        P("pb", None, None, None),
        P("pb", "ka", None, None, None),
        P("pb", "ka", None),
        P("pb", "ka", None),
        P("ka"),
        P("ka"),
        P("pb", None),
        P("pb", None),
    )
    out_specs = (P("ka", None), P("pb", None))
    return jax.shard_map(
        on_device, mesh=mesh, in_specs=in_specs, out_specs=out_specs, check_vma=False
    )
```
